256 devices in a mesh: layer: 32 (over x, z), dp: 8 (over y, core).
Axes of the slice: x: 4, y: 4, z: 8, core: 2. Of those that a mesh axis runs over, the one named last changes fastest.
Arguments:
- coarse_guess: float32 [32, 8, 64, 512], P('layer', 'dp'), may hold values from -6 to 6
- adjoint_guess: float32 [32, 8, 64, 512], P('layer', 'dp'), may hold values from -6 to 6
- weights: float32 [64, 64, 576], P('layer'), may hold values from -0.25 to 0.25
- biases: float32 [64, 64], P('layer'), may hold values from -3 to 3
Outputs:
- states: float32 [64, 8, 64, 512], P('layer', 'dp')
- adjoints: float32 [64, 8, 64, 512], P('layer', 'dp')
- grad_weight: float32 [64, 64, 576], P('layer')
- grad_bias: float32 [64, 64], P('layer')
The draws below stay inside these ranges and needn't reach their ends.
All inputs are finite; a program needn't handle non-finite values.
Results may differ from the reference program's by a relative error of at most 0.0003.
Values sent between devices are 32-bit elements; how exact they have to be, the bound alone decides.
No kernel may reach another device: no remote copies, remote signals or barrier semaphores. Data moves between devices by JAX's collectives and lax.ppermute only.
A program may use at most 64 MiB of HBM per device.

```python
import jax
import jax.numpy as jnp
from jax import lax

C = 64
COLS = 32
CELLS = 512
COARSE = 32
LAYERS = 64
IMAGES = 8


def levels(rng, extent, cuts, smallest, top_value):
    factor_of, own = 1.0, jax.random.fold_in(rng, 6)
    for position, parts in cuts:
        draws = jnp.exp(jax.random.uniform(jax.random.fold_in(own, position), (parts,), jnp.float32, smallest / len(cuts), top_value / len(cuts)))
        factor_of = factor_of * jnp.repeat(draws, extent[position] // parts).reshape([-1 if axis == position else 1 for axis in range(len(extent))])
    return factor_of


def centred(key, dims, spread, limit, pieces=(), held_as=jnp.bfloat16):
    gain = levels(key, dims, pieces, -0.22, 0.18) if pieces else 1.0
    array = jax.random.normal(key, dims, jnp.float32) * spread * gain
    return jnp.minimum(jnp.maximum(array, -limit), limit).astype(held_as)


def setup_inputs(seed: int = 0) -> dict:
    splits = jax.random.split(jax.random.key(seed), 5)
    return {
        "coarse_guess": centred(splits[0], (COARSE, IMAGES, C, CELLS), 1.0, 6.0, ((0, 32), (1, 8)), jnp.float32),
        "adjoint_guess": centred(splits[1], (COARSE, IMAGES, C, CELLS), 1.0, 6.0, ((0, 32), (1, 8)), jnp.float32),
        "weights": centred(splits[2], (LAYERS, C, 9 * C), (9 * C) ** -0.5, 0.25, ((0, 32),), jnp.float32),
        "biases": centred(splits[3], (LAYERS, C), 0.5, 3.0, ((0, 32),), jnp.float32),
    }


step_size = 0.125


def patches(state_field, orient):
    cell_count = state_field.shape[-1]
    padded = jnp.pad(state_field, ((0, 0), (0, 0), (COLS + 1, COLS + 1)))
    col_index = jnp.arange(cell_count, dtype=jnp.int32) % COLS
    tap_fields = []
    for row_step in (-1, 0, 1):
        for col_step in (-1, 0, 1):
            offset = orient * (row_step * COLS + col_step)
            shifted = lax.slice_in_dim(padded, COLS + 1 + offset, COLS + 1 + offset + cell_count, axis=2)
            target = col_index + orient * col_step
            inside = (target >= 0) & (target < COLS)
            tap_fields.append(jnp.where(inside, shifted, 0.0))
    return jnp.concatenate(tap_fields, axis=1)


def convolve(matrix, state_field, orient):
    return jnp.einsum("ok,bkc->boc", matrix, patches(state_field, orient), precision=lax.Precision.HIGHEST)


def flipped(matrix):
    channel_count = matrix.shape[0]
    return matrix.reshape(channel_count, 9, channel_count).transpose(2, 1, 0).reshape(channel_count, 9 * channel_count)


def tangent(matrix, bias_row, state_field):
    return jnp.tanh(convolve(matrix, state_field, 1) + bias_row[:, None])


def advance(matrix, bias_row, state_field, step_scale):
    return state_field + step_scale * tangent(matrix, bias_row, state_field)


def pull_back(matrix, slope_field, cotangent, step_scale):
    return cotangent + step_scale * convolve(flipped(matrix), slope_field * cotangent, -1)


def weight_term(term_field, state_field):
    return jnp.einsum("boc,bkc->ok", term_field, patches(state_field, 1), precision=lax.Precision.HIGHEST)


def reference(coarse_guess, adjoint_guess, weights, biases):
    even_matrix = weights[0::2]
    odd_matrix = weights[1::2]
    even_bias = biases[0::2]
    odd_bias = biases[1::2]
    double_step = 2.0 * step_size
    batched_advance = jax.vmap(advance, in_axes=(0, 0, 0, None))
    batched_tangent = jax.vmap(tangent)
    batched_pull = jax.vmap(pull_back, in_axes=(0, 0, 0, None))
    fine_first = batched_advance(even_matrix, even_bias, coarse_guess, step_size)
    fine_second = batched_advance(odd_matrix, odd_bias, fine_first, step_size)
    forward_tau = fine_second - batched_advance(even_matrix, even_bias, coarse_guess, double_step)
    current = fine_second[0]
    end_list = [current]
    for layer_slot in range(1, COARSE):
        current = advance(even_matrix[layer_slot], even_bias[layer_slot], current, double_step) + forward_tau[layer_slot]
        end_list.append(current)
    end_fields = jnp.stack(end_list)
    begin_fields = jnp.concatenate([coarse_guess[0:1], end_fields[:-1]], axis=0)
    even_tangent = batched_tangent(even_matrix, even_bias, begin_fields)
    mid_fields = begin_fields + step_size * even_tangent
    even_slope = 1.0 - even_tangent * even_tangent
    odd_tangent = batched_tangent(odd_matrix, odd_bias, mid_fields)
    odd_slope = 1.0 - odd_tangent * odd_tangent
    relaxed = batched_pull(odd_matrix, odd_slope, adjoint_guess, step_size)
    fine_adjoint = batched_pull(even_matrix, even_slope, relaxed, step_size)
    adjoint_tau = fine_adjoint - batched_pull(even_matrix, even_slope, adjoint_guess, double_step)
    received_list = [adjoint_guess[COARSE - 1]]
    even_list = [fine_adjoint[COARSE - 1]]
    current = fine_adjoint[COARSE - 1]
    for layer_slot in range(COARSE - 2, -1, -1):
        received_list.append(current)
        current = pull_back(even_matrix[layer_slot], even_slope[layer_slot], current, double_step) + adjoint_tau[layer_slot]
        even_list.append(current)
    received_adjoint = jnp.stack(received_list[::-1])
    even_adjoint = jnp.stack(even_list[::-1])
    odd_adjoint = batched_pull(odd_matrix, odd_slope, received_adjoint, step_size)
    even_term = step_size * even_slope * odd_adjoint
    odd_term = step_size * odd_slope * received_adjoint
    inverse = 1.0 / IMAGES
    grad_even = jax.vmap(weight_term)(even_term, begin_fields)
    grad_odd = jax.vmap(weight_term)(odd_term, mid_fields)
    channel_count = weights.shape[1]
    grad_weight = jnp.stack([grad_even, grad_odd], axis=1).reshape(LAYERS, channel_count, 9 * channel_count) * inverse
    grad_bias = jnp.stack([jnp.sum(even_term, axis=(1, 3)), jnp.sum(odd_term, axis=(1, 3))], axis=1).reshape(LAYERS, channel_count) * inverse
    field_shape = coarse_guess.shape[1:]
    states = jnp.stack([mid_fields, end_fields], axis=1).reshape((LAYERS,) + field_shape)
    adjoints = jnp.stack([even_adjoint, odd_adjoint], axis=1).reshape((LAYERS,) + field_shape)
    return states, adjoints, grad_weight, grad_bias
```

```python
import jax
import jax.numpy as jnp
from jax import lax
from jax.experimental import pallas as pl
from jax.experimental.pallas import tpu as pltpu
from jax.sharding import PartitionSpec as P

F32 = jnp.float32
BF16 = jnp.bfloat16
H = 0.125
CH, CELLS = 64, 512
WPAD = 640
BLK = WPAD + CELLS
RING = 8
AXES = ("layer", "dp")
ANY = pl.BlockSpec(memory_space=pl.ANY)
SMEM = pl.BlockSpec(memory_space=pltpu.SMEM)
VMEM = pl.BlockSpec(memory_space=pltpu.VMEM)
PARAMS = pltpu.CompilerParams(vmem_limit_bytes=40 << 20)


def split(x):
    hi = x.astype(BF16)
    return hi, (x - hi.astype(F32)).astype(BF16)


def lane_index():
    return lax.broadcasted_iota(jnp.int32, (CH, 128), 1)


def columns(x):
    return [x[:, 128 * a : 128 * (a + 1)] for a in range(4)]


def swap(x):
    parts, lane, out = columns(x), lane_index(), []
    for a in range(4):
        acc = None
        for b in range(4):
            shift = ((b - a) * 32) % 128
            part = parts[b] if shift == 0 else pltpu.roll(parts[b], shift, 1)
            acc = part if acc is None else jnp.where(lane >= 32 * b, part, acc)
        out.append(acc)
    return jnp.concatenate(out, 1)


def lhs_forward(w):
    hi = w.astype(BF16).astype(F32)
    lo = w - hi
    rows = []
    for t in range(9):
        a, b = hi[:, 64 * t : 64 * t + 64], lo[:, 64 * t : 64 * t + 64]
        rows.append(jnp.concatenate([a, a, b], 1).astype(BF16))
    return jnp.concatenate(rows, 0)


def lhs_backward(w):
    wt = w.T
    hi = wt.astype(BF16).astype(F32)
    lo = wt - hi
    return jnp.concatenate([hi, hi, lo], 1).astype(BF16)


def conv(lhs, x, sign):
    hi, lo = split(x)
    z = jnp.dot(lhs, jnp.concatenate([hi, lo, hi], 0), preferred_element_type=F32)
    lane = lane_index()
    q = lane % 32
    lower, upper, right, left = lane < 96, lane >= 32, q < 31, q > 0

    def tap(a, e, col):
        t = 3 * (sign * a + 1) + (sign * e + 1)
        return z[64 * t : 64 * t + 64, 128 * col : 128 * col + 128]

    out = []
    for col in range(4):
        s = []
        for e in (-1, 0, 1):
            if col < 3:
                up = tap(1, e, col + 1)
            else:
                up = jnp.where(lower, pltpu.roll(tap(1, e, 0), 96, 1), 0.0)
            if col > 0:
                down = tap(-1, e, col - 1)
            else:
                down = jnp.where(upper, pltpu.roll(tap(-1, e, 3), 32, 1), 0.0)
            s.append(tap(0, e, col) + up + down)
        out.append(
            s[1]
            + jnp.where(right, pltpu.roll(s[2], 127, 1), 0.0)
            + jnp.where(left, pltpu.roll(s[0], 1, 1), 0.0)
        )
    return jnp.concatenate(out, 1)


def patches(x):
    lane = lane_index()
    q = lane % 32
    lower, upper, right, left = lane < 96, lane >= 32, q < 31, q > 0
    mid = columns(x)
    base = {
        0: mid,
        1: [jnp.where(right, pltpu.roll(c, 127, 1), 0.0) for c in mid],
        -1: [jnp.where(left, pltpu.roll(c, 1, 1), 0.0) for c in mid],
    }
    hi, lo = [], []
    for a in (-1, 0, 1):
        for e in (-1, 0, 1):
            c = base[e]
            if a == 1:
                c = c[1:] + [jnp.where(lower, pltpu.roll(c[0], 96, 1), 0.0)]
            elif a == -1:
                c = [jnp.where(upper, pltpu.roll(c[3], 32, 1), 0.0)] + c[:3]
            h, l = split(jnp.concatenate(c, 1))
            hi.append(h)
            lo.append(l)
    return jnp.concatenate(hi, 0), jnp.concatenate(lo, 0)


def dot_t(a, b):
    return lax.dot_general(a, b, (((1,), (1,)), ((), ())), preferred_element_type=F32)


def correlate(term, x):
    t_hi, t_lo = split(term)
    p_hi, p_lo = patches(x)
    return dot_t(t_hi, p_hi) + dot_t(t_hi, p_lo) + dot_t(t_lo, p_hi)


def as_column(row):
    r = lax.broadcasted_iota(jnp.int32, (CH, CH), 0)
    c = lax.broadcasted_iota(jnp.int32, (CH, CH), 1)
    spread = jnp.broadcast_to(row, (CH, CH))
    return jnp.sum(jnp.where(r == c, spread, 0.0), axis=1, keepdims=True)


def relax_kernel(c_ref, a_ref, w_ref, b_ref, one_ref, two_ref):
    c = swap(c_ref[...])
    w0, w1 = w_ref[0], w_ref[1]
    b0, b1 = as_column(b_ref[0:1]), as_column(b_ref[1:2])
    t0 = jnp.tanh(conv(lhs_forward(w0), c, 1) + b0)
    t1 = jnp.tanh(conv(lhs_forward(w1), c + H * t0, 1) + b1)
    pad = WPAD - 576
    one_ref[:, 0:576] = w0
    one_ref[:, 576:WPAD] = jnp.broadcast_to(b0, (CH, pad))
    one_ref[:, WPAD:BLK] = H * (t1 - t0)
    two_ref[:, 0:576] = w1
    two_ref[:, 576:WPAD] = jnp.broadcast_to(b1, (CH, pad))
    two_ref[:, WPAD:BLK] = swap(a_ref[...])


def relax(c, a, w, b):
    shape = jax.ShapeDtypeStruct((CH, BLK), F32)
    return pl.pallas_call(
        relax_kernel, out_shape=(shape, shape), compiler_params=PARAMS, name="relax"
    )(c, a, w, b)


def chain_kernel(stage, *refs):
    info_ref, refs = refs[0], refs[1:]
    g_refs, v_ref = refs[:RING], refs[RING]
    vt_ref, out_ref, g, vt, lhs, sems = refs[-6:]

    @pl.when((info_ref[0] == stage) & (info_ref[1] == 1))
    def _():
        copies = [pltpu.make_async_copy(g_refs[j], g.at[j], sems.at[j]) for j in range(RING)]
        for copy in copies:
            copy.start()
        for copy in copies:
            copy.wait()
        start = v_ref[...]
        if stage == 0:
            start = swap(start)

        def prepare(j, carry):
            lhs[j] = lhs_forward(g[j][:, 0:576])
            return carry

        lax.fori_loop(0, RING, prepare, 0)

        def step(j, v):
            t = jnp.tanh(conv(lhs[j], v, 1) + g[j][:, 576:577])
            vt[j, :, 0:CELLS] = v
            vt[j, :, CELLS:] = t
            return v + 2 * H * t + g[j][:, WPAD:BLK]

        out_ref[...] = lax.fori_loop(0, RING, step, start)
        copy = pltpu.make_async_copy(vt, vt_ref, sems.at[0])
        copy.start()
        copy.wait()


def chain(stage, info, blocks, v, previous):
    args = [info, *blocks, v]
    specs = [SMEM] + [ANY] * RING + [VMEM]
    aliases = {}
    if previous is not None:
        aliases = {len(args): 0}
        args.append(previous)
        specs.append(ANY)
    return pl.pallas_call(
        lambda *refs: chain_kernel(stage, *refs),
        out_shape=(
            jax.ShapeDtypeStruct((RING, CH, 2 * CELLS), F32),
            jax.ShapeDtypeStruct((CH, CELLS), F32),
        ),
        in_specs=specs,
        out_specs=(ANY, VMEM),
        scratch_shapes=[
            pltpu.VMEM((RING, CH, BLK), F32),
            pltpu.VMEM((RING, CH, 2 * CELLS), F32),
            pltpu.VMEM((RING, 9 * CH, 3 * CH), BF16),
            pltpu.SemaphoreType.DMA((RING,)),
        ],
        input_output_aliases=aliases,
        compiler_params=PARAMS,
        name=f"chain_{stage}",
    )(*args)


def middle_kernel(*refs):
    info_ref, refs = refs[0], refs[1:]
    one_refs, two_refs, vt_ref = refs[:RING], refs[RING : 2 * RING], refs[2 * RING]
    outs = refs[2 * RING + 1 : 3 * RING + 1]
    slope_ref, back_ref, one, two, vt, vs, slope, back, sems = refs[3 * RING + 1 :]

    @pl.when(info_ref[1] == 1)
    def _():
        copies = [pltpu.make_async_copy(one_refs[j], one.at[j], sems.at[j]) for j in range(RING)]
        copies += [
            pltpu.make_async_copy(two_refs[j], two.at[j], sems.at[RING + j]) for j in range(RING)
        ]
        copies.append(pltpu.make_async_copy(vt_ref, vt, sems.at[2 * RING]))
        for copy in copies:
            copy.start()
        for copy in copies:
            copy.wait()

        def step(j, carry):
            v, t0 = vt[j, :, 0:CELLS], vt[j, :, CELLS:]
            w0, w1 = one[j][:, 0:576], two[j][:, 0:576]
            b1, a = two[j][:, 576:577], two[j][:, WPAD:BLK]
            s0 = 1.0 - t0 * t0
            t1 = jnp.tanh(conv(lhs_forward(w1), v + H * t0, 1) + b1)
            s1 = 1.0 - t1 * t1
            shift = H * conv(lhs_backward(w1), s1 * a, -1)
            lhs = lhs_backward(w0)
            back[j] = lhs
            slope[j] = s0
            vs[j, :, 0:CELLS] = v
            vs[j, :, CELLS:] = shift + conv(lhs, s0 * (H * (a + shift) - 2 * H * a), -1)
            return carry

        lax.fori_loop(0, RING, step, 0)
        copies = [pltpu.make_async_copy(vs.at[j], outs[j], sems.at[j]) for j in range(RING)]
        copies.append(pltpu.make_async_copy(slope, slope_ref, sems.at[RING]))
        copies.append(pltpu.make_async_copy(back, back_ref, sems.at[RING + 1]))
        for copy in copies:
            copy.start()
        for copy in copies:
            copy.wait()


def middle(info, ones, twos, vt):
    vs_shape = jax.ShapeDtypeStruct((CH, 2 * CELLS), F32)
    out = pl.pallas_call(
        middle_kernel,
        out_shape=(vs_shape,) * RING
        + (
            jax.ShapeDtypeStruct((RING, CH, CELLS), F32),
            jax.ShapeDtypeStruct((RING, 9 * CH, 3 * CH), BF16),
        ),
        in_specs=[SMEM] + [ANY] * (2 * RING + 1),
        out_specs=(ANY,) * (RING + 2),
        scratch_shapes=[
            pltpu.VMEM((RING, CH, BLK), F32),
            pltpu.VMEM((RING, CH, BLK), F32),
            pltpu.VMEM((RING, CH, 2 * CELLS), F32),
            pltpu.VMEM((RING, CH, 2 * CELLS), F32),
            pltpu.VMEM((RING, CH, CELLS), F32),
            pltpu.VMEM((RING, 9 * CH, 3 * CH), BF16),
            pltpu.SemaphoreType.DMA((2 * RING + 1,)),
        ],
        compiler_params=PARAMS,
        name="middle",
    )(info, *ones, *twos, vt)
    return out[:RING], out[RING], out[RING + 1]


def back_kernel(stage, last, *refs):
    info_ref, slope_ref, back_ref, refs = refs[0], refs[1], refs[2], refs[3:]
    vs_refs, mu_ref = refs[:RING], refs[RING]
    outs = refs[-(RING + 6) : -6]
    out_ref, sigma, slope, back, mus, sems = refs[-6:]

    @pl.when((info_ref[0] == stage) & (info_ref[1] == 1))
    def _():
        copies = [
            pltpu.make_async_copy(vs_refs[j].at[:, pl.ds(CELLS, CELLS)], sigma.at[j], sems.at[j])
            for j in range(RING)
        ]
        copies.append(pltpu.make_async_copy(slope_ref, slope, sems.at[RING]))
        copies.append(pltpu.make_async_copy(back_ref, back, sems.at[RING + 1]))
        for copy in copies:
            copy.start()
        for copy in copies:
            copy.wait()
        start = mu_ref[:, WPAD:BLK] if stage == last else mu_ref[...]

        def step(k, mu):
            j = RING - 1 - k
            mus[j] = mu
            return mu + 2 * H * conv(back[j], slope[j] * mu, -1) + sigma[j]

        out_ref[...] = lax.fori_loop(0, RING, step, start)
        copies = [pltpu.make_async_copy(mus.at[j], outs[j], sems.at[j]) for j in range(RING)]
        for copy in copies:
            copy.start()
        for copy in copies:
            copy.wait()


def back_chain(stage, last, info, slope, back, vs, mu, previous):
    args = [info, slope, back, *vs, mu]
    specs = [SMEM, ANY, ANY] + [ANY] * RING + [VMEM]
    aliases = {}
    if previous is not None:
        aliases = {len(args) + j: j for j in range(RING)}
        args += list(previous)
        specs += [ANY] * RING
    shape = jax.ShapeDtypeStruct((CH, CELLS), F32)
    out = pl.pallas_call(
        lambda *refs: back_kernel(stage, last, *refs),
        out_shape=(shape,) * (RING + 1),
        in_specs=specs,
        out_specs=(ANY,) * RING + (VMEM,),
        scratch_shapes=[
            pltpu.VMEM((RING, CH, CELLS), F32),
            pltpu.VMEM((RING, CH, CELLS), F32),
            pltpu.VMEM((RING, 9 * CH, 3 * CH), BF16),
            pltpu.VMEM((RING, CH, CELLS), F32),
            pltpu.SemaphoreType.DMA((RING + 2,)),
        ],
        input_output_aliases=aliases,
        compiler_params=PARAMS,
        name=f"back_{stage}",
    )(*args)
    return out[:RING], out[RING]


def fetch(place, refs, target, sem):
    for m in range(RING):

        @pl.when(place == m)
        def _():
            copy = pltpu.make_async_copy(refs[m], target, sem)
            copy.start()
            copy.wait()


def early_kernel(*refs):
    info_ref, one_ref, w_ref, b_ref, refs = refs[0], refs[1], refs[2], refs[3], refs[4:]
    vs_refs = refs[:RING]
    states_ref, m_ref, s0_ref, s1_ref, vs_ref, sem = refs[RING:]
    fetch(info_ref[2], vs_refs, vs_ref, sem)
    v = vs_ref[:, 0:CELLS]
    t0 = jnp.tanh(conv(lhs_forward(w_ref[0]), v, 1) + as_column(b_ref[0:1]))
    m = v + H * t0
    t1 = jnp.tanh(conv(lhs_forward(w_ref[1]), m, 1) + as_column(b_ref[1:2]))
    m_ref[...] = m
    states_ref[0] = swap(m)
    states_ref[1] = swap(v + 2 * H * t0 + one_ref[:, WPAD:BLK])
    s0_ref[...] = 1.0 - t0 * t0
    s1_ref[...] = 1.0 - t1 * t1


def early(info, one, w, b, vs):
    shape = jax.ShapeDtypeStruct((CH, CELLS), F32)
    return pl.pallas_call(
        early_kernel,
        out_shape=(
            jax.ShapeDtypeStruct((2, CH, CELLS), F32),
            shape,
            shape,
            shape,
            jax.ShapeDtypeStruct((CH, 2 * CELLS), F32),
        ),
        in_specs=[SMEM, VMEM, VMEM, VMEM] + [ANY] * RING,
        scratch_shapes=[pltpu.SemaphoreType.DMA],
        compiler_params=PARAMS,
        name="early",
    )(info, one, w, b, *vs)


def late_kernel(*refs):
    info_ref, w_ref, m_ref, s0_ref, s1_ref, vs_ref = refs[:6]
    mu_refs = refs[6 : 6 + RING]
    adjoints_ref, mine_ref, other_ref, mu_scratch, sem = refs[6 + RING :]
    fetch(info_ref[2], mu_refs, mu_scratch, sem)
    mu = mu_scratch[...]
    v, sigma = vs_ref[:, 0:CELLS], vs_ref[:, CELLS:]
    s0 = s0_ref[...]
    odd_product = s1_ref[...] * mu
    odd = mu + H * conv(lhs_backward(w_ref[1]), odd_product, -1)
    even = mu + 2 * H * conv(lhs_backward(w_ref[0]), s0 * mu, -1) + sigma
    adjoints_ref[0] = swap(even)
    adjoints_ref[1] = swap(odd)
    even_term = (H / 8) * (s0 * odd)
    odd_term = (H / 8) * odd_product
    even_grad, odd_grad = correlate(even_term, v), correlate(odd_term, m_ref[...])
    pad = (CH, WPAD - 576)
    even_bias = jnp.broadcast_to(jnp.sum(even_term, axis=1, keepdims=True), pad)
    odd_bias = jnp.broadcast_to(jnp.sum(odd_term, axis=1, keepdims=True), pad)

    def write(ref, grad, bias):
        ref[:, 0:576] = grad
        ref[:, 576:WPAD] = bias

    @pl.when(info_ref[3] == 0)
    def _():
        write(mine_ref, even_grad, even_bias)
        write(other_ref, odd_grad, odd_bias)

    @pl.when(info_ref[3] == 1)
    def _():
        write(mine_ref, odd_grad, odd_bias)
        write(other_ref, even_grad, even_bias)


def late(info, w, m, s0, s1, vs, mus):
    grad = jax.ShapeDtypeStruct((CH, WPAD), F32)
    return pl.pallas_call(
        late_kernel,
        out_shape=(jax.ShapeDtypeStruct((2, CH, CELLS), F32), grad, grad),
        in_specs=[SMEM] + [VMEM] * 5 + [ANY] * RING,
        scratch_shapes=[pltpu.VMEM((CH, CELLS), F32), pltpu.SemaphoreType.DMA],
        compiler_params=PARAMS,
        name="late",
    )(info, w, m, s0, s1, vs, *mus)


def after(first, *others):
    return lax.optimization_barrier((first, *others))[1:]


def body(coarse_guess, adjoint_guess, weights, biases):
    images = lax.axis_size("dp")
    groups = lax.axis_size("layer") // RING
    layer, image = lax.axis_index("layer"), lax.axis_index("dp")

    def device(x, z, d):
        return (RING * x + z) * images + d

    def lead(d):
        return (RING // 2) * (d % 2)

    def gather(value, m):
        pairs = [
            (device(x, m, d), device(x, lead(d), d)) for x in range(groups) for d in range(images)
        ]
        return lax.ppermute(value, AXES, pairs)

    def scatter(value, m):
        pairs = [
            (device(x, lead(d), d), device(x, m, d)) for x in range(groups) for d in range(images)
        ]
        return lax.ppermute(value, AXES, pairs)

    def hop(value, source, target):
        pairs = [
            (device(source, lead(d), d), device(target, lead(d), d)) for d in range(images)
        ]
        return lax.ppermute(value, AXES, pairs)

    place = layer % RING
    info = jnp.stack(
        [layer // RING, (place == lead(image)).astype(jnp.int32), place, image % 2]
    ).astype(jnp.int32)
    c, a = coarse_guess[0, 0], adjoint_guess[0, 0]
    v = lax.ppermute(c, AXES, [(device(0, 0, d), device(0, lead(d), d)) for d in range(images)])
    one, two = relax(c, a, weights, biases)
    ones = [gather(one, m) for m in range(RING)]
    twos, waiting = [], list(range(RING))
    vt = None
    for stage in range(groups):
        vt, end = chain(stage, info, ones, v, vt)
        if stage < groups - 1:
            v = hop(end, stage, stage + 1)
            for m in waiting[: 3 if stage < groups - 2 else RING]:
                (operand,) = after(end, two)
                twos.append(gather(operand, m))
                waiting = waiting[1:]
    vs, slope, back = middle(info, ones, twos, vt)
    mus, mu = None, twos[RING - 1]
    own, waiting = [], list(range(RING))
    for stage in range(groups - 1, -1, -1):
        mus, end = back_chain(stage, groups - 1, info, slope, back, vs, mu, mus)
        if stage > 0:
            mu = hop(end, stage, stage - 1)
            for m in waiting[: 3 if stage > 1 else RING]:
                (operand,) = after(end, vs[m])
                own.append(scatter(operand, m))
                waiting = waiting[1:]
        if stage == 1:
            states, mid, s0, s1, own_vs = early(info, one, weights, biases, own)
            (mu,) = after(s1, mu)
    own_mu = [scatter(mus[m], m) for m in range(RING)]
    adjoints, mine, other = late(info, weights, mid, s0, s1, own_vs, own_mu)
    mine = mine + lax.ppermute(other, "dp", [(i, i ^ 1) for i in range(images)])
    for flip in (2, 6):
        mine = mine + lax.ppermute(mine, "dp", [(i, i ^ flip) for i in range(images)])
    other = lax.ppermute(mine, "dp", [(i, i ^ 1) for i in range(images)])
    first = image % 2 == 0
    even, odd = jnp.where(first, mine, other), jnp.where(first, other, mine)
    grad = jnp.stack([even[:, :576], odd[:, :576]])
    bias = jnp.stack([even[:, 576], odd[:, 576]])
    return states[:, None], adjoints[:, None], grad, bias


def solution(mesh):
    return jax.shard_map(
        body,
        mesh=mesh,
        in_specs=(
            P("layer", "dp", None, None),
            P("layer", "dp", None, None),
            P("layer", None, None),
            P("layer", None),
        ),
        out_specs=(
            P("layer", "dp", None, None),
            P("layer", "dp", None, None),
            P("layer", None, None),
            P("layer", None),
        ),
        check_vma=False,
    )
```

```python
import jax
import jax.numpy as jnp
from jax import lax
from jax.experimental import pallas as pl
from jax.experimental.pallas import tpu as pltpu
from jax.sharding import PartitionSpec as P

F32 = jnp.float32
BF16 = jnp.bfloat16
H = 0.125
CH, CELLS = 64, 512
WPAD = 640
BLK = WPAD + CELLS
RING = 8
AXES = ("layer", "dp")
ANY = pl.BlockSpec(memory_space=pl.ANY)
HBM = pl.BlockSpec(memory_space=pltpu.HBM)
VMEM = pl.BlockSpec(memory_space=pltpu.VMEM)
PARAMS = pltpu.CompilerParams(vmem_limit_bytes=40 << 20)


def split(x):
    hi = x.astype(BF16)
    return hi, (x - hi.astype(F32)).astype(BF16)


def lane_index():
    return lax.broadcasted_iota(jnp.int32, (CH, 128), 1)


def columns(x):
    return [x[:, 128 * a : 128 * (a + 1)] for a in range(4)]


def swap(x):
    parts, lane, out = columns(x), lane_index(), []
    for a in range(4):
        acc = None
        for b in range(4):
            shift = ((b - a) * 32) % 128
            part = parts[b] if shift == 0 else pltpu.roll(parts[b], shift, 1)
            acc = part if acc is None else jnp.where(lane >= 32 * b, part, acc)
        out.append(acc)
    return jnp.concatenate(out, 1)


def lhs_forward(w):
    hi = w.astype(BF16).astype(F32)
    lo = w - hi
    rows = []
    for t in range(9):
        a, b = hi[:, 64 * t : 64 * t + 64], lo[:, 64 * t : 64 * t + 64]
        rows.append(jnp.concatenate([a, a, b], 1).astype(BF16))
    return jnp.concatenate(rows, 0)


def lhs_backward(w):
    wt = w.T
    hi = wt.astype(BF16).astype(F32)
    lo = wt - hi
    return jnp.concatenate([hi, hi, lo], 1).astype(BF16)


def conv(lhs, x, sign):
    hi, lo = split(x)
    z = jnp.dot(lhs, jnp.concatenate([hi, lo, hi], 0), preferred_element_type=F32)
    lane = lane_index()
    q = lane % 32
    lower, upper, right, left = lane < 96, lane >= 32, q < 31, q > 0

    def tap(a, e, col):
        t = 3 * (sign * a + 1) + (sign * e + 1)
        return z[64 * t : 64 * t + 64, 128 * col : 128 * col + 128]

    out = []
    for col in range(4):
        s = []
        for e in (-1, 0, 1):
            if col < 3:
                up = tap(1, e, col + 1)
            else:
                up = jnp.where(lower, pltpu.roll(tap(1, e, 0), 96, 1), 0.0)
            if col > 0:
                down = tap(-1, e, col - 1)
            else:
                down = jnp.where(upper, pltpu.roll(tap(-1, e, 3), 32, 1), 0.0)
            s.append(tap(0, e, col) + up + down)
        out.append(
            s[1]
            + jnp.where(right, pltpu.roll(s[2], 127, 1), 0.0)
            + jnp.where(left, pltpu.roll(s[0], 1, 1), 0.0)
        )
    return jnp.concatenate(out, 1)


def patches(x):
    lane = lane_index()
    q = lane % 32
    lower, upper, right, left = lane < 96, lane >= 32, q < 31, q > 0
    mid = columns(x)
    base = {
        0: mid,
        1: [jnp.where(right, pltpu.roll(c, 127, 1), 0.0) for c in mid],
        -1: [jnp.where(left, pltpu.roll(c, 1, 1), 0.0) for c in mid],
    }
    hi, lo = [], []
    for a in (-1, 0, 1):
        for e in (-1, 0, 1):
            c = base[e]
            if a == 1:
                c = c[1:] + [jnp.where(lower, pltpu.roll(c[0], 96, 1), 0.0)]
            elif a == -1:
                c = [jnp.where(upper, pltpu.roll(c[3], 32, 1), 0.0)] + c[:3]
            h, l = split(jnp.concatenate(c, 1))
            hi.append(h)
            lo.append(l)
    return jnp.concatenate(hi, 0), jnp.concatenate(lo, 0)


def dot_t(a, b):
    return lax.dot_general(a, b, (((1,), (1,)), ((), ())), preferred_element_type=F32)


def correlate(term, x):
    t_hi, t_lo = split(term)
    p_hi, p_lo = patches(x)
    return dot_t(t_hi, p_hi) + dot_t(t_hi, p_lo) + dot_t(t_lo, p_hi)


def as_column(row):
    r = lax.broadcasted_iota(jnp.int32, (CH, CH), 0)
    c = lax.broadcasted_iota(jnp.int32, (CH, CH), 1)
    spread = jnp.broadcast_to(row, (CH, CH))
    return jnp.sum(jnp.where(r == c, spread, 0.0), axis=1, keepdims=True)


def place():
    layer, image = lax.axis_index("layer"), lax.axis_index("dp")
    core = image % 2
    return layer // RING, layer % RING, (RING // 2) * core, core


def start_all(copies):
    for copy in copies:
        copy.start()
    return copies


def wait_all(copies):
    for copy in copies:
        copy.wait()


def field(*lead):
    return jax.ShapeDtypeStruct((*lead, CH, CELLS), F32)


def lhs_shape(*lead):
    return jax.ShapeDtypeStruct((*lead, 9 * CH, 3 * CH), BF16)


def vmem(shape):
    return pltpu.VMEM(shape.shape, shape.dtype)


def relax_kernel(c_hbm, a_hbm, w_hbm, b_hbm, one_ref, two_ref, c_ref, a_ref, w_ref, b_ref, sems):
    copies = start_all(
        [
            pltpu.make_async_copy(source, target, sems.at[i])
            for i, (source, target) in enumerate(
                [(b_hbm, b_ref), (w_hbm, w_ref), (c_hbm, c_ref), (a_hbm, a_ref)]
            )
        ]
    )
    wait_all(copies[:3])
    c = swap(c_ref[...])
    w0, w1 = w_ref[0], w_ref[1]
    b0, b1 = as_column(b_ref[0:1]), as_column(b_ref[1:2])
    t0 = jnp.tanh(conv(lhs_forward(w0), c, 1) + b0)
    t1 = jnp.tanh(conv(lhs_forward(w1), c + H * t0, 1) + b1)
    pad = WPAD - 576
    one_ref[:, 0:576] = w0
    one_ref[:, 576:WPAD] = jnp.broadcast_to(b0, (CH, pad))
    ring, spot, _, _ = place()
    keep = jnp.where((ring == 0) & (spot == 0), 1.0, 0.0)
    one_ref[:, WPAD:BLK] = jnp.where(keep > 0.0, c + H * t0 + H * t1, H * (t1 - t0))
    two_ref[:, 0:576] = w1
    two_ref[:, 576:WPAD] = jnp.broadcast_to(b1, (CH, pad))
    wait_all(copies[3:])
    two_ref[:, WPAD:BLK] = swap(a_ref[...])


def relax(c, a, w, b):
    shape = jax.ShapeDtypeStruct((CH, BLK), F32)
    return pl.pallas_call(
        relax_kernel,
        out_shape=(shape, shape),
        in_specs=[HBM] * 4,
        scratch_shapes=[
            pltpu.VMEM(c.shape, F32),
            pltpu.VMEM(a.shape, F32),
            pltpu.VMEM(w.shape, F32),
            pltpu.VMEM(b.shape, F32),
            pltpu.SemaphoreType.DMA((4,)),
        ],
        compiler_params=pltpu.CompilerParams(vmem_limit_bytes=63 << 20),
        name="relax",
    )(c, a, w, b)


def collect(refs, target, sems, lead, part=None):
    copies = []
    for k, ref in enumerate(refs):
        j = (lead + k) % RING
        source = ref if part is None else ref.at[:, part]
        copies.append(pltpu.make_async_copy(source, target.at[j], sems.at[k]))
    return start_all(copies)


def first_kernel(*refs):
    g_refs, v_refs = refs[:RING], refs[RING : 2 * RING]
    t_ref, out_ref, g, vs, t, lhs, sems, t_sem = refs[2 * RING :]
    ring, spot, lead, _ = place()

    @pl.when((ring == 0) & (spot == lead))
    def _():
        wait_all(collect(g_refs, g, sems, lead))

        def prepare(j, carry):
            lhs[j] = lhs_forward(g[j][:, 0:576])
            return carry

        lax.fori_loop(1, RING, prepare, 0)

        def step(j, v):
            now = jnp.tanh(conv(lhs[j], v, 1) + g[j][:, 576:577])
            vs[j] = v
            t[j] = now
            return v + 2 * H * now + g[j][:, WPAD:BLK]

        out_ref[...] = lax.fori_loop(1, RING, step, g[0][:, WPAD:BLK])
        copies = [
            pltpu.make_async_copy(vs.at[(lead + k) % RING], v_refs[k], sems.at[k])
            for k in range(RING)
        ]
        copies.append(pltpu.make_async_copy(t, t_ref, t_sem))
        wait_all(start_all(copies))


def first_chain(blocks):
    out = pl.pallas_call(
        first_kernel,
        out_shape=(field(),) * RING + (field(RING), field()),
        in_specs=[ANY] * RING,
        out_specs=(ANY,) * (RING + 1) + (VMEM,),
        scratch_shapes=[
            pltpu.VMEM((RING, CH, BLK), F32),
            vmem(field(RING)),
            vmem(field(RING)),
            vmem(lhs_shape(RING)),
            pltpu.SemaphoreType.DMA((RING,)),
            pltpu.SemaphoreType.DMA,
        ],
        compiler_params=PARAMS,
        name="chain_0",
    )(*blocks)
    return out[:RING], out[RING], out[RING + 1]


def prepare_kernel(*refs):
    g_refs, outs = refs[:RING], refs[RING : RING + 2]
    g, ahead, behind, sems, out_sems = refs[RING + 2 :]
    ring, spot, lead, _ = place()

    @pl.when(spot == lead)
    def _():
        wait_all(collect(g_refs, g, sems, lead))

        def step(j, carry):
            w = g[j][:, 0:576]
            ahead[j] = lhs_forward(w)
            behind[j] = lhs_backward(w)
            return carry

        lax.fori_loop(0, RING, step, 0)
        wait_all(
            start_all(
                [
                    pltpu.make_async_copy(ahead, outs[0], out_sems.at[0]),
                    pltpu.make_async_copy(behind, outs[1], out_sems.at[1]),
                ]
            )
        )


def prepare(blocks, name):
    return pl.pallas_call(
        prepare_kernel,
        out_shape=(lhs_shape(RING), lhs_shape(RING)),
        in_specs=[ANY] * RING,
        out_specs=(ANY, ANY),
        scratch_shapes=[
            pltpu.VMEM((RING, CH, BLK), F32),
            vmem(lhs_shape(RING)),
            vmem(lhs_shape(RING)),
            pltpu.SemaphoreType.DMA((RING,)),
            pltpu.SemaphoreType.DMA((2,)),
        ],
        compiler_params=PARAMS,
        cost_estimate=pl.CostEstimate(flops=0, bytes_accessed=20 << 20, transcendentals=0),
        name=name,
    )(*blocks)


def chain_kernel(stage, *refs):
    g_refs, ahead_ref, v_ref = refs[:RING], refs[RING], refs[RING + 1]
    outs = refs[-(RING + 2 + 6) : -6]
    v_refs, t_ref, out_ref = outs[:RING], outs[RING], outs[RING + 1]
    g, vs, t, ahead, sems, ahead_sems = refs[-6:]
    ring, spot, lead, _ = place()

    @pl.when((ring == stage) & (spot == lead))
    def _():
        copies = [
            pltpu.make_async_copy(ahead_ref.at[j], ahead.at[j], ahead_sems.at[j])
            for j in range(RING)
        ]
        start_all(copies)
        wait_all(collect(g_refs, g, sems, lead))
        wait_all(copies)

        def step(j, v):
            now = jnp.tanh(conv(ahead[j], v, 1) + g[j][:, 576:577])
            vs[j] = v
            t[j] = now
            return v + 2 * H * now + g[j][:, WPAD:BLK]

        out_ref[...] = lax.fori_loop(0, RING, step, v_ref[...], unroll=2)
        copies = [
            pltpu.make_async_copy(vs.at[(lead + k) % RING], v_refs[k], sems.at[k])
            for k in range(RING)
        ]
        copies.append(pltpu.make_async_copy(t, t_ref, ahead_sems.at[0]))
        wait_all(start_all(copies))


def chain(stage, blocks, ahead, v, vs, t):
    args = [*blocks, ahead, v]
    aliases = {len(args) + k: k for k in range(RING + 1)}
    out = pl.pallas_call(
        lambda *refs: chain_kernel(stage, *refs),
        out_shape=(field(),) * RING + (field(RING), field()),
        in_specs=[ANY] * (RING + 1) + [VMEM] + [ANY] * (RING + 1),
        out_specs=(ANY,) * (RING + 1) + (VMEM,),
        scratch_shapes=[
            pltpu.VMEM((RING, CH, BLK), F32),
            vmem(field(RING)),
            vmem(field(RING)),
            vmem(lhs_shape(RING)),
            pltpu.SemaphoreType.DMA((RING,)),
            pltpu.SemaphoreType.DMA((RING,)),
        ],
        input_output_aliases=aliases,
        compiler_params=PARAMS,
        name=f"chain_{stage}",
    )(*args, *vs, t)
    return out[:RING], out[RING], out[RING + 1]


def correction(w1, v, t0, b1, a):
    t1 = jnp.tanh(conv(lhs_forward(w1), v + H * t0, 1) + b1)
    shift = H * conv(lhs_backward(w1), (1.0 - t1 * t1) * a, -1)
    s0 = 1.0 - t0 * t0
    return shift, s0 * (H * (shift - a)), (2 * H) * s0


def back_step(behind, mu, shift, part, slope):
    return mu + shift + conv(behind, slope * mu + part, -1)


def middle_kernel(last, *refs):
    two_refs, v_refs = refs[:RING], refs[RING : 2 * RING]
    near_ref, far_ref, c_ref, t_ref, ahead0_ref = refs[2 * RING : 2 * RING + 5]
    refs = refs[2 * RING + 5 :]
    outs = refs[:3]
    two, vs, t, ahead0, c, out, two_sems, v_sems, sems = refs[3:]
    ring, spot, lead, _ = place()

    @pl.when((spot == lead) & (ring < last))
    def _():
        copies = collect(two_refs, two, two_sems, lead)
        copies += collect(v_refs, vs, v_sems, lead)
        copies += start_all(
            [
                pltpu.make_async_copy(t_ref, t, sems.at[0]),
                pltpu.make_async_copy(ahead0_ref.at[0], ahead0, sems.at[1]),
                pltpu.make_async_copy(c_ref, c, sems.at[2]),
            ]
        )
        wait_all(copies)

        @pl.when(ring == 0)
        def _():
            v = swap(c[...])
            vs[0] = v
            bias = jnp.where(lead > 0, far_ref[:, 576:577], near_ref[:, 576:577])
            t[0] = jnp.tanh(conv(ahead0[...], v, 1) + bias)

        def step(j, carry):
            b1, a = two[j][:, 576:577], two[j][:, WPAD:BLK]
            got = correction(two[j][:, 0:576], vs[j], t[j], b1, a)
            for i in range(3):
                out[i, j] = got[i]
            return carry

        lax.fori_loop(0, RING, step, 0, unroll=2)
        wait_all(
            start_all([pltpu.make_async_copy(out.at[i], outs[i], sems.at[i]) for i in range(3)])
        )


def middle(last, twos, vs, ones, c, t, ahead0):
    return pl.pallas_call(
        lambda *refs: middle_kernel(last, *refs),
        out_shape=(field(RING),) * 3,
        in_specs=[ANY] * (2 * RING) + [VMEM] * 2 + [ANY] * 3,
        out_specs=(ANY,) * 3,
        scratch_shapes=[
            pltpu.VMEM((RING, CH, BLK), F32),
            vmem(field(RING)),
            vmem(field(RING)),
            vmem(lhs_shape()),
            vmem(field()),
            vmem(field(3, RING)),
            pltpu.SemaphoreType.DMA((RING,)),
            pltpu.SemaphoreType.DMA((RING,)),
            pltpu.SemaphoreType.DMA((3,)),
        ],
        compiler_params=PARAMS,
        name="middle",
    )(*twos, *vs, ones[0], ones[RING // 2], c, t, ahead0)


def turn_kernel(stage, *refs):
    one_refs, two_refs = refs[:RING], refs[RING : 2 * RING]
    lhs_refs, v_ref = refs[2 * RING : 2 * RING + 2], refs[2 * RING + 2]
    tail = 7
    v_refs = refs[-(2 * RING + 1 + tail) : -(RING + 1 + tail)]
    mu_refs = refs[-(RING + 1 + tail) : -(1 + tail)]
    out_ref = refs[-(1 + tail)]
    one, two, vs, lhs, out, sems, lhs_sems = refs[-tail:]
    ring, spot, lead, _ = place()

    @pl.when((ring == stage) & (spot == lead))
    def _():
        copies = [
            pltpu.make_async_copy(lhs_refs[i], lhs.at[i], lhs_sems.at[i]) for i in range(2)
        ]
        start_all(copies)
        late_copies = collect(two_refs, two, sems.at[1], lead)
        wait_all(collect(one_refs, one, sems.at[0], lead))
        wait_all(copies[:1])

        def ahead_step(j, v):
            now = jnp.tanh(conv(lhs[0, j], v, 1) + one[j][:, 576:577])
            vs[j] = v
            return v + 2 * H * now + one[j][:, WPAD:BLK], now

        def correct(j, v, t0):
            b1, a = two[j][:, 576:577], two[j][:, WPAD:BLK]
            got = correction(two[j][:, 0:576], v, t0, b1, a)
            for i in range(3):
                out[i, j] = got[i]

        def step(j, carry):
            v, old_v, old_t = carry
            new_v, now = ahead_step(j, v)
            correct(j - 1, old_v, old_t)
            return new_v, v, now

        start = v_ref[...]
        v, now = ahead_step(0, start)
        wait_all(late_copies)
        wait_all(copies[1:])
        _, v, now = lax.fori_loop(1, RING, step, (v, start, now))
        correct(RING - 1, v, now)
        copies = start_all(
            [
                pltpu.make_async_copy(vs.at[(lead + k) % RING], v_refs[k], sems.at[0, k])
                for k in range(RING)
            ]
        )
        wait_all(copies)

        def back(k, mu):
            j = RING - 1 - k
            vs[j] = mu
            return back_step(lhs[1, j], mu, out[0, j], out[1, j], out[2, j])

        out_ref[...] = lax.fori_loop(0, RING, back, two[RING - 1][:, WPAD:BLK], unroll=2)
        wait_all(
            start_all(
                [
                    pltpu.make_async_copy(vs.at[(lead + k) % RING], mu_refs[k], sems.at[1, k])
                    for k in range(RING)
                ]
            )
        )


def turn(stage, ones, twos, lhs, v, vs):
    args = [*ones, *twos, *lhs, v]
    aliases = {len(args) + k: k for k in range(RING)}
    out = pl.pallas_call(
        lambda *refs: turn_kernel(stage, *refs),
        out_shape=(field(),) * (2 * RING + 1),
        in_specs=[ANY] * (2 * RING + 2) + [VMEM] + [ANY] * RING,
        out_specs=(ANY,) * (2 * RING) + (VMEM,),
        scratch_shapes=[
            pltpu.VMEM((RING, CH, BLK), F32),
            pltpu.VMEM((RING, CH, BLK), F32),
            vmem(field(RING)),
            vmem(lhs_shape(2, RING)),
            vmem(field(3, RING)),
            pltpu.SemaphoreType.DMA((2, RING)),
            pltpu.SemaphoreType.DMA((2,)),
        ],
        input_output_aliases=aliases,
        compiler_params=PARAMS,
        name="turn",
    )(*args, *vs)
    return out[:RING], out[RING : 2 * RING], out[2 * RING]


def back_kernel(stage, *refs):
    part_refs, behind_ref, mu_ref = refs[:3], refs[3], refs[4]
    outs = refs[-(RING + 1 + 5) : -5]
    parts, behind, mus, sems, out_sems = refs[-5:]
    ring, spot, lead, _ = place()

    @pl.when((ring == stage) & (spot == lead))
    def _():
        copies = [pltpu.make_async_copy(part_refs[i], parts.at[i], sems.at[i]) for i in range(3)]
        copies.append(pltpu.make_async_copy(behind_ref, behind, sems.at[3]))
        wait_all(start_all(copies))

        def step(k, mu):
            j = RING - 1 - k
            mus[j] = mu
            return back_step(behind[j], mu, parts[0, j], parts[1, j], parts[2, j])

        outs[RING][...] = lax.fori_loop(0, RING, step, mu_ref[...], unroll=2)
        wait_all(
            start_all(
                [
                    pltpu.make_async_copy(mus.at[(lead + k) % RING], outs[k], out_sems.at[k])
                    for k in range(RING)
                ]
            )
        )


def back_chain(stage, parts, behind, mu, mus):
    args = [*parts, behind, mu]
    aliases = {len(args) + k: k for k in range(RING)}
    out = pl.pallas_call(
        lambda *refs: back_kernel(stage, *refs),
        out_shape=(field(),) * (RING + 1),
        in_specs=[ANY] * 4 + [VMEM] + [ANY] * RING,
        out_specs=(ANY,) * RING + (VMEM,),
        scratch_shapes=[
            vmem(field(3, RING)),
            vmem(lhs_shape(RING)),
            vmem(field(RING)),
            pltpu.SemaphoreType.DMA((4,)),
            pltpu.SemaphoreType.DMA((RING,)),
        ],
        input_output_aliases=aliases,
        compiler_params=PARAMS,
        name=f"back_{stage}",
    )(*args, *mus)
    return out[:RING], out[RING]


def fetch(refs, target, sem):
    _, spot, lead, _ = place()
    step = (spot + RING - lead) % RING
    for k in range(RING):

        @pl.when(step == k)
        def _():
            copy = pltpu.make_async_copy(refs[k], target, sem)
            copy.start()
            copy.wait()


def early_kernel(*refs):
    one_ref, two_ref, c_ref, refs = refs[0], refs[1], refs[2], refs[3:]
    v_refs = refs[:RING]
    states_ref, keep_ref, lhs_ref, v_ref, sem = refs[RING:]
    fetch(v_refs, v_ref, sem)
    ring, spot, _, _ = place()

    @pl.when((ring == 0) & (spot == 0))
    def _():
        v_ref[...] = swap(c_ref[...])

    v = v_ref[...]
    w0, w1 = one_ref[:, 0:576], two_ref[:, 0:576]
    t0 = jnp.tanh(conv(lhs_forward(w0), v, 1) + one_ref[:, 576:577])
    m = v + H * t0
    b1, a = two_ref[:, 576:577], two_ref[:, WPAD:BLK]
    t1 = jnp.tanh(conv(lhs_forward(w1), m, 1) + b1)
    s1 = 1.0 - t1 * t1
    s0 = 1.0 - t0 * t0
    lhs_ref[0] = lhs_backward(w0)
    behind = lhs_backward(w1)
    lhs_ref[1] = behind
    shift = H * conv(behind, s1 * a, -1)
    states_ref[0] = swap(m)
    slot = one_ref[:, WPAD:BLK]
    keep = jnp.where((ring == 0) & (spot == 0), 1.0, 0.0)
    states_ref[1] = swap(jnp.where(keep > 0.0, slot, v + 2 * H * t0 + slot))
    keep_ref[0] = v
    keep_ref[1] = m
    keep_ref[2] = s0
    keep_ref[3] = s1
    keep_ref[4] = shift
    keep_ref[5] = s0 * (H * (shift - a))


def early(one, two, c, vs):
    return pl.pallas_call(
        early_kernel,
        out_shape=(field(2), field(6), lhs_shape(2)),
        in_specs=[VMEM, VMEM, VMEM] + [ANY] * RING,
        scratch_shapes=[vmem(field()), pltpu.SemaphoreType.DMA],
        compiler_params=PARAMS,
        name="early",
    )(one, two, c, *vs)


def late_kernel(*refs):
    keep_ref, lhs_ref = refs[:2]
    mu_refs = refs[2 : 2 + RING]
    adjoints_ref, mine_ref, other_ref, mu_scratch, sem = refs[2 + RING :]
    fetch(mu_refs, mu_scratch, sem)
    mu = mu_scratch[...]
    s0 = keep_ref[2]
    odd_product = keep_ref[3] * mu
    odd = mu + H * conv(lhs_ref[1], odd_product, -1)
    even_term = (H / 8) * (s0 * odd)
    odd_term = (H / 8) * odd_product
    odd_grad = correlate(odd_term, keep_ref[1])
    even_grad = correlate(even_term, keep_ref[0])
    even = back_step(lhs_ref[0], mu, keep_ref[4], keep_ref[5], (2 * H) * s0)
    adjoints_ref[0] = swap(even)
    adjoints_ref[1] = swap(odd)
    pad = (CH, WPAD - 576)
    even_bias = jnp.broadcast_to(jnp.sum(even_term, axis=1, keepdims=True), pad)
    odd_bias = jnp.broadcast_to(jnp.sum(odd_term, axis=1, keepdims=True), pad)

    def write(ref, grad, bias):
        ref[:, 0:576] = grad
        ref[:, 576:WPAD] = bias

    core = place()[3]

    @pl.when(core == 0)
    def _():
        write(mine_ref, even_grad, even_bias)
        write(other_ref, odd_grad, odd_bias)

    @pl.when(core == 1)
    def _():
        write(mine_ref, odd_grad, odd_bias)
        write(other_ref, even_grad, even_bias)


def late(keep, lhs, mus):
    grad = jax.ShapeDtypeStruct((CH, WPAD), F32)
    return pl.pallas_call(
        late_kernel,
        out_shape=(field(2), grad, grad),
        in_specs=[VMEM] * 2 + [ANY] * RING,
        scratch_shapes=[vmem(field()), pltpu.SemaphoreType.DMA],
        compiler_params=PARAMS,
        name="late",
    )(keep, lhs, *mus)


def finish_kernel(mine_ref, other_ref, grad_ref, bias_ref):
    core = place()[3]
    r = lax.broadcasted_iota(jnp.int32, (CH, CH), 0)
    c = lax.broadcasted_iota(jnp.int32, (CH, CH), 1)

    def write(slot, ref):
        grad_ref[slot] = ref[:, 0:576]
        spread = jnp.broadcast_to(ref[:, 576:577], (CH, CH))
        bias_ref[slot : slot + 1] = jnp.sum(jnp.where(r == c, spread, 0.0), axis=0, keepdims=True)

    @pl.when(core == 0)
    def _():
        write(0, mine_ref)
        write(1, other_ref)

    @pl.when(core == 1)
    def _():
        write(1, mine_ref)
        write(0, other_ref)


def finish(mine, other):
    return pl.pallas_call(
        finish_kernel,
        out_shape=(
            jax.ShapeDtypeStruct((2, CH, 576), F32),
            jax.ShapeDtypeStruct((2, CH), F32),
        ),
        compiler_params=PARAMS,
        name="finish",
    )(mine, other)


def tie(*values):
    return lax.optimization_barrier(values)


NEAR = (1, 7, 2, 6, 3, 5, 4)
FAR = NEAR[::-1]


def body(coarse_guess, adjoint_guess, weights, biases):
    images = lax.axis_size("dp")
    groups = lax.axis_size("layer") // RING
    last = groups - 1

    def device(x, z, d):
        return (RING * x + z % RING) * images + d

    def lead(d):
        return (RING // 2) * (d % 2)

    everyone = [(x, d) for x in range(groups) for d in range(images)]

    def gather(value, k):
        pairs = [(device(x, lead(d) + k, d), device(x, lead(d), d)) for x, d in everyone]
        return lax.ppermute(value, AXES, pairs)

    def scatter(value, k):
        pairs = [(device(x, lead(d), d), device(x, lead(d) + k, d)) for x, d in everyone]
        return lax.ppermute(value, AXES, pairs)

    def hop(value, source, target):
        pairs = [
            (device(source, lead(d), d), device(target, lead(d), d)) for d in range(images)
        ]
        return lax.ppermute(value, AXES, pairs)

    c, a = coarse_guess[0, 0], adjoint_guess[0, 0]
    one, two = relax(c, a, weights, biases)
    ones, twos = {0: one}, {0: two}
    for k in NEAR:
        ones[k] = gather(one, k)
    ones = [ones[k] for k in range(RING)]
    vs, t, end = first_chain(ones)
    v = hop(end, 0, 1)
    ones[0] = tie(end, one)[1]
    ahead0, behind0 = prepare(ones, "prepare")
    for stage in range(1, last):
        vs, t, end = chain(stage, ones, ahead0, v, vs, t)
        v = hop(end, stage, stage + 1)
        for k in NEAR[:4] if stage == 1 else NEAR[4:]:
            twos[k] = gather(two, k)
    twos = [twos[k] for k in range(RING)]
    vs, mus, end = turn(last, ones, twos, [ahead0, behind0], v, vs)
    mu = hop(end, last, last - 1)
    c0 = lax.ppermute(
        tie(end, c)[1],
        AXES,
        [(device(0, 0, d), device(0, lead(d), d)) for d in range(images)],
    )
    parts = middle(last, twos, vs, ones, c0, t, ahead0)
    own_v = [vs[0]] + [None] * (RING - 1)
    keep = None
    for stage in range(last - 1, -1, -1):
        if stage == last - 1:
            chunk, gate = FAR[:4], parts[0]
        elif stage == last - 2:
            chunk, gate = FAR[4:], end
        else:
            chunk = ()
        for k in chunk:
            own_v[k] = scatter(tie(gate, vs[k])[1], k)
        mu, *parts = tie(mu, *parts)
        if stage == last - 2:
            states, keep, lhs = early(one, two, c, own_v)
            mu, keep = tie(mu, keep)
        mus, end = back_chain(stage, parts, behind0, mu, mus)
        if stage > 0:
            mu = hop(end, stage, stage - 1)
    own_mu = [mus[0]] + [None] * (RING - 1)
    for k in FAR:
        own_mu[k] = scatter(mus[k], k)
    adjoints, mine, other = late(keep, lhs, own_mu)
    mine = mine + lax.ppermute(other, "dp", [(i, i ^ 1) for i in range(images)])
    for flip in (2, 6):
        mine = mine + lax.ppermute(mine, "dp", [(i, i ^ flip) for i in range(images)])
    other = lax.ppermute(mine, "dp", [(i, i ^ 1) for i in range(images)])
    grad, bias = finish(mine, other)
    return states[:, None], adjoints[:, None], grad, bias


def solution(mesh):
    return jax.shard_map(
        body,
        mesh=mesh,
        in_specs=(
            P("layer", "dp", None, None),
            P("layer", "dp", None, None),
            P("layer", None, None),
            P("layer", None),
        ),
        out_specs=(
            P("layer", "dp", None, None),
            P("layer", "dp", None, None),
            P("layer", None, None),
            P("layer", None),
        ),
        check_vma=False,
    )
```

```python
import jax
import jax.numpy as jnp
from jax import lax
from jax.experimental import pallas as pl
from jax.experimental.pallas import tpu as pltpu
from jax.sharding import PartitionSpec as P

F32 = jnp.float32
BF16 = jnp.bfloat16
H = 0.125
CH, CELLS = 64, 512
WPAD = 640
BLK = WPAD + CELLS
RING = 8
AXES = ("layer", "dp")
ANY = pl.BlockSpec(memory_space=pl.ANY)
HBM = pl.BlockSpec(memory_space=pltpu.HBM)
VMEM = pl.BlockSpec(memory_space=pltpu.VMEM)
PARAMS = pltpu.CompilerParams(vmem_limit_bytes=40 << 20)


def split(x):
    hi = x.astype(BF16)
    return hi, (x - hi.astype(F32)).astype(BF16)


def lane_index():
    return lax.broadcasted_iota(jnp.int32, (CH, 128), 1)


def columns(x):
    return [x[:, 128 * a : 128 * (a + 1)] for a in range(4)]


def swap(x):
    parts, lane, out = columns(x), lane_index(), []
    for a in range(4):
        acc = None
        for b in range(4):
            shift = ((b - a) * 32) % 128
            part = parts[b] if shift == 0 else pltpu.roll(parts[b], shift, 1)
            acc = part if acc is None else jnp.where(lane >= 32 * b, part, acc)
        out.append(acc)
    return jnp.concatenate(out, 1)


def lhs_forward(w):
    hi = w.astype(BF16).astype(F32)
    lo = w - hi
    rows = []
    for t in range(9):
        a, b = hi[:, 64 * t : 64 * t + 64], lo[:, 64 * t : 64 * t + 64]
        rows.append(jnp.concatenate([a, a, b], 1).astype(BF16))
    return jnp.concatenate(rows, 0)


def lhs_backward(w):
    wt = w.T
    hi = wt.astype(BF16).astype(F32)
    lo = wt - hi
    return jnp.concatenate([hi, hi, lo], 1).astype(BF16)


def conv(lhs, x, sign):
    hi, lo = split(x)
    z = jnp.dot(lhs, jnp.concatenate([hi, lo, hi], 0), preferred_element_type=F32)
    lane = lane_index()
    q = lane % 32
    lower, upper, right, left = lane < 96, lane >= 32, q < 31, q > 0

    def tap(a, e, col):
        t = 3 * (sign * a + 1) + (sign * e + 1)
        return z[64 * t : 64 * t + 64, 128 * col : 128 * col + 128]

    out = []
    for col in range(4):
        s = []
        for e in (-1, 0, 1):
            if col < 3:
                up = tap(1, e, col + 1)
            else:
                up = jnp.where(lower, pltpu.roll(tap(1, e, 0), 96, 1), 0.0)
            if col > 0:
                down = tap(-1, e, col - 1)
            else:
                down = jnp.where(upper, pltpu.roll(tap(-1, e, 3), 32, 1), 0.0)
            s.append(tap(0, e, col) + up + down)
        out.append(
            s[1]
            + jnp.where(right, pltpu.roll(s[2], 127, 1), 0.0)
            + jnp.where(left, pltpu.roll(s[0], 1, 1), 0.0)
        )
    return jnp.concatenate(out, 1)


def patches(x):
    lane = lane_index()
    q = lane % 32
    lower, upper, right, left = lane < 96, lane >= 32, q < 31, q > 0
    mid = columns(x)
    base = {
        0: mid,
        1: [jnp.where(right, pltpu.roll(c, 127, 1), 0.0) for c in mid],
        -1: [jnp.where(left, pltpu.roll(c, 1, 1), 0.0) for c in mid],
    }
    hi, lo = [], []
    for a in (-1, 0, 1):
        for e in (-1, 0, 1):
            c = base[e]
            if a == 1:
                c = c[1:] + [jnp.where(lower, pltpu.roll(c[0], 96, 1), 0.0)]
            elif a == -1:
                c = [jnp.where(upper, pltpu.roll(c[3], 32, 1), 0.0)] + c[:3]
            h, l = split(jnp.concatenate(c, 1))
            hi.append(h)
            lo.append(l)
    return jnp.concatenate(hi, 0), jnp.concatenate(lo, 0)


def dot_t(a, b):
    return lax.dot_general(a, b, (((1,), (1,)), ((), ())), preferred_element_type=F32)


def correlate(term, x):
    t_hi, t_lo = split(term)
    p_hi, p_lo = patches(x)
    return dot_t(t_hi, p_hi) + dot_t(t_hi, p_lo) + dot_t(t_lo, p_hi)


def as_column(row):
    r = lax.broadcasted_iota(jnp.int32, (CH, CH), 0)
    c = lax.broadcasted_iota(jnp.int32, (CH, CH), 1)
    spread = jnp.broadcast_to(row, (CH, CH))
    return jnp.sum(jnp.where(r == c, spread, 0.0), axis=1, keepdims=True)


def place():
    layer, image = lax.axis_index("layer"), lax.axis_index("dp")
    core = image % 2
    return layer // RING, layer % RING, (RING // 2) * core, core


def start_all(copies):
    for copy in copies:
        copy.start()
    return copies


def wait_all(copies):
    for copy in copies:
        copy.wait()


def field(*lead):
    return jax.ShapeDtypeStruct((*lead, CH, CELLS), F32)


def lhs_shape(*lead):
    return jax.ShapeDtypeStruct((*lead, 9 * CH, 3 * CH), BF16)


def vmem(shape):
    return pltpu.VMEM(shape.shape, shape.dtype)


def relax_kernel(c_hbm, a_hbm, w_hbm, b_hbm, *refs):
    outs, (c_ref, a_ref, w_ref, b_ref, sems) = refs[:6], refs[6:]
    low_ref, high_ref, mid_ref, tau_ref, even_ref, two_ref = outs
    copies = start_all(
        [
            pltpu.make_async_copy(source, target, sems.at[i])
            for i, (source, target) in enumerate(
                [(b_hbm, b_ref), (w_hbm, w_ref), (c_hbm, c_ref), (a_hbm, a_ref)]
            )
        ]
    )
    wait_all(copies[:3])
    c = swap(c_ref[...])
    w0, w1 = w_ref[0], w_ref[1]
    b0, b1 = as_column(b_ref[0:1]), as_column(b_ref[1:2])
    t0 = jnp.tanh(conv(lhs_forward(w0), c, 1) + b0)
    t1 = jnp.tanh(conv(lhs_forward(w1), c + H * t0, 1) + b1)
    ring, spot, _, core = place()
    keep = jnp.where((ring == 0) & (spot == 0), 1.0, 0.0)
    tau = jnp.where(keep > 0.0, c + H * t0 + H * t1, H * (t1 - t0))

    def write_tau(ref):
        ref[:, 0:CELLS] = tau
        ref[:, CELLS:WPAD] = jnp.broadcast_to(b0, (CH, WPAD - CELLS))

    def write_even(ref):
        ref[:, 0:576] = w0
        ref[:, 576:WPAD] = jnp.zeros((CH, WPAD - 576), F32)

    write_tau(tau_ref)
    write_even(even_ref)

    first = (core == 0) == (spot < RING // 2)
    middle_first = (core == 0) == (spot == RING // 2)

    @pl.when(first)
    def _():
        write_tau(low_ref)
        write_even(high_ref)

    @pl.when(jnp.logical_not(first))
    def _():
        write_even(low_ref)
        write_tau(high_ref)

    @pl.when(middle_first)
    def _():
        write_tau(mid_ref)

    @pl.when(jnp.logical_not(middle_first))
    def _():
        write_even(mid_ref)

    two_ref[:, 0:576] = w1
    two_ref[:, 576:WPAD] = jnp.broadcast_to(b1, (CH, WPAD - 576))
    wait_all(copies[3:])
    two_ref[:, WPAD:BLK] = swap(a_ref[...])


def relax(c, a, w, b):
    short = jax.ShapeDtypeStruct((CH, WPAD), F32)
    return pl.pallas_call(
        relax_kernel,
        out_shape=(short,) * 5 + (jax.ShapeDtypeStruct((CH, BLK), F32),),
        in_specs=[HBM] * 4,
        scratch_shapes=[
            pltpu.VMEM(c.shape, F32),
            pltpu.VMEM(a.shape, F32),
            pltpu.VMEM(w.shape, F32),
            pltpu.VMEM(b.shape, F32),
            pltpu.SemaphoreType.DMA((4,)),
        ],
        compiler_params=pltpu.CompilerParams(vmem_limit_bytes=63 << 20),
        name="relax",
    )(c, a, w, b)


def slots(refs, target, sems, lead):
    copies = []
    for k, ref in enumerate(refs):
        j = (lead + k) % RING
        copies.append(pltpu.make_async_copy(ref, target.at[j], sems.at[j]))
    return copies


def stack_kernel(*refs):
    block_refs, stack_ref, sems = refs[: RING - 1], refs[RING - 1], refs[RING]
    _, spot, lead, _ = place()

    @pl.when(spot == RING // 2 - lead)
    def _():
        wait_all(
            start_all(
                [
                    pltpu.make_async_copy(block_refs[k], stack_ref.at[k], sems.at[k])
                    for k in range(RING - 1)
                ]
            )
        )


def stack(blocks):
    return pl.pallas_call(
        stack_kernel,
        out_shape=jax.ShapeDtypeStruct((RING - 1, CH, WPAD), F32),
        in_specs=[ANY] * (RING - 1),
        out_specs=ANY,
        scratch_shapes=[pltpu.SemaphoreType.DMA((RING - 1,))],
        compiler_params=PARAMS,
        name="stack",
    )(*blocks)


def even_slots(own_ref, stack_ref, target, sems, lead):
    return slots([own_ref] + [stack_ref.at[k] for k in range(RING - 1)], target, sems, lead)


def first_kernel(*refs):
    tau_refs, own_ref, stack_ref = refs[:RING], refs[RING], refs[RING + 1]
    vt_ref, out_ref, tau, even, vt, lhs, tau_sems, even_sems, sems = refs[RING + 2 :]
    ring, spot, lead, _ = place()

    @pl.when((ring == 0) & (spot == lead))
    def _():
        copies = even_slots(own_ref, stack_ref, even, even_sems, lead)
        copies += slots(tau_refs, tau, tau_sems, lead)
        wait_all(start_all(copies))

        def prepare(j, carry):
            lhs[j] = lhs_forward(even[j][:, 0:576])
            return carry

        lax.fori_loop(1, RING, prepare, 0)

        def step(j, v):
            now = jnp.tanh(conv(lhs[j], v, 1) + tau[j][:, CELLS : CELLS + 1])
            vt[0, j] = v
            vt[1, j] = now
            start_all(
                [pltpu.make_async_copy(vt.at[i, j], vt_ref.at[i, j], sems.at[i, j]) for i in (0, 1)]
            )
            return v + 2 * H * now + tau[j][:, 0:CELLS]

        out_ref[...] = lax.fori_loop(1, RING, step, tau[0][:, 0:CELLS])
        wait_all(
            [
                pltpu.make_async_copy(vt.at[i, j], vt_ref.at[i, j], sems.at[i, j])
                for i in (0, 1)
                for j in range(1, RING)
            ]
        )


def first_chain(taus, own, others):
    return pl.pallas_call(
        first_kernel,
        out_shape=(field(2, RING), field()),
        in_specs=[ANY] * (RING + 2),
        out_specs=(ANY, VMEM),
        scratch_shapes=[
            pltpu.VMEM((RING, CH, WPAD), F32),
            pltpu.VMEM((RING, CH, WPAD), F32),
            vmem(field(2, RING)),
            vmem(lhs_shape(RING)),
            pltpu.SemaphoreType.DMA((RING,)),
            pltpu.SemaphoreType.DMA((RING,)),
            pltpu.SemaphoreType.DMA((2, RING)),
        ],
        compiler_params=PARAMS,
        name="chain_0",
    )(*taus, own, others)


def prepare_kernel(sizes, *refs):
    block_refs, outs, work = refs[:sizes], refs[sizes : sizes + 2], refs[sizes + 2 :]
    w, ahead, behind, sems, out_sems = work
    _, spot, lead, _ = place()

    @pl.when(spot == lead)
    def _():
        if sizes == 2:
            copies = even_slots(block_refs[0], block_refs[1], w, sems, lead)
        else:
            copies = slots([r.at[:, pl.ds(0, WPAD)] for r in block_refs], w, sems, lead)
        wait_all(start_all(copies))

        def step(j, carry):
            ahead[j] = lhs_forward(w[j][:, 0:576])
            behind[j] = lhs_backward(w[j][:, 0:576])
            return carry

        lax.fori_loop(0, RING, step, 0)
        wait_all(
            start_all(
                [
                    pltpu.make_async_copy(ahead, outs[0], out_sems.at[0]),
                    pltpu.make_async_copy(behind, outs[1], out_sems.at[1]),
                ]
            )
        )


def prepare(blocks, name):
    return pl.pallas_call(
        lambda *refs: prepare_kernel(len(blocks), *refs),
        out_shape=(lhs_shape(RING), lhs_shape(RING)),
        in_specs=[ANY] * len(blocks),
        out_specs=(ANY, ANY),
        scratch_shapes=[
            pltpu.VMEM((RING, CH, WPAD), F32),
            vmem(lhs_shape(RING)),
            vmem(lhs_shape(RING)),
            pltpu.SemaphoreType.DMA((RING,)),
            pltpu.SemaphoreType.DMA((2,)),
        ],
        compiler_params=PARAMS,
        cost_estimate=pl.CostEstimate(flops=0, bytes_accessed=20 << 20, transcendentals=0),
        name=name,
    )(*blocks)


def chain_kernel(stage, *refs):
    tau_refs, ahead_ref, v_ref = refs[:RING], refs[RING], refs[RING + 1]
    vt_ref, out_ref, tau, vt, ahead, tau_sems, ahead_sems, sems = refs[-8:]
    ring, spot, lead, _ = place()

    @pl.when((ring == stage) & (spot == lead))
    def _():
        start_all(slots(tau_refs, tau, tau_sems, lead))

        def ahead_copy(j):
            return pltpu.make_async_copy(ahead_ref.at[j], ahead.at[j], ahead_sems.at[j])

        start_all([ahead_copy(j) for j in range(RING)])

        def step(j, v):
            ahead_copy(j).wait()
            pltpu.make_async_copy(tau_refs[0], tau.at[j], tau_sems.at[j]).wait()
            now = jnp.tanh(conv(ahead[j], v, 1) + tau[j][:, CELLS : CELLS + 1])
            vt[0, j] = v
            vt[1, j] = now
            start_all(
                [pltpu.make_async_copy(vt.at[i, j], vt_ref.at[i, j], sems.at[i, j]) for i in (0, 1)]
            )
            return v + 2 * H * now + tau[j][:, 0:CELLS]

        out_ref[...] = lax.fori_loop(0, RING, step, v_ref[...])
        wait_all(
            [
                pltpu.make_async_copy(vt.at[i, j], vt_ref.at[i, j], sems.at[i, j])
                for i in (0, 1)
                for j in range(RING)
            ]
        )


def chain(stage, taus, ahead, v, vt):
    args = [*taus, ahead, v]
    return pl.pallas_call(
        lambda *refs: chain_kernel(stage, *refs),
        out_shape=(field(2, RING), field()),
        in_specs=[ANY] * (RING + 1) + [VMEM, ANY],
        out_specs=(ANY, VMEM),
        scratch_shapes=[
            pltpu.VMEM((RING, CH, WPAD), F32),
            vmem(field(2, RING)),
            vmem(lhs_shape(RING)),
            pltpu.SemaphoreType.DMA((RING,)),
            pltpu.SemaphoreType.DMA((RING,)),
            pltpu.SemaphoreType.DMA((2, RING)),
        ],
        input_output_aliases={len(args): 0},
        compiler_params=PARAMS,
        name=f"chain_{stage}",
    )(*args, vt)


def correction(ahead, behind, v, t0, b1, a):
    t1 = jnp.tanh(conv(ahead, v + H * t0, 1) + b1)
    shift = H * conv(behind, (1.0 - t1 * t1) * a, -1)
    s0 = 1.0 - t0 * t0
    return shift, s0 * (H * (shift - a)), (2 * H) * s0


def back_step(behind, mu, shift, part, slope):
    return mu + shift + conv(behind, slope * mu + part, -1)


def middle_kernel(last, *refs):
    two_refs, (vt_ref, ahead_ref, behind_ref) = refs[:RING], refs[RING : RING + 3]
    outs = refs[-(RING + 3 + 7) : -7]
    two, vt, ahead, behind, out, two_sems, sems = refs[-7:]
    ring, spot, lead, _ = place()

    @pl.when((spot == lead) & (ring < last))
    def _():
        copies = start_all(slots(two_refs, two, two_sems, lead))
        copies += start_all(
            [
                pltpu.make_async_copy(vt_ref, vt, sems.at[0]),
                pltpu.make_async_copy(ahead_ref, ahead, sems.at[1]),
                pltpu.make_async_copy(behind_ref, behind, sems.at[2]),
            ]
        )
        wait_all(copies)
        copies = start_all(
            [
                pltpu.make_async_copy(vt.at[0, (lead + k) % RING], outs[k], two_sems.at[k])
                for k in range(RING)
            ]
        )

        def step(j, carry):
            b1, a = two[j][:, 576:577], two[j][:, WPAD:BLK]
            got = correction(ahead[j], behind[j], vt[0, j], vt[1, j], b1, a)
            for i in range(3):
                out[i, j] = got[i]
            return carry

        lax.fori_loop(0, RING, step, 0, unroll=2)
        copies += start_all(
            [pltpu.make_async_copy(out.at[i], outs[RING + i], sems.at[i]) for i in range(3)]
        )
        wait_all(copies)


def middle(last, twos, vt, ahead, behind, vs):
    args = [*twos, vt, ahead, behind]
    out = pl.pallas_call(
        lambda *refs: middle_kernel(last, *refs),
        out_shape=(field(),) * RING + (field(RING),) * 3,
        in_specs=[ANY] * (2 * RING + 3),
        out_specs=(ANY,) * (RING + 3),
        scratch_shapes=[
            pltpu.VMEM((RING, CH, BLK), F32),
            vmem(field(2, RING)),
            vmem(lhs_shape(RING)),
            vmem(lhs_shape(RING)),
            vmem(field(3, RING)),
            pltpu.SemaphoreType.DMA((RING,)),
            pltpu.SemaphoreType.DMA((3,)),
        ],
        input_output_aliases={len(args) + k: k for k in range(RING)},
        compiler_params=PARAMS,
        name="middle",
    )(*args, *vs)
    return out[:RING], out[RING:]


def turn_kernel(stage, *refs):
    tau_refs, two_refs = refs[:RING], refs[RING : 2 * RING]
    lhs_refs, v_ref = refs[2 * RING : 2 * RING + 4], refs[2 * RING + 4]
    v_refs = refs[2 * RING + 5 : 3 * RING + 5]
    mu_refs = refs[3 * RING + 5 : 4 * RING + 5]
    out_ref, tau, two, vs, mus, lhs, out, sems, lhs_sems = refs[4 * RING + 5 :]
    ring, spot, lead, _ = place()

    @pl.when((ring == stage) & (spot == lead))
    def _():
        def lhs_copy(i, j):
            return pltpu.make_async_copy(lhs_refs[i].at[j], lhs.at[i, j], lhs_sems.at[i, j])

        start_all(slots(tau_refs, tau, sems.at[0], lead))
        start_all([lhs_copy(0, j) for j in range(RING)])
        start_all(slots(two_refs, two, sems.at[1], lead))
        start_all([lhs_copy(i, j) for j in range(RING) for i in (2, 3)])
        start_all([lhs_copy(1, RING - 1 - j) for j in range(RING)])

        def ahead_step(j, v):
            lhs_copy(0, j).wait()
            pltpu.make_async_copy(tau_refs[0], tau.at[j], sems.at[0, j]).wait()
            now = jnp.tanh(conv(lhs[0, j], v, 1) + tau[j][:, CELLS : CELLS + 1])
            vs[j] = v
            return v + 2 * H * now + tau[j][:, 0:CELLS], now

        def correct(j, v, t0):
            b1, a = two[j][:, 576:577], two[j][:, WPAD:BLK]
            got = correction(lhs[2, j], lhs[3, j], v, t0, b1, a)
            for i in range(3):
                out[i, j] = got[i]

        def arrive(j):
            pltpu.make_async_copy(two_refs[0], two.at[j], sems.at[1, j]).wait()
            lhs_copy(2, j).wait()
            lhs_copy(3, j).wait()

        def step(j, carry):
            v, old_v, old_t = carry
            arrive(j - 1)
            new_v, now = ahead_step(j, v)
            correct(j - 1, old_v, old_t)
            return new_v, v, now

        start = v_ref[...]
        v, now = ahead_step(0, start)
        _, v, now = lax.fori_loop(1, RING, step, (v, start, now))
        copies = start_all(
            [
                pltpu.make_async_copy(vs.at[(lead + k) % RING], v_refs[k], sems.at[0, k])
                for k in range(RING)
            ]
        )
        arrive(RING - 1)
        correct(RING - 1, v, now)

        def back(k, mu):
            j = RING - 1 - k
            lhs_copy(1, j).wait()
            mus[j] = mu
            return back_step(lhs[1, j], mu, out[0, j], out[1, j], out[2, j])

        out_ref[...] = lax.fori_loop(0, RING, back, two[RING - 1][:, WPAD:BLK])
        copies += start_all(
            [
                pltpu.make_async_copy(mus.at[(lead + k) % RING], mu_refs[k], sems.at[1, k])
                for k in range(RING)
            ]
        )
        wait_all(copies)


def turn(stage, taus, twos, lhs, v):
    out = pl.pallas_call(
        lambda *refs: turn_kernel(stage, *refs),
        out_shape=(field(),) * (2 * RING + 1),
        in_specs=[ANY] * (2 * RING + 4) + [VMEM],
        out_specs=(ANY,) * (2 * RING) + (VMEM,),
        scratch_shapes=[
            pltpu.VMEM((RING, CH, WPAD), F32),
            pltpu.VMEM((RING, CH, BLK), F32),
            vmem(field(RING)),
            vmem(field(RING)),
            vmem(lhs_shape(4, RING)),
            vmem(field(3, RING)),
            pltpu.SemaphoreType.DMA((2, RING)),
            pltpu.SemaphoreType.DMA((4, RING)),
        ],
        compiler_params=PARAMS,
        name="turn",
    )(*taus, *twos, *lhs, v)
    return out[:RING], out[RING : 2 * RING], out[2 * RING]


def back_kernel(stage, *refs):
    part_refs, behind_ref, mu_ref = refs[:3], refs[3], refs[4]
    outs = refs[-(RING + 1 + 5) : -5]
    parts, behind, mus, sems, out_sems = refs[-5:]
    ring, spot, lead, _ = place()

    @pl.when((ring == stage) & (spot == lead))
    def _():
        def copies(j):
            return [
                pltpu.make_async_copy(behind_ref.at[j], behind.at[j], sems.at[3, j]),
            ] + [
                pltpu.make_async_copy(part_refs[i].at[j], parts.at[i, j], sems.at[i, j])
                for i in range(3)
            ]

        for j in range(RING - 1, -1, -1):
            start_all(copies(j))

        def step(k, mu):
            j = RING - 1 - k
            wait_all(copies(j))
            mus[j] = mu
            return back_step(behind[j], mu, parts[0, j], parts[1, j], parts[2, j])

        steps = RING - 1 if stage == 0 else RING
        end = lax.fori_loop(0, steps, step, mu_ref[...])
        if stage == 0:
            mus[0] = end
            wait_all(copies(0))
        outs[RING][...] = end
        wait_all(
            start_all(
                [
                    pltpu.make_async_copy(mus.at[(lead + k) % RING], outs[k], out_sems.at[k])
                    for k in range(RING)
                ]
            )
        )


def back_chain(stage, parts, behind, mu, mus):
    args = [*parts, behind, mu]
    aliases = {len(args) + k: k for k in range(RING)}
    out = pl.pallas_call(
        lambda *refs: back_kernel(stage, *refs),
        out_shape=(field(),) * (RING + 1),
        in_specs=[ANY] * 4 + [VMEM] + [ANY] * RING,
        out_specs=(ANY,) * RING + (VMEM,),
        scratch_shapes=[
            vmem(field(3, RING)),
            vmem(lhs_shape(RING)),
            vmem(field(RING)),
            pltpu.SemaphoreType.DMA((4, RING)),
            pltpu.SemaphoreType.DMA((RING,)),
        ],
        input_output_aliases=aliases,
        compiler_params=PARAMS,
        name=f"back_{stage}",
    )(*args, *mus)
    return out[:RING], out[RING]


def fetch(refs, target, sem):
    _, spot, lead, _ = place()
    step = (spot + RING - lead) % RING
    for k in range(RING):

        @pl.when(step == k)
        def _():
            copy = pltpu.make_async_copy(refs[k], target, sem)
            copy.start()
            copy.wait()


def early_kernel(*refs):
    tau_ref, even_ref, two_ref, c_ref, refs = refs[0], refs[1], refs[2], refs[3], refs[4:]
    v_refs = refs[:RING]
    states_ref, keep_ref, lhs_ref, v_ref, sem = refs[RING:]
    fetch(v_refs, v_ref, sem)
    ring, spot, _, _ = place()

    @pl.when((ring == 0) & (spot == 0))
    def _():
        v_ref[...] = swap(c_ref[...])

    v = v_ref[...]
    w0, w1 = even_ref[:, 0:576], two_ref[:, 0:576]
    t0 = jnp.tanh(conv(lhs_forward(w0), v, 1) + tau_ref[:, CELLS : CELLS + 1])
    m = v + H * t0
    b1, a = two_ref[:, 576:577], two_ref[:, WPAD:BLK]
    t1 = jnp.tanh(conv(lhs_forward(w1), m, 1) + b1)
    s1 = 1.0 - t1 * t1
    s0 = 1.0 - t0 * t0
    lhs_ref[0] = lhs_backward(w0)
    behind = lhs_backward(w1)
    lhs_ref[1] = behind
    shift = H * conv(behind, s1 * a, -1)
    states_ref[0] = swap(m)
    slot = tau_ref[:, 0:CELLS]
    keep = jnp.where((ring == 0) & (spot == 0), 1.0, 0.0)
    states_ref[1] = swap(jnp.where(keep > 0.0, slot, v + 2 * H * t0 + slot))
    keep_ref[0] = v
    keep_ref[1] = m
    keep_ref[2] = s0
    keep_ref[3] = s1
    keep_ref[4] = shift
    keep_ref[5] = s0 * (H * (shift - a))


def early(tau, even, two, c, vs):
    return pl.pallas_call(
        early_kernel,
        out_shape=(field(2), field(6), lhs_shape(2)),
        in_specs=[VMEM] * 4 + [ANY] * RING,
        scratch_shapes=[vmem(field()), pltpu.SemaphoreType.DMA],
        compiler_params=PARAMS,
        name="early",
    )(tau, even, two, c, *vs)


def late_kernel(*refs):
    keep_ref, lhs_ref = refs[:2]
    mu_refs = refs[2 : 2 + RING]
    adjoints_ref, mine_ref, other_ref, mu_scratch, sem = refs[2 + RING :]
    fetch(mu_refs, mu_scratch, sem)
    mu = mu_scratch[...]
    s0 = keep_ref[2]
    odd_product = keep_ref[3] * mu
    odd = mu + H * conv(lhs_ref[1], odd_product, -1)
    even_term = (H / 8) * (s0 * odd)
    odd_term = (H / 8) * odd_product
    odd_grad = correlate(odd_term, keep_ref[1])
    even_grad = correlate(even_term, keep_ref[0])
    even = back_step(lhs_ref[0], mu, keep_ref[4], keep_ref[5], (2 * H) * s0)
    adjoints_ref[0] = swap(even)
    adjoints_ref[1] = swap(odd)
    pad = (CH, WPAD - 576)
    even_bias = jnp.broadcast_to(jnp.sum(even_term, axis=1, keepdims=True), pad)
    odd_bias = jnp.broadcast_to(jnp.sum(odd_term, axis=1, keepdims=True), pad)

    def write(ref, grad, bias):
        ref[:, 0:576] = grad
        ref[:, 576:WPAD] = bias

    core = place()[3]

    @pl.when(core == 0)
    def _():
        write(mine_ref, even_grad, even_bias)
        write(other_ref, odd_grad, odd_bias)

    @pl.when(core == 1)
    def _():
        write(mine_ref, odd_grad, odd_bias)
        write(other_ref, even_grad, even_bias)


def late(keep, lhs, mus):
    grad = jax.ShapeDtypeStruct((CH, WPAD), F32)
    return pl.pallas_call(
        late_kernel,
        out_shape=(field(2), grad, grad),
        in_specs=[VMEM] * 2 + [ANY] * RING,
        scratch_shapes=[vmem(field()), pltpu.SemaphoreType.DMA],
        compiler_params=PARAMS,
        name="late",
    )(keep, lhs, *mus)


def finish_kernel(mine_ref, other_ref, grad_ref, bias_ref):
    core = place()[3]
    r = lax.broadcasted_iota(jnp.int32, (CH, CH), 0)
    c = lax.broadcasted_iota(jnp.int32, (CH, CH), 1)

    def write(slot, ref):
        grad_ref[slot] = ref[:, 0:576]
        spread = jnp.broadcast_to(ref[:, 576:577], (CH, CH))
        bias_ref[slot : slot + 1] = jnp.sum(jnp.where(r == c, spread, 0.0), axis=0, keepdims=True)

    @pl.when(core == 0)
    def _():
        write(0, mine_ref)
        write(1, other_ref)

    @pl.when(core == 1)
    def _():
        write(1, mine_ref)
        write(0, other_ref)


def finish(mine, other):
    return pl.pallas_call(
        finish_kernel,
        out_shape=(
            jax.ShapeDtypeStruct((2, CH, 576), F32),
            jax.ShapeDtypeStruct((2, CH), F32),
        ),
        compiler_params=PARAMS,
        name="finish",
    )(mine, other)


def tie(*values):
    return lax.optimization_barrier(values)


NEAR = (1, 7, 2, 6, 3, 5, 4)
FAR = NEAR[::-1]


def body(coarse_guess, adjoint_guess, weights, biases):
    images = lax.axis_size("dp")
    groups = lax.axis_size("layer") // RING
    last = groups - 1

    def device(x, z, d):
        return (RING * x + z % RING) * images + d

    def lead(d):
        return (RING // 2) * (d % 2)

    everyone = [(x, d) for x in range(groups) for d in range(images)]

    def gather(value, k):
        pairs = [(device(x, lead(d) + k, d), device(x, lead(d), d)) for x, d in everyone]
        return lax.ppermute(value, AXES, pairs)

    def gather_both(value, k):
        pairs = [
            (device(x, z + k, d), device(x, z, d)) for x, d in everyone for z in (0, RING // 2)
        ]
        return lax.ppermute(value, AXES, pairs)

    def hand_over(value):
        pairs = [(device(x, lead(d), d ^ 1), device(x, lead(d), d)) for x, d in everyone]
        return lax.ppermute(value, AXES, pairs)

    def scatter(value, k):
        pairs = [(device(x, lead(d), d), device(x, lead(d) + k, d)) for x, d in everyone]
        return lax.ppermute(value, AXES, pairs)

    def hop(value, source, target):
        pairs = [
            (device(source, lead(d), d), device(target, lead(d), d)) for d in range(images)
        ]
        return lax.ppermute(value, AXES, pairs)

    c, a = coarse_guess[0, 0], adjoint_guess[0, 0]
    low, high, mid, tau, even, two = relax(c, a, weights, biases)
    taus, twos = [tau] + [None] * (RING - 1), [two] + [None] * (RING - 1)
    for k in NEAR:
        taus[k] = gather_both(mid if k == RING // 2 else low if k < RING // 2 else high, k)
    others = hand_over(stack(taus[1:]))
    vt, end = first_chain(taus, even, others)
    v = hop(end, 0, 1)
    even_late = tie(end, even)[1]
    ahead0, behind0 = prepare([even_late, others], "prepare")
    for k in NEAR:
        twos[k] = gather(two, k)
    for stage in range(1, last):
        vt, end = chain(stage, taus, ahead0, v, vt)
        v = hop(end, stage, stage + 1)
    ahead1, behind1 = prepare(twos, "prepare2")
    vs, mus, end = turn(last, taus, twos, [ahead0, behind0, ahead1, behind1], v)
    mu = hop(end, last, last - 1)
    vs, parts = middle(last, twos, vt, ahead1, behind1, vs)
    own_v = [vs[0]] + [None] * (RING - 1)
    for stage in range(last - 1, -1, -1):
        if stage == last - 1:
            chunk, gate = FAR[:3], parts[0]
        elif stage == last - 2:
            chunk, gate = FAR[3:], end
        else:
            chunk = ()
        for k in chunk:
            own_v[k] = scatter(tie(gate, vs[k])[1], k)
        if stage == last - 1:
            got = tie(mu, *parts, *[own_v[k] for k in chunk])
            mu, parts = got[0], got[1:4]
            for k, value in zip(chunk, got[4:]):
                own_v[k] = value
        if stage == 0:
            states, keep, lhs = early(tau, even, two, c, own_v)
            mu, keep = tie(mu, keep)
        mus, end = back_chain(stage, parts, behind0, mu, mus)
        if stage > 0:
            mu = hop(end, stage, stage - 1)
    own_mu = [mus[0]] + [None] * (RING - 1)
    for k in FAR:
        own_mu[k] = scatter(mus[k], k)
    adjoints, mine, other = late(keep, lhs, own_mu)
    mine = mine + lax.ppermute(other, "dp", [(i, i ^ 1) for i in range(images)])
    for flip in (2, 6):
        mine = mine + lax.ppermute(mine, "dp", [(i, i ^ flip) for i in range(images)])
    other = lax.ppermute(mine, "dp", [(i, i ^ 1) for i in range(images)])
    grad, bias = finish(mine, other)
    return states[:, None], adjoints[:, None], grad, bias


def solution(mesh):
    return jax.shard_map(
        body,
        mesh=mesh,
        in_specs=(
            P("layer", "dp", None, None),
            P("layer", "dp", None, None),
            P("layer", None, None),
            P("layer", None),
        ),
        out_specs=(
            P("layer", "dp", None, None),
            P("layer", "dp", None, None),
            P("layer", None, None),
            P("layer", None),
        ),
        check_vma=False,
    )
```

```python
import jax
import jax.numpy as jnp
from jax import lax
from jax.experimental import pallas as pl
from jax.experimental.pallas import tpu as pltpu
from jax.sharding import PartitionSpec as P

F32 = jnp.float32
BF16 = jnp.bfloat16
H = 0.125
CH, CELLS = 64, 512
WPAD = 640
BLK = WPAD + CELLS
RING = 8
AXES = ("layer", "dp")
ANY = pl.BlockSpec(memory_space=pl.ANY)
HBM = pl.BlockSpec(memory_space=pltpu.HBM)
VMEM = pl.BlockSpec(memory_space=pltpu.VMEM)
PARAMS = pltpu.CompilerParams(vmem_limit_bytes=40 << 20)


def split(x):
    hi = x.astype(BF16)
    return hi, (x - hi.astype(F32)).astype(BF16)


def lane_index():
    return lax.broadcasted_iota(jnp.int32, (CH, 128), 1)


def columns(x):
    return [x[:, 128 * a : 128 * (a + 1)] for a in range(4)]


def swap(x):
    parts, lane, out = columns(x), lane_index(), []
    for a in range(4):
        acc = None
        for b in range(4):
            shift = ((b - a) * 32) % 128
            part = parts[b] if shift == 0 else pltpu.roll(parts[b], shift, 1)
            acc = part if acc is None else jnp.where(lane >= 32 * b, part, acc)
        out.append(acc)
    return jnp.concatenate(out, 1)


def lhs_forward(w):
    hi = w.astype(BF16).astype(F32)
    lo = w - hi
    rows = []
    for t in range(9):
        a, b = hi[:, 64 * t : 64 * t + 64], lo[:, 64 * t : 64 * t + 64]
        rows.append(jnp.concatenate([a, a, b], 1).astype(BF16))
    return jnp.concatenate(rows, 0)


def lhs_backward(w):
    wt = w.T
    hi = wt.astype(BF16).astype(F32)
    lo = wt - hi
    return jnp.concatenate([hi, hi, lo], 1).astype(BF16)


def conv(lhs, x, sign):
    hi, lo = split(x)
    z = jnp.dot(lhs, jnp.concatenate([hi, lo, hi], 0), preferred_element_type=F32)
    lane = lane_index()
    q = lane % 32
    lower, upper, right, left = lane < 96, lane >= 32, q < 31, q > 0

    def tap(a, e, col):
        t = 3 * (sign * a + 1) + (sign * e + 1)
        return z[64 * t : 64 * t + 64, 128 * col : 128 * col + 128]

    out = []
    for col in range(4):
        s = []
        for e in (-1, 0, 1):
            if col < 3:
                up = tap(1, e, col + 1)
            else:
                up = jnp.where(lower, pltpu.roll(tap(1, e, 0), 96, 1), 0.0)
            if col > 0:
                down = tap(-1, e, col - 1)
            else:
                down = jnp.where(upper, pltpu.roll(tap(-1, e, 3), 32, 1), 0.0)
            s.append(tap(0, e, col) + up + down)
        out.append(
            s[1]
            + jnp.where(right, pltpu.roll(s[2], 127, 1), 0.0)
            + jnp.where(left, pltpu.roll(s[0], 1, 1), 0.0)
        )
    return jnp.concatenate(out, 1)


def patches(x):
    lane = lane_index()
    q = lane % 32
    lower, upper, right, left = lane < 96, lane >= 32, q < 31, q > 0
    mid = columns(x)
    base = {
        0: mid,
        1: [jnp.where(right, pltpu.roll(c, 127, 1), 0.0) for c in mid],
        -1: [jnp.where(left, pltpu.roll(c, 1, 1), 0.0) for c in mid],
    }
    hi, lo = [], []
    for a in (-1, 0, 1):
        for e in (-1, 0, 1):
            c = base[e]
            if a == 1:
                c = c[1:] + [jnp.where(lower, pltpu.roll(c[0], 96, 1), 0.0)]
            elif a == -1:
                c = [jnp.where(upper, pltpu.roll(c[3], 32, 1), 0.0)] + c[:3]
            h, l = split(jnp.concatenate(c, 1))
            hi.append(h)
            lo.append(l)
    return jnp.concatenate(hi, 0), jnp.concatenate(lo, 0)


def dot_t(a, b):
    return lax.dot_general(a, b, (((1,), (1,)), ((), ())), preferred_element_type=F32)


def correlate(term, x):
    t_hi, t_lo = split(term)
    p_hi, p_lo = patches(x)
    return dot_t(t_hi, p_hi) + dot_t(t_hi, p_lo) + dot_t(t_lo, p_hi)


def as_column(row):
    r = lax.broadcasted_iota(jnp.int32, (CH, CH), 0)
    c = lax.broadcasted_iota(jnp.int32, (CH, CH), 1)
    spread = jnp.broadcast_to(row, (CH, CH))
    return jnp.sum(jnp.where(r == c, spread, 0.0), axis=1, keepdims=True)


def place():
    layer, image = lax.axis_index("layer"), lax.axis_index("dp")
    core = image % 2
    return layer // RING, layer % RING, RING // 2 - 1 + core, core


def start_all(copies):
    for copy in copies:
        copy.start()
    return copies


def wait_all(copies):
    for copy in copies:
        copy.wait()


def field(*lead):
    return jax.ShapeDtypeStruct((*lead, CH, CELLS), F32)


def lhs_shape(*lead):
    return jax.ShapeDtypeStruct((*lead, 9 * CH, 3 * CH), BF16)


def vmem(shape):
    return pltpu.VMEM(shape.shape, shape.dtype)


def relax_kernel(c_hbm, a_hbm, w_hbm, b_hbm, one_ref, two_ref, c_ref, a_ref, w_ref, b_ref, sems):
    copies = start_all(
        [
            pltpu.make_async_copy(source, target, sems.at[i])
            for i, (source, target) in enumerate(
                [(b_hbm, b_ref), (w_hbm, w_ref), (c_hbm, c_ref), (a_hbm, a_ref)]
            )
        ]
    )
    wait_all(copies[:3])
    c = swap(c_ref[...])
    w0, w1 = w_ref[0], w_ref[1]
    b0, b1 = as_column(b_ref[0:1]), as_column(b_ref[1:2])
    t0 = jnp.tanh(conv(lhs_forward(w0), c, 1) + b0)
    t1 = jnp.tanh(conv(lhs_forward(w1), c + H * t0, 1) + b1)
    pad = WPAD - 576
    one_ref[:, 0:576] = w0
    one_ref[:, 576:WPAD] = jnp.broadcast_to(b0, (CH, pad))
    ring, spot, _, _ = place()
    keep = jnp.where((ring == 0) & (spot == 0), 1.0, 0.0)
    one_ref[:, WPAD:BLK] = jnp.where(keep > 0.0, c + H * t0 + H * t1, H * (t1 - t0))
    two_ref[:, 0:576] = w1
    two_ref[:, 576:WPAD] = jnp.broadcast_to(b1, (CH, pad))
    wait_all(copies[3:])
    two_ref[:, WPAD:BLK] = swap(a_ref[...])


def relax(c, a, w, b):
    shape = jax.ShapeDtypeStruct((CH, BLK), F32)
    return pl.pallas_call(
        relax_kernel,
        out_shape=(shape, shape),
        in_specs=[HBM] * 4,
        scratch_shapes=[
            pltpu.VMEM(c.shape, F32),
            pltpu.VMEM(a.shape, F32),
            pltpu.VMEM(w.shape, F32),
            pltpu.VMEM(b.shape, F32),
            pltpu.SemaphoreType.DMA((4,)),
        ],
        compiler_params=pltpu.CompilerParams(vmem_limit_bytes=63 << 20),
        name="relax",
    )(c, a, w, b)


MATRIX = pl.ds(0, WPAD)
REST = pl.ds(CELLS, WPAD)
BIAS = WPAD - 576


def slots(refs, target, sems, lead, part=None):
    if part is not None:
        refs = [ref.at[:, part] for ref in refs]
    copies = []
    for k, ref in enumerate(refs):
        j = (lead + k) % RING
        copies.append(pltpu.make_async_copy(ref, target.at[j], sems.at[j]))
    return copies


HALF = RING // 2


def half(array, i):
    return array.at[pl.ds(HALF * i, HALF)]


def half_out(vt, vt_ref, sems, part):
    return start_all(
        [
            pltpu.make_async_copy(half(vt.at[i], part), half(vt_ref.at[i], part), sems.at[i, part])
            for i in (0, 1)
        ]
    )


def first_kernel(*refs):
    one_refs = refs[:RING]
    vt_ref, out_ref, tau, even, vt, lhs, tau_sems, even_sems, sems = refs[RING:]
    ring, spot, lead, _ = place()

    @pl.when((ring == 0) & (spot == lead))
    def _():
        copies = slots(one_refs, even, even_sems, lead, MATRIX)
        copies += slots(one_refs, tau, tau_sems, lead, REST)
        wait_all(start_all(copies))

        def prepare(j, carry):
            lhs[j] = lhs_forward(even[j][:, 0:576])
            return carry

        lax.fori_loop(1, RING, prepare, 0)

        def step(j, v):
            now = jnp.tanh(conv(lhs[j], v, 1) + tau[j][:, BIAS : BIAS + 1])
            vt[0, j] = v
            vt[1, j] = now
            return v + 2 * H * now + tau[j][:, WPAD - CELLS :]

        v = lax.fori_loop(1, HALF, step, tau[0][:, WPAD - CELLS :])
        copies = half_out(vt, vt_ref, sems, 0)
        out_ref[...] = lax.fori_loop(HALF, RING, step, v)
        wait_all(copies + half_out(vt, vt_ref, sems, 1))


def first_chain(ones):
    return pl.pallas_call(
        first_kernel,
        out_shape=(field(2, RING), field()),
        in_specs=[ANY] * RING,
        out_specs=(ANY, VMEM),
        scratch_shapes=[
            pltpu.VMEM((RING, CH, WPAD), F32),
            pltpu.VMEM((RING, CH, WPAD), F32),
            vmem(field(2, RING)),
            vmem(lhs_shape(RING)),
            pltpu.SemaphoreType.DMA((RING,)),
            pltpu.SemaphoreType.DMA((RING,)),
            pltpu.SemaphoreType.DMA((2, 2)),
        ],
        compiler_params=PARAMS,
        name="chain_0",
    )(*ones)


def prepare_kernel(*refs):
    block_refs, outs = refs[:RING], refs[RING : RING + 2]
    w, ahead, behind, sems, out_sems = refs[RING + 2 :]
    _, spot, lead, _ = place()

    @pl.when(spot == lead)
    def _():
        wait_all(start_all(slots(block_refs, w, sems, lead, MATRIX)))

        def step(j, carry):
            ahead[j] = lhs_forward(w[j][:, 0:576])
            behind[j] = lhs_backward(w[j][:, 0:576])
            return carry

        lax.fori_loop(0, RING, step, 0)
        wait_all(
            start_all(
                [
                    pltpu.make_async_copy(ahead, outs[0], out_sems.at[0]),
                    pltpu.make_async_copy(behind, outs[1], out_sems.at[1]),
                ]
            )
        )


def prepare(blocks, name):
    return pl.pallas_call(
        prepare_kernel,
        out_shape=(lhs_shape(RING), lhs_shape(RING)),
        in_specs=[ANY] * RING,
        out_specs=(ANY, ANY),
        scratch_shapes=[
            pltpu.VMEM((RING, CH, WPAD), F32),
            vmem(lhs_shape(RING)),
            vmem(lhs_shape(RING)),
            pltpu.SemaphoreType.DMA((RING,)),
            pltpu.SemaphoreType.DMA((2,)),
        ],
        compiler_params=PARAMS,
        cost_estimate=pl.CostEstimate(flops=0, bytes_accessed=20 << 20, transcendentals=0),
        name=name,
    )(*blocks)


def chain_kernel(stage, *refs):
    tau_refs, ahead_ref, v_ref = refs[:RING], refs[RING], refs[RING + 1]
    vt_ref, out_ref, tau, vt, ahead, tau_sems, ahead_sems, sems = refs[-8:]
    ring, spot, lead, _ = place()

    @pl.when((ring == stage) & (spot == lead))
    def _():
        copies = start_all(slots(tau_refs, tau, tau_sems, lead, REST))
        halves = start_all(
            [
                pltpu.make_async_copy(half(ahead_ref, i), half(ahead, i), ahead_sems.at[i])
                for i in (0, 1)
            ]
        )
        wait_all(copies + halves[:1])

        def step(j, v):
            now = jnp.tanh(conv(ahead[j], v, 1) + tau[j][:, BIAS : BIAS + 1])
            vt[0, j] = v
            vt[1, j] = now
            return v + 2 * H * now + tau[j][:, WPAD - CELLS :]

        v = lax.fori_loop(0, HALF, step, v_ref[...], unroll=2)
        wait_all(halves[1:])
        copies = half_out(vt, vt_ref, sems, 0)
        out_ref[...] = lax.fori_loop(HALF, RING, step, v, unroll=2)
        wait_all(copies + half_out(vt, vt_ref, sems, 1))


def chain(stage, taus, ahead, v, vt):
    args = [*taus, ahead, v]
    return pl.pallas_call(
        lambda *refs: chain_kernel(stage, *refs),
        out_shape=(field(2, RING), field()),
        in_specs=[ANY] * (RING + 1) + [VMEM, ANY],
        out_specs=(ANY, VMEM),
        scratch_shapes=[
            pltpu.VMEM((RING, CH, WPAD), F32),
            vmem(field(2, RING)),
            vmem(lhs_shape(RING)),
            pltpu.SemaphoreType.DMA((RING,)),
            pltpu.SemaphoreType.DMA((2,)),
            pltpu.SemaphoreType.DMA((2, 2)),
        ],
        input_output_aliases={len(args): 0},
        compiler_params=PARAMS,
        name=f"chain_{stage}",
    )(*args, vt)


def correction(ahead, behind, v, t0, b1, a):
    t1 = jnp.tanh(conv(ahead, v + H * t0, 1) + b1)
    shift = H * conv(behind, (1.0 - t1 * t1) * a, -1)
    s0 = 1.0 - t0 * t0
    return shift, s0 * (H * (shift - a)), (2 * H) * s0


def back_step(behind, mu, shift, part, slope):
    return mu + shift + conv(behind, slope * mu + part, -1)


def middle_kernel(last, *refs):
    two_refs, (vt_ref, ahead_ref, behind_ref) = refs[:RING], refs[RING : RING + 3]
    outs = refs[-(RING + 3 + 7) : -7]
    two, vt, ahead, behind, out, two_sems, sems = refs[-7:]
    ring, spot, lead, _ = place()

    @pl.when((spot == lead) & (ring < last))
    def _():
        copies = start_all(slots(two_refs, two, two_sems, lead))
        copies += start_all(
            [
                pltpu.make_async_copy(vt_ref, vt, sems.at[0]),
                pltpu.make_async_copy(ahead_ref, ahead, sems.at[1]),
                pltpu.make_async_copy(behind_ref, behind, sems.at[2]),
            ]
        )
        wait_all(copies)
        copies = start_all(
            [
                pltpu.make_async_copy(vt.at[0, (lead + k) % RING], outs[k], two_sems.at[k])
                for k in range(RING)
            ]
        )

        def step(j, carry):
            b1, a = two[j][:, 576:577], two[j][:, WPAD:BLK]
            got = correction(ahead[j], behind[j], vt[0, j], vt[1, j], b1, a)
            for i in range(3):
                out[i, j] = got[i]
            return carry

        lax.fori_loop(0, RING, step, 0, unroll=2)
        copies += start_all(
            [pltpu.make_async_copy(out.at[i], outs[RING + i], sems.at[i]) for i in range(3)]
        )
        wait_all(copies)


def middle(last, twos, vt, ahead, behind, vs):
    args = [*twos, vt, ahead, behind]
    out = pl.pallas_call(
        lambda *refs: middle_kernel(last, *refs),
        out_shape=(field(),) * RING + (field(RING),) * 3,
        in_specs=[ANY] * (2 * RING + 3),
        out_specs=(ANY,) * (RING + 3),
        scratch_shapes=[
            pltpu.VMEM((RING, CH, BLK), F32),
            vmem(field(2, RING)),
            vmem(lhs_shape(RING)),
            vmem(lhs_shape(RING)),
            vmem(field(3, RING)),
            pltpu.SemaphoreType.DMA((RING,)),
            pltpu.SemaphoreType.DMA((3,)),
        ],
        input_output_aliases={len(args) + k: k for k in range(RING)},
        compiler_params=PARAMS,
        name="middle",
    )(*args, *vs)
    return out[:RING], out[RING:]


def turn_kernel(stage, *refs):
    tau_refs, two_refs = refs[:RING], refs[RING : 2 * RING]
    lhs_refs, v_ref = refs[2 * RING : 2 * RING + 4], refs[2 * RING + 4]
    v_refs = refs[2 * RING + 5 : 3 * RING + 5]
    mu_refs = refs[3 * RING + 5 : 4 * RING + 5]
    out_ref, tau, two, vs, mus, lhs, out, sems, lhs_sems = refs[4 * RING + 5 :]
    ring, spot, lead, _ = place()

    @pl.when((ring == stage) & (spot == lead))
    def _():
        copies = start_all(slots(tau_refs, tau, sems.at[0], lead, REST))
        matrices = [
            pltpu.make_async_copy(lhs_refs[i], lhs.at[i], lhs_sems.at[i]) for i in range(4)
        ]
        start_all(matrices[:1])
        block_copies = start_all(slots(two_refs, two, sems.at[1], lead))
        start_all(matrices[2:] + matrices[1:2])
        wait_all(copies + matrices[:1])

        def ahead_step(j, v):
            now = jnp.tanh(conv(lhs[0, j], v, 1) + tau[j][:, BIAS : BIAS + 1])
            vs[j] = v
            return v + 2 * H * now + tau[j][:, WPAD - CELLS :], now

        def correct(j, v, t0):
            b1, a = two[j][:, 576:577], two[j][:, WPAD:BLK]
            got = correction(lhs[2, j], lhs[3, j], v, t0, b1, a)
            for i in range(3):
                out[i, j] = got[i]

        def step(j, carry):
            v, old_v, old_t = carry
            new_v, now = ahead_step(j, v)
            correct(j - 1, old_v, old_t)
            return new_v, v, now

        start = v_ref[...]
        v, now = ahead_step(0, start)
        wait_all(block_copies + matrices[2:])
        _, v, now = lax.fori_loop(1, RING, step, (v, start, now))
        copies = start_all(
            [
                pltpu.make_async_copy(vs.at[(lead + k) % RING], v_refs[k], sems.at[0, k])
                for k in range(RING)
            ]
        )
        correct(RING - 1, v, now)
        wait_all(matrices[1:2])

        def back(k, mu):
            j = RING - 1 - k
            mus[j] = mu
            return back_step(lhs[1, j], mu, out[0, j], out[1, j], out[2, j])

        out_ref[...] = lax.fori_loop(0, RING, back, two[RING - 1][:, WPAD:BLK], unroll=2)
        copies += start_all(
            [
                pltpu.make_async_copy(mus.at[(lead + k) % RING], mu_refs[k], sems.at[1, k])
                for k in range(RING)
            ]
        )
        wait_all(copies)


def turn(stage, taus, twos, lhs, v):
    out = pl.pallas_call(
        lambda *refs: turn_kernel(stage, *refs),
        out_shape=(field(),) * (2 * RING + 1),
        in_specs=[ANY] * (2 * RING + 4) + [VMEM],
        out_specs=(ANY,) * (2 * RING) + (VMEM,),
        scratch_shapes=[
            pltpu.VMEM((RING, CH, WPAD), F32),
            pltpu.VMEM((RING, CH, BLK), F32),
            vmem(field(RING)),
            vmem(field(RING)),
            vmem(lhs_shape(4, RING)),
            vmem(field(3, RING)),
            pltpu.SemaphoreType.DMA((2, RING)),
            pltpu.SemaphoreType.DMA((4,)),
        ],
        compiler_params=PARAMS,
        name="turn",
    )(*taus, *twos, *lhs, v)
    return out[:RING], out[RING : 2 * RING], out[2 * RING]


def back_kernel(stage, *refs):
    part_refs, behind_ref, mu_ref = refs[:3], refs[3], refs[4]
    outs = refs[-(RING + 1 + 5) : -5]
    parts, behind, mus, sems, out_sems = refs[-5:]
    ring, spot, lead, _ = place()

    @pl.when((ring == stage) & (spot == lead))
    def _():
        def copies(i):
            return [
                pltpu.make_async_copy(half(source, i), half(target, i), sems.at[n, i])
                for n, (source, target) in enumerate(
                    [(behind_ref, behind)] + [(part_refs[p], parts.at[p]) for p in range(3)]
                )
            ]

        start_all(copies(1) + copies(0))
        wait_all(copies(1))

        def step(k, mu):
            j = RING - 1 - k
            mus[j] = mu
            return back_step(behind[j], mu, parts[0, j], parts[1, j], parts[2, j])

        end = lax.fori_loop(0, HALF, step, mu_ref[...], unroll=2)
        wait_all(copies(0))
        if stage == 0:
            end = lax.fori_loop(HALF, RING - 1, step, end)
            mus[0] = end
        else:
            end = lax.fori_loop(HALF, RING, step, end, unroll=2)
        outs[RING][...] = end
        wait_all(
            start_all(
                [
                    pltpu.make_async_copy(mus.at[(lead + k) % RING], outs[k], out_sems.at[k])
                    for k in range(RING)
                ]
            )
        )


def back_chain(stage, parts, behind, mu, mus):
    args = [*parts, behind, mu]
    aliases = {len(args) + k: k for k in range(RING)}
    out = pl.pallas_call(
        lambda *refs: back_kernel(stage, *refs),
        out_shape=(field(),) * (RING + 1),
        in_specs=[ANY] * 4 + [VMEM] + [ANY] * RING,
        out_specs=(ANY,) * RING + (VMEM,),
        scratch_shapes=[
            vmem(field(3, RING)),
            vmem(lhs_shape(RING)),
            vmem(field(RING)),
            pltpu.SemaphoreType.DMA((4, 2)),
            pltpu.SemaphoreType.DMA((RING,)),
        ],
        input_output_aliases=aliases,
        compiler_params=PARAMS,
        name=f"back_{stage}",
    )(*args, *mus)
    return out[:RING], out[RING]


def fetch(refs, target, sem):
    _, spot, lead, _ = place()
    step = (spot + RING - lead) % RING
    for k in range(RING):

        @pl.when(step == k)
        def _():
            copy = pltpu.make_async_copy(refs[k], target, sem)
            copy.start()
            copy.wait()


def early_kernel(*refs):
    one_ref, two_ref, c_ref, refs = refs[0], refs[1], refs[2], refs[3:]
    v_refs = refs[:RING]
    states_ref, keep_ref, lhs_ref, v_ref, sem = refs[RING:]
    fetch(v_refs, v_ref, sem)
    ring, spot, _, _ = place()

    @pl.when((ring == 0) & (spot == 0))
    def _():
        v_ref[...] = swap(c_ref[...])

    v = v_ref[...]
    w0, w1 = one_ref[:, 0:576], two_ref[:, 0:576]
    t0 = jnp.tanh(conv(lhs_forward(w0), v, 1) + one_ref[:, 576:577])
    m = v + H * t0
    b1, a = two_ref[:, 576:577], two_ref[:, WPAD:BLK]
    t1 = jnp.tanh(conv(lhs_forward(w1), m, 1) + b1)
    s1 = 1.0 - t1 * t1
    s0 = 1.0 - t0 * t0
    lhs_ref[0] = lhs_backward(w0)
    behind = lhs_backward(w1)
    lhs_ref[1] = behind
    shift = H * conv(behind, s1 * a, -1)
    states_ref[0] = swap(m)
    slot = one_ref[:, WPAD:BLK]
    keep = jnp.where((ring == 0) & (spot == 0), 1.0, 0.0)
    states_ref[1] = swap(jnp.where(keep > 0.0, slot, v + 2 * H * t0 + slot))
    keep_ref[0] = v
    keep_ref[1] = m
    keep_ref[2] = s0
    keep_ref[3] = s1
    keep_ref[4] = shift
    keep_ref[5] = s0 * (H * (shift - a))


def early(one, two, c, vs):
    return pl.pallas_call(
        early_kernel,
        out_shape=(field(2), field(6), lhs_shape(2)),
        in_specs=[VMEM] * 3 + [ANY] * RING,
        scratch_shapes=[vmem(field()), pltpu.SemaphoreType.DMA],
        compiler_params=PARAMS,
        name="early",
    )(one, two, c, *vs)


def late_kernel(*refs):
    keep_ref, lhs_ref = refs[:2]
    mu_refs = refs[2 : 2 + RING]
    adjoints_ref, mine_ref, other_ref, mu_scratch, sem = refs[2 + RING :]
    fetch(mu_refs, mu_scratch, sem)
    mu = mu_scratch[...]
    s0 = keep_ref[2]
    odd_product = keep_ref[3] * mu
    odd = mu + H * conv(lhs_ref[1], odd_product, -1)
    even_term = (H / 8) * (s0 * odd)
    odd_term = (H / 8) * odd_product
    odd_grad = correlate(odd_term, keep_ref[1])
    even_grad = correlate(even_term, keep_ref[0])
    even = back_step(lhs_ref[0], mu, keep_ref[4], keep_ref[5], (2 * H) * s0)
    adjoints_ref[0] = swap(even)
    adjoints_ref[1] = swap(odd)
    pad = (CH, WPAD - 576)
    even_bias = jnp.broadcast_to(jnp.sum(even_term, axis=1, keepdims=True), pad)
    odd_bias = jnp.broadcast_to(jnp.sum(odd_term, axis=1, keepdims=True), pad)

    def write(ref, grad, bias):
        ref[:, 0:576] = grad
        ref[:, 576:WPAD] = bias

    core = place()[3]

    @pl.when(core == 0)
    def _():
        write(mine_ref, even_grad, even_bias)
        write(other_ref, odd_grad, odd_bias)

    @pl.when(core == 1)
    def _():
        write(mine_ref, odd_grad, odd_bias)
        write(other_ref, even_grad, even_bias)


def late(keep, lhs, mus):
    grad = jax.ShapeDtypeStruct((CH, WPAD), F32)
    return pl.pallas_call(
        late_kernel,
        out_shape=(field(2), grad, grad),
        in_specs=[VMEM] * 2 + [ANY] * RING,
        scratch_shapes=[vmem(field()), pltpu.SemaphoreType.DMA],
        compiler_params=PARAMS,
        name="late",
    )(keep, lhs, *mus)


def finish_kernel(mine_ref, other_ref, grad_ref, bias_ref):
    core = place()[3]
    r = lax.broadcasted_iota(jnp.int32, (CH, CH), 0)
    c = lax.broadcasted_iota(jnp.int32, (CH, CH), 1)

    def write(slot, ref):
        grad_ref[slot] = ref[:, 0:576]
        spread = jnp.broadcast_to(ref[:, 576:577], (CH, CH))
        bias_ref[slot : slot + 1] = jnp.sum(jnp.where(r == c, spread, 0.0), axis=0, keepdims=True)

    @pl.when(core == 0)
    def _():
        write(0, mine_ref)
        write(1, other_ref)

    @pl.when(core == 1)
    def _():
        write(1, mine_ref)
        write(0, other_ref)


def finish(mine, other):
    return pl.pallas_call(
        finish_kernel,
        out_shape=(
            jax.ShapeDtypeStruct((2, CH, 576), F32),
            jax.ShapeDtypeStruct((2, CH), F32),
        ),
        compiler_params=PARAMS,
        name="finish",
    )(mine, other)


def tie(*values):
    return lax.optimization_barrier(values)


NEAR = (1, 7, 2, 6, 3, 5, 4)
FAR = NEAR[::-1]


def body(coarse_guess, adjoint_guess, weights, biases):
    images = lax.axis_size("dp")
    groups = lax.axis_size("layer") // RING
    last = groups - 1

    def device(x, z, d):
        return (RING * x + z % RING) * images + d

    def lead(d):
        return RING // 2 - 1 + d % 2

    everyone = [(x, d) for x in range(groups) for d in range(images)]

    def gather(value, k):
        pairs = [(device(x, lead(d) + k, d), device(x, lead(d), d)) for x, d in everyone]
        return lax.ppermute(value, AXES, pairs)

    def scatter(value, k):
        pairs = [(device(x, lead(d), d), device(x, lead(d) + k, d)) for x, d in everyone]
        return lax.ppermute(value, AXES, pairs)

    def hop(value, source, target):
        pairs = [
            (device(source, lead(d), d), device(target, lead(d), d)) for d in range(images)
        ]
        return lax.ppermute(value, AXES, pairs)

    c, a = coarse_guess[0, 0], adjoint_guess[0, 0]
    one, two = relax(c, a, weights, biases)
    ones, twos = [one] + [None] * (RING - 1), [two] + [None] * (RING - 1)
    for k in NEAR:
        ones[k] = gather(one, k)
    vt, end = first_chain(ones)
    v = hop(end, 0, 1)
    ahead0, behind0 = prepare([tie(end, one)[1]] + ones[1:], "prepare")
    for k in NEAR:
        twos[k] = gather(two, k)
    for stage in range(1, last):
        vt, end = chain(stage, ones, ahead0, v, vt)
        v = hop(end, stage, stage + 1)
    ahead1, behind1 = prepare(twos, "prepare2")
    vs, mus, end = turn(last, ones, twos, [ahead0, behind0, ahead1, behind1], v)
    mu = hop(end, last, last - 1)
    vs, parts = middle(last, twos, vt, ahead1, behind1, vs)
    own_v = [vs[0]] + [None] * (RING - 1)
    for stage in range(last - 1, -1, -1):
        if stage == last - 1:
            chunk, gate = FAR[:4], parts[0]
        elif stage == last - 2:
            chunk, gate = FAR[4:], end
        else:
            chunk = ()
        for k in chunk:
            own_v[k] = scatter(tie(gate, vs[k])[1], k)
        if stage == last - 1:
            mu, *parts = tie(mu, *parts)
        if stage == 0:
            states, keep, lhs = early(one, two, c, own_v)
            mu, keep = tie(mu, keep)
        mus, end = back_chain(stage, parts, behind0, mu, mus)
        if stage == last - 1:
            got = tie(end, *[own_v[k] for k in chunk])
            end = got[0]
            for k, value in zip(chunk, got[1:]):
                own_v[k] = value
        if stage > 0:
            mu = hop(end, stage, stage - 1)
    own_mu = [mus[0]] + [None] * (RING - 1)
    for k in FAR:
        own_mu[k] = scatter(mus[k], k)
    adjoints, mine, other = late(keep, lhs, own_mu)
    mine = mine + lax.ppermute(other, "dp", [(i, i ^ 1) for i in range(images)])
    for flip in (2, 6):
        mine = mine + lax.ppermute(mine, "dp", [(i, i ^ flip) for i in range(images)])
    other = lax.ppermute(mine, "dp", [(i, i ^ 1) for i in range(images)])
    grad, bias = finish(mine, other)
    return states[:, None], adjoints[:, None], grad, bias


def solution(mesh):
    return jax.shard_map(
        body,
        mesh=mesh,
        in_specs=(
            P("layer", "dp", None, None),
            P("layer", "dp", None, None),
            P("layer", None, None),
            P("layer", None),
        ),
        out_specs=(
            P("layer", "dp", None, None),
            P("layer", "dp", None, None),
            P("layer", None, None),
            P("layer", None),
        ),
        check_vma=False,
    )
```

```python
import jax
import jax.numpy as jnp
from jax import lax
from jax.experimental import pallas as pl
from jax.experimental.pallas import tpu as pltpu
from jax.sharding import PartitionSpec as P

F32 = jnp.float32
BF16 = jnp.bfloat16
H = 0.125
CH, CELLS = 64, 512
WPAD = 640
BLK = WPAD + CELLS
RING = 8
AXES = ("layer", "dp")
ANY = pl.BlockSpec(memory_space=pl.ANY)
HBM = pl.BlockSpec(memory_space=pltpu.HBM)
VMEM = pl.BlockSpec(memory_space=pltpu.VMEM)
PARAMS = pltpu.CompilerParams(vmem_limit_bytes=40 << 20)


def split(x):
    hi = x.astype(BF16)
    return hi, (x - hi.astype(F32)).astype(BF16)


def lane_index():
    return lax.broadcasted_iota(jnp.int32, (CH, 128), 1)


def columns(x):
    return [x[:, 128 * a : 128 * (a + 1)] for a in range(4)]


def swap(x):
    parts, lane, out = columns(x), lane_index(), []
    for a in range(4):
        acc = None
        for b in range(4):
            shift = ((b - a) * 32) % 128
            part = parts[b] if shift == 0 else pltpu.roll(parts[b], shift, 1)
            acc = part if acc is None else jnp.where(lane >= 32 * b, part, acc)
        out.append(acc)
    return jnp.concatenate(out, 1)


def lhs_forward(w):
    hi = w.astype(BF16).astype(F32)
    lo = w - hi
    rows = []
    for t in range(9):
        a, b = hi[:, 64 * t : 64 * t + 64], lo[:, 64 * t : 64 * t + 64]
        rows.append(jnp.concatenate([a, a, b], 1).astype(BF16))
    return jnp.concatenate(rows, 0)


def lhs_backward(w):
    wt = w.T
    hi = wt.astype(BF16).astype(F32)
    lo = wt - hi
    return jnp.concatenate([hi, hi, lo], 1).astype(BF16)


def conv(lhs, x, sign):
    hi, lo = split(x)
    z = jnp.dot(lhs, jnp.concatenate([hi, lo, hi], 0), preferred_element_type=F32)
    lane = lane_index()
    q = lane % 32
    lower, upper, right, left = lane < 96, lane >= 32, q < 31, q > 0

    def tap(a, e, col):
        t = 3 * (sign * a + 1) + (sign * e + 1)
        return z[64 * t : 64 * t + 64, 128 * col : 128 * col + 128]

    out = []
    for col in range(4):
        s = []
        for e in (-1, 0, 1):
            if col < 3:
                up = tap(1, e, col + 1)
            else:
                up = jnp.where(lower, pltpu.roll(tap(1, e, 0), 96, 1), 0.0)
            if col > 0:
                down = tap(-1, e, col - 1)
            else:
                down = jnp.where(upper, pltpu.roll(tap(-1, e, 3), 32, 1), 0.0)
            s.append(tap(0, e, col) + up + down)
        out.append(
            s[1]
            + jnp.where(right, pltpu.roll(s[2], 127, 1), 0.0)
            + jnp.where(left, pltpu.roll(s[0], 1, 1), 0.0)
        )
    return jnp.concatenate(out, 1)


def patches(x):
    lane = lane_index()
    q = lane % 32
    lower, upper, right, left = lane < 96, lane >= 32, q < 31, q > 0
    mid = columns(x)
    base = {
        0: mid,
        1: [jnp.where(right, pltpu.roll(c, 127, 1), 0.0) for c in mid],
        -1: [jnp.where(left, pltpu.roll(c, 1, 1), 0.0) for c in mid],
    }
    hi, lo = [], []
    for a in (-1, 0, 1):
        for e in (-1, 0, 1):
            c = base[e]
            if a == 1:
                c = c[1:] + [jnp.where(lower, pltpu.roll(c[0], 96, 1), 0.0)]
            elif a == -1:
                c = [jnp.where(upper, pltpu.roll(c[3], 32, 1), 0.0)] + c[:3]
            h, l = split(jnp.concatenate(c, 1))
            hi.append(h)
            lo.append(l)
    return jnp.concatenate(hi, 0), jnp.concatenate(lo, 0)


def dot_t(a, b):
    return lax.dot_general(a, b, (((1,), (1,)), ((), ())), preferred_element_type=F32)


def correlate(term, x):
    t_hi, t_lo = split(term)
    p_hi, p_lo = patches(x)
    return dot_t(t_hi, p_hi) + dot_t(t_hi, p_lo) + dot_t(t_lo, p_hi)


def as_column(row):
    r = lax.broadcasted_iota(jnp.int32, (CH, CH), 0)
    c = lax.broadcasted_iota(jnp.int32, (CH, CH), 1)
    spread = jnp.broadcast_to(row, (CH, CH))
    return jnp.sum(jnp.where(r == c, spread, 0.0), axis=1, keepdims=True)


def place():
    layer, image = lax.axis_index("layer"), lax.axis_index("dp")
    core = image % 2
    return layer // RING, layer % RING, 2 + 3 * core, core


def start_all(copies):
    for copy in copies:
        copy.start()
    return copies


def wait_all(copies):
    for copy in copies:
        copy.wait()


def field(*lead):
    return jax.ShapeDtypeStruct((*lead, CH, CELLS), F32)


def lhs_shape(*lead):
    return jax.ShapeDtypeStruct((*lead, 9 * CH, 3 * CH), BF16)


def vmem(shape):
    return pltpu.VMEM(shape.shape, shape.dtype)


def relax_kernel(c_hbm, a_hbm, w_hbm, b_hbm, one_ref, two_ref, c_ref, a_ref, w_ref, b_ref, sems):
    copies = start_all(
        [
            pltpu.make_async_copy(source, target, sems.at[i])
            for i, (source, target) in enumerate(
                [(b_hbm, b_ref), (w_hbm, w_ref), (c_hbm, c_ref), (a_hbm, a_ref)]
            )
        ]
    )
    wait_all(copies[:3])
    c = swap(c_ref[...])
    w0, w1 = w_ref[0], w_ref[1]
    b0, b1 = as_column(b_ref[0:1]), as_column(b_ref[1:2])
    t0 = jnp.tanh(conv(lhs_forward(w0), c, 1) + b0)
    t1 = jnp.tanh(conv(lhs_forward(w1), c + H * t0, 1) + b1)
    pad = WPAD - 576
    one_ref[:, 0:576] = w0
    one_ref[:, 576:WPAD] = jnp.broadcast_to(b0, (CH, pad))
    ring, spot, _, _ = place()
    keep = jnp.where((ring == 0) & (spot == 0), 1.0, 0.0)
    one_ref[:, WPAD:BLK] = jnp.where(keep > 0.0, c + H * t0 + H * t1, H * (t1 - t0))
    two_ref[:, 0:576] = w1
    two_ref[:, 576:WPAD] = jnp.broadcast_to(b1, (CH, pad))
    wait_all(copies[3:])
    two_ref[:, WPAD:BLK] = swap(a_ref[...])


def relax(c, a, w, b):
    shape = jax.ShapeDtypeStruct((CH, BLK), F32)
    return pl.pallas_call(
        relax_kernel,
        out_shape=(shape, shape),
        in_specs=[HBM] * 4,
        scratch_shapes=[
            pltpu.VMEM(c.shape, F32),
            pltpu.VMEM(a.shape, F32),
            pltpu.VMEM(w.shape, F32),
            pltpu.VMEM(b.shape, F32),
            pltpu.SemaphoreType.DMA((4,)),
        ],
        compiler_params=pltpu.CompilerParams(vmem_limit_bytes=63 << 20),
        name="relax",
    )(c, a, w, b)


MATRIX = pl.ds(0, WPAD)
REST = pl.ds(CELLS, WPAD)
BIAS = WPAD - 576


def slots(refs, target, sems, lead, part=None):
    if part is not None:
        refs = [ref.at[:, part] for ref in refs]
    copies = []
    for k, ref in enumerate(refs):
        j = (lead + k) % RING
        copies.append(pltpu.make_async_copy(ref, target.at[j], sems.at[j]))
    return copies


HALF = RING // 2


def half(array, i):
    return array.at[pl.ds(HALF * i, HALF)]


def half_out(vt, vt_ref, sems, part):
    return start_all(
        [
            pltpu.make_async_copy(half(vt.at[i], part), half(vt_ref.at[i], part), sems.at[i, part])
            for i in (0, 1)
        ]
    )


def first_kernel(*refs):
    one_refs = refs[:RING]
    vt_ref, out_ref, tau, even, vt, lhs, tau_sems, even_sems, sems = refs[RING:]
    ring, spot, lead, _ = place()

    @pl.when((ring == 0) & (spot == lead))
    def _():
        copies = slots(one_refs, even, even_sems, lead, MATRIX)
        copies += slots(one_refs, tau, tau_sems, lead, REST)
        wait_all(start_all(copies))

        def prepare(j, carry):
            lhs[j] = lhs_forward(even[j][:, 0:576])
            return carry

        lax.fori_loop(1, RING, prepare, 0)

        def step(j, v):
            now = jnp.tanh(conv(lhs[j], v, 1) + tau[j][:, BIAS : BIAS + 1])
            vt[0, j] = v
            vt[1, j] = now
            return v + 2 * H * now + tau[j][:, WPAD - CELLS :]

        v = lax.fori_loop(1, HALF, step, tau[0][:, WPAD - CELLS :])
        copies = half_out(vt, vt_ref, sems, 0)
        out_ref[...] = lax.fori_loop(HALF, RING, step, v)
        wait_all(copies + half_out(vt, vt_ref, sems, 1))


def first_chain(ones):
    return pl.pallas_call(
        first_kernel,
        out_shape=(field(2, RING), field()),
        in_specs=[ANY] * RING,
        out_specs=(ANY, VMEM),
        scratch_shapes=[
            pltpu.VMEM((RING, CH, WPAD), F32),
            pltpu.VMEM((RING, CH, WPAD), F32),
            vmem(field(2, RING)),
            vmem(lhs_shape(RING)),
            pltpu.SemaphoreType.DMA((RING,)),
            pltpu.SemaphoreType.DMA((RING,)),
            pltpu.SemaphoreType.DMA((2, 2)),
        ],
        compiler_params=PARAMS,
        name="chain_0",
    )(*ones)


def prepare_kernel(*refs):
    block_refs, outs = refs[:RING], refs[RING : RING + 2]
    w, ahead, behind, sems, out_sems = refs[RING + 2 :]
    _, spot, lead, _ = place()

    @pl.when(spot == lead)
    def _():
        wait_all(start_all(slots(block_refs, w, sems, lead, MATRIX)))

        def step(j, carry):
            ahead[j] = lhs_forward(w[j][:, 0:576])
            behind[j] = lhs_backward(w[j][:, 0:576])
            return carry

        lax.fori_loop(0, RING, step, 0)
        wait_all(
            start_all(
                [
                    pltpu.make_async_copy(ahead, outs[0], out_sems.at[0]),
                    pltpu.make_async_copy(behind, outs[1], out_sems.at[1]),
                ]
            )
        )


def prepare(blocks, name):
    return pl.pallas_call(
        prepare_kernel,
        out_shape=(lhs_shape(RING), lhs_shape(RING)),
        in_specs=[ANY] * RING,
        out_specs=(ANY, ANY),
        scratch_shapes=[
            pltpu.VMEM((RING, CH, WPAD), F32),
            vmem(lhs_shape(RING)),
            vmem(lhs_shape(RING)),
            pltpu.SemaphoreType.DMA((RING,)),
            pltpu.SemaphoreType.DMA((2,)),
        ],
        compiler_params=PARAMS,
        cost_estimate=pl.CostEstimate(flops=0, bytes_accessed=20 << 20, transcendentals=0),
        name=name,
    )(*blocks)


def chain_kernel(stage, *refs):
    tau_refs, ahead_ref, v_ref = refs[:RING], refs[RING], refs[RING + 1]
    vt_ref, out_ref, tau, vt, ahead, tau_sems, ahead_sems, sems = refs[-8:]
    ring, spot, lead, _ = place()

    @pl.when((ring == stage) & (spot == lead))
    def _():
        copies = start_all(slots(tau_refs, tau, tau_sems, lead, REST))
        halves = start_all(
            [
                pltpu.make_async_copy(half(ahead_ref, i), half(ahead, i), ahead_sems.at[i])
                for i in (0, 1)
            ]
        )
        wait_all(copies + halves[:1])

        def step(j, v):
            now = jnp.tanh(conv(ahead[j], v, 1) + tau[j][:, BIAS : BIAS + 1])
            vt[0, j] = v
            vt[1, j] = now
            return v + 2 * H * now + tau[j][:, WPAD - CELLS :]

        v = lax.fori_loop(0, HALF, step, v_ref[...], unroll=2)
        wait_all(halves[1:])
        copies = half_out(vt, vt_ref, sems, 0)
        out_ref[...] = lax.fori_loop(HALF, RING, step, v, unroll=2)
        wait_all(copies + half_out(vt, vt_ref, sems, 1))


def chain(stage, taus, ahead, v, vt):
    args = [*taus, ahead, v]
    return pl.pallas_call(
        lambda *refs: chain_kernel(stage, *refs),
        out_shape=(field(2, RING), field()),
        in_specs=[ANY] * (RING + 1) + [VMEM, ANY],
        out_specs=(ANY, VMEM),
        scratch_shapes=[
            pltpu.VMEM((RING, CH, WPAD), F32),
            vmem(field(2, RING)),
            vmem(lhs_shape(RING)),
            pltpu.SemaphoreType.DMA((RING,)),
            pltpu.SemaphoreType.DMA((2,)),
            pltpu.SemaphoreType.DMA((2, 2)),
        ],
        input_output_aliases={len(args): 0},
        compiler_params=PARAMS,
        name=f"chain_{stage}",
    )(*args, vt)


def correction(ahead, behind, v, t0, b1, a):
    t1 = jnp.tanh(conv(ahead, v + H * t0, 1) + b1)
    shift = H * conv(behind, (1.0 - t1 * t1) * a, -1)
    s0 = 1.0 - t0 * t0
    return shift, s0 * (H * (shift - a)), (2 * H) * s0


def back_step(behind, mu, shift, part, slope):
    return mu + shift + conv(behind, slope * mu + part, -1)


def middle_kernel(last, *refs):
    two_refs, (vt_ref, ahead_ref, behind_ref) = refs[:RING], refs[RING : RING + 3]
    outs = refs[-(RING + 3 + 7) : -7]
    two, vt, ahead, behind, out, two_sems, sems = refs[-7:]
    ring, spot, lead, _ = place()

    @pl.when((spot == lead) & (ring < last))
    def _():
        copies = start_all(slots(two_refs, two, two_sems, lead))
        copies += start_all(
            [
                pltpu.make_async_copy(vt_ref, vt, sems.at[0]),
                pltpu.make_async_copy(ahead_ref, ahead, sems.at[1]),
                pltpu.make_async_copy(behind_ref, behind, sems.at[2]),
            ]
        )
        wait_all(copies)
        copies = start_all(
            [
                pltpu.make_async_copy(vt.at[0, (lead + k) % RING], outs[k], two_sems.at[k])
                for k in range(RING)
            ]
        )

        def step(j, carry):
            b1, a = two[j][:, 576:577], two[j][:, WPAD:BLK]
            got = correction(ahead[j], behind[j], vt[0, j], vt[1, j], b1, a)
            for i in range(3):
                out[i, j] = got[i]
            return carry

        lax.fori_loop(0, RING, step, 0, unroll=2)
        copies += start_all(
            [pltpu.make_async_copy(out.at[i], outs[RING + i], sems.at[i]) for i in range(3)]
        )
        wait_all(copies)


def middle(last, twos, vt, ahead, behind, vs):
    args = [*twos, vt, ahead, behind]
    out = pl.pallas_call(
        lambda *refs: middle_kernel(last, *refs),
        out_shape=(field(),) * RING + (field(RING),) * 3,
        in_specs=[ANY] * (2 * RING + 3),
        out_specs=(ANY,) * (RING + 3),
        scratch_shapes=[
            pltpu.VMEM((RING, CH, BLK), F32),
            vmem(field(2, RING)),
            vmem(lhs_shape(RING)),
            vmem(lhs_shape(RING)),
            vmem(field(3, RING)),
            pltpu.SemaphoreType.DMA((RING,)),
            pltpu.SemaphoreType.DMA((3,)),
        ],
        input_output_aliases={len(args) + k: k for k in range(RING)},
        compiler_params=PARAMS,
        name="middle",
    )(*args, *vs)
    return out[:RING], out[RING:]


def turn_kernel(stage, *refs):
    tau_refs, two_refs = refs[:RING], refs[RING : 2 * RING]
    lhs_refs, v_ref = refs[2 * RING : 2 * RING + 4], refs[2 * RING + 4]
    v_refs = refs[2 * RING + 5 : 3 * RING + 5]
    mu_refs = refs[3 * RING + 5 : 4 * RING + 5]
    out_ref, tau, two, vs, mus, lhs, out, sems, lhs_sems = refs[4 * RING + 5 :]
    ring, spot, lead, _ = place()

    @pl.when((ring == stage) & (spot == lead))
    def _():
        copies = start_all(slots(tau_refs, tau, sems.at[0], lead, REST))
        matrices = [
            pltpu.make_async_copy(lhs_refs[i], lhs.at[i], lhs_sems.at[i]) for i in range(4)
        ]
        start_all(matrices[:1])
        block_copies = start_all(slots(two_refs, two, sems.at[1], lead))
        start_all(matrices[2:] + matrices[1:2])
        wait_all(copies + matrices[:1])

        def ahead_step(j, v):
            now = jnp.tanh(conv(lhs[0, j], v, 1) + tau[j][:, BIAS : BIAS + 1])
            vs[j] = v
            return v + 2 * H * now + tau[j][:, WPAD - CELLS :], now

        def correct(j, v, t0):
            b1, a = two[j][:, 576:577], two[j][:, WPAD:BLK]
            got = correction(lhs[2, j], lhs[3, j], v, t0, b1, a)
            for i in range(3):
                out[i, j] = got[i]

        def step(j, carry):
            v, old_v, old_t = carry
            new_v, now = ahead_step(j, v)
            correct(j - 1, old_v, old_t)
            return new_v, v, now

        start = v_ref[...]
        v, now = ahead_step(0, start)
        wait_all(block_copies + matrices[2:])
        _, v, now = lax.fori_loop(1, RING, step, (v, start, now))
        copies = start_all(
            [
                pltpu.make_async_copy(vs.at[(lead + k) % RING], v_refs[k], sems.at[0, k])
                for k in range(RING)
            ]
        )
        correct(RING - 1, v, now)
        wait_all(matrices[1:2])

        def back(k, mu):
            j = RING - 1 - k
            mus[j] = mu
            return back_step(lhs[1, j], mu, out[0, j], out[1, j], out[2, j])

        out_ref[...] = lax.fori_loop(0, RING, back, two[RING - 1][:, WPAD:BLK], unroll=2)
        copies += start_all(
            [
                pltpu.make_async_copy(mus.at[(lead + k) % RING], mu_refs[k], sems.at[1, k])
                for k in range(RING)
            ]
        )
        wait_all(copies)


def turn(stage, taus, twos, lhs, v):
    out = pl.pallas_call(
        lambda *refs: turn_kernel(stage, *refs),
        out_shape=(field(),) * (2 * RING + 1),
        in_specs=[ANY] * (2 * RING + 4) + [VMEM],
        out_specs=(ANY,) * (2 * RING) + (VMEM,),
        scratch_shapes=[
            pltpu.VMEM((RING, CH, WPAD), F32),
            pltpu.VMEM((RING, CH, BLK), F32),
            vmem(field(RING)),
            vmem(field(RING)),
            vmem(lhs_shape(4, RING)),
            vmem(field(3, RING)),
            pltpu.SemaphoreType.DMA((2, RING)),
            pltpu.SemaphoreType.DMA((4,)),
        ],
        compiler_params=PARAMS,
        name="turn",
    )(*taus, *twos, *lhs, v)
    return out[:RING], out[RING : 2 * RING], out[2 * RING]


def back_kernel(stage, *refs):
    part_refs, behind_ref, mu_ref = refs[:3], refs[3], refs[4]
    outs = refs[-(RING + 1 + 5) : -5]
    parts, behind, mus, sems, out_sems = refs[-5:]
    ring, spot, lead, _ = place()

    @pl.when((ring == stage) & (spot == lead))
    def _():
        copies = [pltpu.make_async_copy(part_refs[i], parts.at[i], sems.at[i]) for i in range(3)]
        copies.append(pltpu.make_async_copy(behind_ref, behind, sems.at[3]))
        wait_all(start_all(copies))

        def step(k, mu):
            j = RING - 1 - k
            mus[j] = mu
            return back_step(behind[j], mu, parts[0, j], parts[1, j], parts[2, j])

        if stage == 0:
            end = lax.fori_loop(0, RING - 1, step, mu_ref[...])
            mus[0] = end
        else:
            end = lax.fori_loop(0, RING, step, mu_ref[...], unroll=2)
        outs[RING][...] = end
        wait_all(
            start_all(
                [
                    pltpu.make_async_copy(mus.at[(lead + k) % RING], outs[k], out_sems.at[k])
                    for k in range(RING)
                ]
            )
        )


def back_chain(stage, parts, behind, mu, mus):
    args = [*parts, behind, mu]
    aliases = {len(args) + k: k for k in range(RING)}
    out = pl.pallas_call(
        lambda *refs: back_kernel(stage, *refs),
        out_shape=(field(),) * (RING + 1),
        in_specs=[ANY] * 4 + [VMEM] + [ANY] * RING,
        out_specs=(ANY,) * RING + (VMEM,),
        scratch_shapes=[
            vmem(field(3, RING)),
            vmem(lhs_shape(RING)),
            vmem(field(RING)),
            pltpu.SemaphoreType.DMA((4,)),
            pltpu.SemaphoreType.DMA((RING,)),
        ],
        input_output_aliases=aliases,
        compiler_params=PARAMS,
        name=f"back_{stage}",
    )(*args, *mus)
    return out[:RING], out[RING]


def fetch(refs, target, sem):
    _, spot, lead, _ = place()
    step = (spot + RING - lead) % RING
    for k in range(RING):

        @pl.when(step == k)
        def _():
            copy = pltpu.make_async_copy(refs[k], target, sem)
            copy.start()
            copy.wait()


def early_kernel(*refs):
    one_ref, two_ref, c_ref, refs = refs[0], refs[1], refs[2], refs[3:]
    v_refs = refs[:RING]
    states_ref, keep_ref, lhs_ref, v_ref, sem = refs[RING:]
    fetch(v_refs, v_ref, sem)
    ring, spot, _, _ = place()

    @pl.when((ring == 0) & (spot == 0))
    def _():
        v_ref[...] = swap(c_ref[...])

    v = v_ref[...]
    w0, w1 = one_ref[:, 0:576], two_ref[:, 0:576]
    t0 = jnp.tanh(conv(lhs_forward(w0), v, 1) + one_ref[:, 576:577])
    m = v + H * t0
    b1, a = two_ref[:, 576:577], two_ref[:, WPAD:BLK]
    t1 = jnp.tanh(conv(lhs_forward(w1), m, 1) + b1)
    s1 = 1.0 - t1 * t1
    s0 = 1.0 - t0 * t0
    lhs_ref[0] = lhs_backward(w0)
    behind = lhs_backward(w1)
    lhs_ref[1] = behind
    shift = H * conv(behind, s1 * a, -1)
    states_ref[0] = swap(m)
    slot = one_ref[:, WPAD:BLK]
    keep = jnp.where((ring == 0) & (spot == 0), 1.0, 0.0)
    states_ref[1] = swap(jnp.where(keep > 0.0, slot, v + 2 * H * t0 + slot))
    keep_ref[0] = v
    keep_ref[1] = m
    keep_ref[2] = s0
    keep_ref[3] = s1
    keep_ref[4] = shift
    keep_ref[5] = s0 * (H * (shift - a))


def early(one, two, c, vs):
    return pl.pallas_call(
        early_kernel,
        out_shape=(field(2), field(6), lhs_shape(2)),
        in_specs=[VMEM] * 3 + [ANY] * RING,
        scratch_shapes=[vmem(field()), pltpu.SemaphoreType.DMA],
        compiler_params=PARAMS,
        name="early",
    )(one, two, c, *vs)


def late_kernel(*refs):
    keep_ref, lhs_ref = refs[:2]
    mu_refs = refs[2 : 2 + RING]
    adjoints_ref, mine_ref, other_ref, mu_scratch, sem = refs[2 + RING :]
    fetch(mu_refs, mu_scratch, sem)
    mu = mu_scratch[...]
    s0 = keep_ref[2]
    odd_product = keep_ref[3] * mu
    odd = mu + H * conv(lhs_ref[1], odd_product, -1)
    even_term = (H / 8) * (s0 * odd)
    odd_term = (H / 8) * odd_product
    odd_grad = correlate(odd_term, keep_ref[1])
    even_grad = correlate(even_term, keep_ref[0])
    even = back_step(lhs_ref[0], mu, keep_ref[4], keep_ref[5], (2 * H) * s0)
    adjoints_ref[0] = swap(even)
    adjoints_ref[1] = swap(odd)
    pad = (CH, WPAD - 576)
    even_bias = jnp.broadcast_to(jnp.sum(even_term, axis=1, keepdims=True), pad)
    odd_bias = jnp.broadcast_to(jnp.sum(odd_term, axis=1, keepdims=True), pad)

    def write(ref, grad, bias):
        ref[:, 0:576] = grad
        ref[:, 576:WPAD] = bias

    core = place()[3]

    @pl.when(core == 0)
    def _():
        write(mine_ref, even_grad, even_bias)
        write(other_ref, odd_grad, odd_bias)

    @pl.when(core == 1)
    def _():
        write(mine_ref, odd_grad, odd_bias)
        write(other_ref, even_grad, even_bias)


def late(keep, lhs, mus):
    grad = jax.ShapeDtypeStruct((CH, WPAD), F32)
    return pl.pallas_call(
        late_kernel,
        out_shape=(field(2), grad, grad),
        in_specs=[VMEM] * 2 + [ANY] * RING,
        scratch_shapes=[vmem(field()), pltpu.SemaphoreType.DMA],
        compiler_params=PARAMS,
        name="late",
    )(keep, lhs, *mus)


def finish_kernel(mine_ref, other_ref, grad_ref, bias_ref):
    core = place()[3]
    r = lax.broadcasted_iota(jnp.int32, (CH, CH), 0)
    c = lax.broadcasted_iota(jnp.int32, (CH, CH), 1)

    def write(slot, ref):
        grad_ref[slot] = ref[:, 0:576]
        spread = jnp.broadcast_to(ref[:, 576:577], (CH, CH))
        bias_ref[slot : slot + 1] = jnp.sum(jnp.where(r == c, spread, 0.0), axis=0, keepdims=True)

    @pl.when(core == 0)
    def _():
        write(0, mine_ref)
        write(1, other_ref)

    @pl.when(core == 1)
    def _():
        write(1, mine_ref)
        write(0, other_ref)


def finish(mine, other):
    return pl.pallas_call(
        finish_kernel,
        out_shape=(
            jax.ShapeDtypeStruct((2, CH, 576), F32),
            jax.ShapeDtypeStruct((2, CH), F32),
        ),
        compiler_params=PARAMS,
        name="finish",
    )(mine, other)


def tie(*values):
    return lax.optimization_barrier(values)


NEAR = (1, 7, 2, 6, 3, 5, 4)
FAR = NEAR[::-1]
EARLY = FAR[:3]


def body(coarse_guess, adjoint_guess, weights, biases):
    images = lax.axis_size("dp")
    groups = lax.axis_size("layer") // RING
    last = groups - 1

    def device(x, z, d):
        return (RING * x + z % RING) * images + d

    def lead(d):
        return 2 + 3 * (d % 2)

    everyone = [(x, d) for x in range(groups) for d in range(images)]

    def gather(value, k):
        pairs = [(device(x, lead(d) + k, d), device(x, lead(d), d)) for x, d in everyone]
        return lax.ppermute(value, AXES, pairs)

    def scatter(value, k):
        pairs = [(device(x, lead(d), d), device(x, lead(d) + k, d)) for x, d in everyone]
        return lax.ppermute(value, AXES, pairs)

    def hop(value, source, target):
        pairs = [
            (device(source, lead(d), d), device(target, lead(d), d)) for d in range(images)
        ]
        return lax.ppermute(value, AXES, pairs)

    c, a = coarse_guess[0, 0], adjoint_guess[0, 0]
    one, two = relax(c, a, weights, biases)
    ones, twos = [one] + [None] * (RING - 1), [two] + [None] * (RING - 1)
    for k in NEAR:
        ones[k] = gather(one, k)
    vt, end = first_chain(ones)
    v = hop(end, 0, 1)
    ahead0, behind0 = prepare([tie(end, one)[1]] + ones[1:], "prepare")
    for k in NEAR:
        twos[k] = gather(two, k)
    for stage in range(1, last):
        if stage == 1:
            got = tie(v, *[twos[k] for k in EARLY])
            v = got[0]
            for k, value in zip(EARLY, got[1:]):
                twos[k] = value
        vt, end = chain(stage, ones, ahead0, v, vt)
        v = hop(end, stage, stage + 1)
    ahead1, behind1 = prepare(twos, "prepare2")
    vs, mus, end = turn(last, ones, twos, [ahead0, behind0, ahead1, behind1], v)
    mu = hop(end, last, last - 1)
    vs, parts = middle(last, twos, vt, ahead1, behind1, vs)
    own_v = [vs[0]] + [None] * (RING - 1)
    for stage in range(last - 1, -1, -1):
        if stage == last - 1:
            chunk, gate = FAR[:4], parts[0]
        elif stage == last - 2:
            chunk, gate = FAR[4:], end
        else:
            chunk = ()
        for k in chunk:
            own_v[k] = scatter(tie(gate, vs[k])[1], k)
        if stage == last - 1:
            mu, *parts = tie(mu, *parts)
        if stage == 0:
            states, keep, lhs = early(one, two, c, own_v)
            mu, keep = tie(mu, keep)
        mus, end = back_chain(stage, parts, behind0, mu, mus)
        if stage == last - 1:
            got = tie(end, *[own_v[k] for k in chunk])
            end = got[0]
            for k, value in zip(chunk, got[1:]):
                own_v[k] = value
        if stage > 0:
            mu = hop(end, stage, stage - 1)
    own_mu = [mus[0]] + [None] * (RING - 1)
    for k in FAR:
        own_mu[k] = scatter(mus[k], k)
    adjoints, mine, other = late(keep, lhs, own_mu)
    mine = mine + lax.ppermute(other, "dp", [(i, i ^ 1) for i in range(images)])
    for flip in (2, 6):
        mine = mine + lax.ppermute(mine, "dp", [(i, i ^ flip) for i in range(images)])
    other = lax.ppermute(mine, "dp", [(i, i ^ 1) for i in range(images)])
    grad, bias = finish(mine, other)
    return states[:, None], adjoints[:, None], grad, bias


def solution(mesh):
    return jax.shard_map(
        body,
        mesh=mesh,
        in_specs=(
            P("layer", "dp", None, None),
            P("layer", "dp", None, None),
            P("layer", None, None),
            P("layer", None),
        ),
        out_specs=(
            P("layer", "dp", None, None),
            P("layer", "dp", None, None),
            P("layer", None, None),
            P("layer", None),
        ),
        check_vma=False,
    )
```

```python
import jax
import jax.numpy as jnp
from jax import lax
from jax.experimental import pallas as pl
from jax.experimental.pallas import tpu as pltpu
from jax.sharding import PartitionSpec as P

F32 = jnp.float32
BF16 = jnp.bfloat16
H = 0.125
CH, CELLS = 64, 512
WPAD = 640
BLK = WPAD + CELLS
RING = 8
AXES = ("layer", "dp")
ANY = pl.BlockSpec(memory_space=pl.ANY)
HBM = pl.BlockSpec(memory_space=pltpu.HBM)
VMEM = pl.BlockSpec(memory_space=pltpu.VMEM)
PARAMS = pltpu.CompilerParams(vmem_limit_bytes=40 << 20)


def split(x):
    hi = x.astype(BF16)
    return hi, (x - hi.astype(F32)).astype(BF16)


def lane_index():
    return lax.broadcasted_iota(jnp.int32, (CH, 128), 1)


def columns(x):
    return [x[:, 128 * a : 128 * (a + 1)] for a in range(4)]


def swap(x):
    parts, lane, out = columns(x), lane_index(), []
    for a in range(4):
        acc = None
        for b in range(4):
            shift = ((b - a) * 32) % 128
            part = parts[b] if shift == 0 else pltpu.roll(parts[b], shift, 1)
            acc = part if acc is None else jnp.where(lane >= 32 * b, part, acc)
        out.append(acc)
    return jnp.concatenate(out, 1)


def lhs_forward(w):
    hi = w.astype(BF16).astype(F32)
    lo = w - hi
    rows = []
    for t in range(9):
        a, b = hi[:, 64 * t : 64 * t + 64], lo[:, 64 * t : 64 * t + 64]
        rows.append(jnp.concatenate([a, a, b], 1).astype(BF16))
    return jnp.concatenate(rows, 0)


def lhs_backward(w):
    wt = w.T
    hi = wt.astype(BF16).astype(F32)
    lo = wt - hi
    return jnp.concatenate([hi, hi, lo], 1).astype(BF16)


def conv(lhs, x, sign):
    hi, lo = split(x)
    z = jnp.dot(lhs, jnp.concatenate([hi, lo, hi], 0), preferred_element_type=F32)
    lane = lane_index()
    q = lane % 32
    lower, upper, right, left = lane < 96, lane >= 32, q < 31, q > 0

    def tap(a, e, col):
        t = 3 * (sign * a + 1) + (sign * e + 1)
        return z[64 * t : 64 * t + 64, 128 * col : 128 * col + 128]

    out = []
    for col in range(4):
        s = []
        for e in (-1, 0, 1):
            if col < 3:
                up = tap(1, e, col + 1)
            else:
                up = jnp.where(lower, pltpu.roll(tap(1, e, 0), 96, 1), 0.0)
            if col > 0:
                down = tap(-1, e, col - 1)
            else:
                down = jnp.where(upper, pltpu.roll(tap(-1, e, 3), 32, 1), 0.0)
            s.append(tap(0, e, col) + up + down)
        out.append(
            s[1]
            + jnp.where(right, pltpu.roll(s[2], 127, 1), 0.0)
            + jnp.where(left, pltpu.roll(s[0], 1, 1), 0.0)
        )
    return jnp.concatenate(out, 1)


def patches(x):
    lane = lane_index()
    q = lane % 32
    lower, upper, right, left = lane < 96, lane >= 32, q < 31, q > 0
    mid = columns(x)
    base = {
        0: mid,
        1: [jnp.where(right, pltpu.roll(c, 127, 1), 0.0) for c in mid],
        -1: [jnp.where(left, pltpu.roll(c, 1, 1), 0.0) for c in mid],
    }
    hi, lo = [], []
    for a in (-1, 0, 1):
        for e in (-1, 0, 1):
            c = base[e]
            if a == 1:
                c = c[1:] + [jnp.where(lower, pltpu.roll(c[0], 96, 1), 0.0)]
            elif a == -1:
                c = [jnp.where(upper, pltpu.roll(c[3], 32, 1), 0.0)] + c[:3]
            h, l = split(jnp.concatenate(c, 1))
            hi.append(h)
            lo.append(l)
    return jnp.concatenate(hi, 0), jnp.concatenate(lo, 0)


def dot_t(a, b):
    return lax.dot_general(a, b, (((1,), (1,)), ((), ())), preferred_element_type=F32)


def correlate(term, x):
    t_hi, t_lo = split(term)
    p_hi, p_lo = patches(x)
    return dot_t(t_hi, p_hi) + dot_t(t_hi, p_lo) + dot_t(t_lo, p_hi)


def as_column(row):
    r = lax.broadcasted_iota(jnp.int32, (CH, CH), 0)
    c = lax.broadcasted_iota(jnp.int32, (CH, CH), 1)
    spread = jnp.broadcast_to(row, (CH, CH))
    return jnp.sum(jnp.where(r == c, spread, 0.0), axis=1, keepdims=True)


def place():
    layer, image = lax.axis_index("layer"), lax.axis_index("dp")
    core = image % 2
    return layer // RING, layer % RING, 2 + 3 * core, core


def start_all(copies):
    for copy in copies:
        copy.start()
    return copies


def wait_all(copies):
    for copy in copies:
        copy.wait()


def field(*lead):
    return jax.ShapeDtypeStruct((*lead, CH, CELLS), F32)


def lhs_shape(*lead):
    return jax.ShapeDtypeStruct((*lead, 9 * CH, 3 * CH), BF16)


def vmem(shape):
    return pltpu.VMEM(shape.shape, shape.dtype)


def relax_kernel(c_hbm, a_hbm, w_hbm, b_hbm, one_ref, two_ref, c_ref, a_ref, w_ref, b_ref, sems):
    copies = start_all(
        [
            pltpu.make_async_copy(source, target, sems.at[i])
            for i, (source, target) in enumerate(
                [(b_hbm, b_ref), (w_hbm, w_ref), (c_hbm, c_ref), (a_hbm, a_ref)]
            )
        ]
    )
    wait_all(copies[:3])
    c = swap(c_ref[...])
    w0, w1 = w_ref[0], w_ref[1]
    b0, b1 = as_column(b_ref[0:1]), as_column(b_ref[1:2])
    t0 = jnp.tanh(conv(lhs_forward(w0), c, 1) + b0)
    t1 = jnp.tanh(conv(lhs_forward(w1), c + H * t0, 1) + b1)
    pad = WPAD - 576
    one_ref[:, 0:576] = w0
    one_ref[:, 576:WPAD] = jnp.broadcast_to(b0, (CH, pad))
    ring, spot, _, _ = place()
    keep = jnp.where((ring == 0) & (spot == 0), 1.0, 0.0)
    one_ref[:, WPAD:BLK] = jnp.where(keep > 0.0, c + H * t0 + H * t1, H * (t1 - t0))
    two_ref[:, 0:576] = w1
    two_ref[:, 576:WPAD] = jnp.broadcast_to(b1, (CH, pad))
    wait_all(copies[3:])
    two_ref[:, WPAD:BLK] = swap(a_ref[...])


def relax(c, a, w, b):
    shape = jax.ShapeDtypeStruct((CH, BLK), F32)
    return pl.pallas_call(
        relax_kernel,
        out_shape=(shape, shape),
        in_specs=[HBM] * 4,
        scratch_shapes=[
            pltpu.VMEM(c.shape, F32),
            pltpu.VMEM(a.shape, F32),
            pltpu.VMEM(w.shape, F32),
            pltpu.VMEM(b.shape, F32),
            pltpu.SemaphoreType.DMA((4,)),
        ],
        compiler_params=pltpu.CompilerParams(vmem_limit_bytes=63 << 20),
        name="relax",
    )(c, a, w, b)


MATRIX = pl.ds(0, WPAD)
REST = pl.ds(CELLS, WPAD)
BIAS = WPAD - 576


def slots(refs, target, sems, lead, part=None):
    if part is not None:
        refs = [ref.at[:, part] for ref in refs]
    copies = []
    for k, ref in enumerate(refs):
        j = (lead + k) % RING
        copies.append(pltpu.make_async_copy(ref, target.at[j], sems.at[j]))
    return copies


HALF = RING // 2


def half(array, i):
    return array.at[pl.ds(HALF * i, HALF)]


def half_out(vt, vt_ref, sems, part):
    return start_all(
        [
            pltpu.make_async_copy(half(vt.at[i], part), half(vt_ref.at[i], part), sems.at[i, part])
            for i in (0, 1)
        ]
    )


def first_kernel(*refs):
    one_refs = refs[:RING]
    vt_ref, out_ref, tau, even, vt, lhs, tau_sems, even_sems, sems = refs[RING:]
    ring, spot, lead, _ = place()

    @pl.when((ring == 0) & (spot == lead))
    def _():
        copies = slots(one_refs, even, even_sems, lead, MATRIX)
        copies += slots(one_refs, tau, tau_sems, lead, REST)
        wait_all(start_all(copies))

        def prepare(j, carry):
            lhs[j] = lhs_forward(even[j][:, 0:576])
            return carry

        lax.fori_loop(1, RING, prepare, 0)

        def step(j, v):
            now = jnp.tanh(conv(lhs[j], v, 1) + tau[j][:, BIAS : BIAS + 1])
            vt[0, j] = v
            vt[1, j] = now
            return v + 2 * H * now + tau[j][:, WPAD - CELLS :]

        v = lax.fori_loop(1, HALF, step, tau[0][:, WPAD - CELLS :])
        copies = half_out(vt, vt_ref, sems, 0)
        out_ref[...] = lax.fori_loop(HALF, RING, step, v)
        wait_all(copies + half_out(vt, vt_ref, sems, 1))


def first_chain(ones):
    return pl.pallas_call(
        first_kernel,
        out_shape=(field(2, RING), field()),
        in_specs=[ANY] * RING,
        out_specs=(ANY, VMEM),
        scratch_shapes=[
            pltpu.VMEM((RING, CH, WPAD), F32),
            pltpu.VMEM((RING, CH, WPAD), F32),
            vmem(field(2, RING)),
            vmem(lhs_shape(RING)),
            pltpu.SemaphoreType.DMA((RING,)),
            pltpu.SemaphoreType.DMA((RING,)),
            pltpu.SemaphoreType.DMA((2, 2)),
        ],
        compiler_params=PARAMS,
        name="chain_0",
    )(*ones)


def prepare_kernel(*refs):
    block_refs, outs = refs[:RING], refs[RING : RING + 2]
    w, ahead, behind, sems, out_sems = refs[RING + 2 :]
    _, spot, lead, _ = place()

    @pl.when(spot == lead)
    def _():
        wait_all(start_all(slots(block_refs, w, sems, lead, MATRIX)))

        def step(j, carry):
            ahead[j] = lhs_forward(w[j][:, 0:576])
            behind[j] = lhs_backward(w[j][:, 0:576])
            return carry

        lax.fori_loop(0, RING, step, 0)
        wait_all(
            start_all(
                [
                    pltpu.make_async_copy(ahead, outs[0], out_sems.at[0]),
                    pltpu.make_async_copy(behind, outs[1], out_sems.at[1]),
                ]
            )
        )


def prepare(blocks, name):
    return pl.pallas_call(
        prepare_kernel,
        out_shape=(lhs_shape(RING), lhs_shape(RING)),
        in_specs=[ANY] * RING,
        out_specs=(ANY, ANY),
        scratch_shapes=[
            pltpu.VMEM((RING, CH, WPAD), F32),
            vmem(lhs_shape(RING)),
            vmem(lhs_shape(RING)),
            pltpu.SemaphoreType.DMA((RING,)),
            pltpu.SemaphoreType.DMA((2,)),
        ],
        compiler_params=PARAMS,
        cost_estimate=pl.CostEstimate(flops=0, bytes_accessed=20 << 20, transcendentals=0),
        name=name,
    )(*blocks)


def chain_kernel(stage, *refs):
    tau_refs, ahead_ref, v_ref = refs[:RING], refs[RING], refs[RING + 1]
    vt_ref, out_ref, tau, vt, ahead, tau_sems, ahead_sems, sems = refs[-8:]
    ring, spot, lead, _ = place()

    @pl.when((ring == stage) & (spot == lead))
    def _():
        copies = start_all(slots(tau_refs, tau, tau_sems, lead, REST))
        halves = start_all(
            [
                pltpu.make_async_copy(half(ahead_ref, i), half(ahead, i), ahead_sems.at[i])
                for i in (0, 1)
            ]
        )
        wait_all(copies + halves[:1])

        def step(j, v):
            now = jnp.tanh(conv(ahead[j], v, 1) + tau[j][:, BIAS : BIAS + 1])
            vt[0, j] = v
            vt[1, j] = now
            return v + 2 * H * now + tau[j][:, WPAD - CELLS :]

        v = lax.fori_loop(0, HALF, step, v_ref[...], unroll=2)
        wait_all(halves[1:])
        copies = half_out(vt, vt_ref, sems, 0)
        out_ref[...] = lax.fori_loop(HALF, RING, step, v, unroll=2)
        wait_all(copies + half_out(vt, vt_ref, sems, 1))


def chain(stage, taus, ahead, v, vt):
    args = [*taus, ahead, v]
    return pl.pallas_call(
        lambda *refs: chain_kernel(stage, *refs),
        out_shape=(field(2, RING), field()),
        in_specs=[ANY] * (RING + 1) + [VMEM, ANY],
        out_specs=(ANY, VMEM),
        scratch_shapes=[
            pltpu.VMEM((RING, CH, WPAD), F32),
            vmem(field(2, RING)),
            vmem(lhs_shape(RING)),
            pltpu.SemaphoreType.DMA((RING,)),
            pltpu.SemaphoreType.DMA((2,)),
            pltpu.SemaphoreType.DMA((2, 2)),
        ],
        input_output_aliases={len(args): 0},
        compiler_params=PARAMS,
        name=f"chain_{stage}",
    )(*args, vt)


def correction(ahead, behind, v, t0, b1, a):
    t1 = jnp.tanh(conv(ahead, v + H * t0, 1) + b1)
    shift = H * conv(behind, (1.0 - t1 * t1) * a, -1)
    s0 = 1.0 - t0 * t0
    return shift, s0 * (H * (shift - a)), (2 * H) * s0


def back_step(behind, mu, shift, part, slope):
    return mu + shift + conv(behind, slope * mu + part, -1)


def middle_kernel(last, *refs):
    two_refs, (vt_ref, ahead_ref, behind_ref) = refs[:RING], refs[RING : RING + 3]
    outs = refs[-(RING + 3 + 7) : -7]
    two, vt, ahead, behind, out, two_sems, sems = refs[-7:]
    ring, spot, lead, _ = place()

    @pl.when((spot == lead) & (ring < last))
    def _():
        copies = start_all(slots(two_refs, two, two_sems, lead))
        copies += start_all(
            [
                pltpu.make_async_copy(vt_ref, vt, sems.at[0]),
                pltpu.make_async_copy(ahead_ref, ahead, sems.at[1]),
                pltpu.make_async_copy(behind_ref, behind, sems.at[2]),
            ]
        )
        wait_all(copies)
        copies = start_all(
            [
                pltpu.make_async_copy(vt.at[0, (lead + k) % RING], outs[k], two_sems.at[k])
                for k in range(RING)
            ]
        )

        def step(j, carry):
            b1, a = two[j][:, 576:577], two[j][:, WPAD:BLK]
            got = correction(ahead[j], behind[j], vt[0, j], vt[1, j], b1, a)
            for i in range(3):
                out[i, j] = got[i]
            return carry

        lax.fori_loop(0, RING, step, 0, unroll=2)
        copies += start_all(
            [pltpu.make_async_copy(out.at[i], outs[RING + i], sems.at[i]) for i in range(3)]
        )
        wait_all(copies)


def middle(last, twos, vt, ahead, behind, vs):
    args = [*twos, vt, ahead, behind]
    out = pl.pallas_call(
        lambda *refs: middle_kernel(last, *refs),
        out_shape=(field(),) * RING + (field(RING),) * 3,
        in_specs=[ANY] * (2 * RING + 3),
        out_specs=(ANY,) * (RING + 3),
        scratch_shapes=[
            pltpu.VMEM((RING, CH, BLK), F32),
            vmem(field(2, RING)),
            vmem(lhs_shape(RING)),
            vmem(lhs_shape(RING)),
            vmem(field(3, RING)),
            pltpu.SemaphoreType.DMA((RING,)),
            pltpu.SemaphoreType.DMA((3,)),
        ],
        input_output_aliases={len(args) + k: k for k in range(RING)},
        compiler_params=PARAMS,
        name="middle",
    )(*args, *vs)
    return out[:RING], out[RING:]


def turn_kernel(stage, *refs):
    tau_refs, two_refs = refs[:RING], refs[RING : 2 * RING]
    lhs_refs, v_ref = refs[2 * RING : 2 * RING + 4], refs[2 * RING + 4]
    v_refs = refs[2 * RING + 5 : 3 * RING + 5]
    mu_refs = refs[3 * RING + 5 : 4 * RING + 5]
    out_ref, tau, two, vs, mus, lhs, out, sems, lhs_sems = refs[4 * RING + 5 :]
    ring, spot, lead, _ = place()

    @pl.when((ring == stage) & (spot == lead))
    def _():
        copies = start_all(slots(tau_refs, tau, sems.at[0], lead, REST))
        matrices = [
            pltpu.make_async_copy(lhs_refs[i], lhs.at[i], lhs_sems.at[i]) for i in range(4)
        ]
        start_all(matrices[:1])
        block_copies = start_all(slots(two_refs, two, sems.at[1], lead))
        start_all(matrices[2:] + matrices[1:2])
        wait_all(copies + matrices[:1])

        def ahead_step(j, v):
            now = jnp.tanh(conv(lhs[0, j], v, 1) + tau[j][:, BIAS : BIAS + 1])
            vs[j] = v
            return v + 2 * H * now + tau[j][:, WPAD - CELLS :], now

        def correct(j, v, t0):
            b1, a = two[j][:, 576:577], two[j][:, WPAD:BLK]
            got = correction(lhs[2, j], lhs[3, j], v, t0, b1, a)
            for i in range(3):
                out[i, j] = got[i]

        def step(j, carry):
            v, old_v, old_t = carry
            new_v, now = ahead_step(j, v)
            correct(j - 1, old_v, old_t)
            return new_v, v, now

        start = v_ref[...]
        v, now = ahead_step(0, start)
        wait_all(block_copies + matrices[2:])
        _, v, now = lax.fori_loop(1, RING, step, (v, start, now))
        copies = start_all(
            [
                pltpu.make_async_copy(vs.at[(lead + k) % RING], v_refs[k], sems.at[0, k])
                for k in range(RING)
            ]
        )
        correct(RING - 1, v, now)
        wait_all(matrices[1:2])

        def back(k, mu):
            j = RING - 1 - k
            mus[j] = mu
            return back_step(lhs[1, j], mu, out[0, j], out[1, j], out[2, j])

        out_ref[...] = lax.fori_loop(0, RING, back, two[RING - 1][:, WPAD:BLK], unroll=2)
        copies += start_all(
            [
                pltpu.make_async_copy(mus.at[(lead + k) % RING], mu_refs[k], sems.at[1, k])
                for k in range(RING)
            ]
        )
        wait_all(copies)


def turn(stage, taus, twos, lhs, v):
    out = pl.pallas_call(
        lambda *refs: turn_kernel(stage, *refs),
        out_shape=(field(),) * (2 * RING + 1),
        in_specs=[ANY] * (2 * RING + 4) + [VMEM],
        out_specs=(ANY,) * (2 * RING) + (VMEM,),
        scratch_shapes=[
            pltpu.VMEM((RING, CH, WPAD), F32),
            pltpu.VMEM((RING, CH, BLK), F32),
            vmem(field(RING)),
            vmem(field(RING)),
            vmem(lhs_shape(4, RING)),
            vmem(field(3, RING)),
            pltpu.SemaphoreType.DMA((2, RING)),
            pltpu.SemaphoreType.DMA((4,)),
        ],
        compiler_params=PARAMS,
        name="turn",
    )(*taus, *twos, *lhs, v)
    return out[:RING], out[RING : 2 * RING], out[2 * RING]


def back_kernel(stage, *refs):
    part_refs, behind_ref, mu_ref = refs[:3], refs[3], refs[4]
    outs = refs[-(RING + 1 + 5) : -5]
    parts, behind, mus, sems, out_sems = refs[-5:]
    ring, spot, lead, _ = place()

    @pl.when((ring == stage) & (spot == lead))
    def _():
        copies = [pltpu.make_async_copy(part_refs[i], parts.at[i], sems.at[i]) for i in range(3)]
        copies.append(pltpu.make_async_copy(behind_ref, behind, sems.at[3]))
        wait_all(start_all(copies))

        def step(k, mu):
            j = RING - 1 - k
            mus[j] = mu
            return back_step(behind[j], mu, parts[0, j], parts[1, j], parts[2, j])

        if stage == 0:
            end = lax.fori_loop(0, RING - 1, step, mu_ref[...])
            mus[0] = end
        else:
            end = lax.fori_loop(0, RING, step, mu_ref[...], unroll=2)
        outs[RING][...] = end
        wait_all(
            start_all(
                [
                    pltpu.make_async_copy(mus.at[(lead + k) % RING], outs[k], out_sems.at[k])
                    for k in range(RING)
                ]
            )
        )


def back_chain(stage, parts, behind, mu, mus):
    args = [*parts, behind, mu]
    aliases = {len(args) + k: k for k in range(RING)}
    out = pl.pallas_call(
        lambda *refs: back_kernel(stage, *refs),
        out_shape=(field(),) * (RING + 1),
        in_specs=[ANY] * 4 + [VMEM] + [ANY] * RING,
        out_specs=(ANY,) * RING + (VMEM,),
        scratch_shapes=[
            vmem(field(3, RING)),
            vmem(lhs_shape(RING)),
            vmem(field(RING)),
            pltpu.SemaphoreType.DMA((4,)),
            pltpu.SemaphoreType.DMA((RING,)),
        ],
        input_output_aliases=aliases,
        compiler_params=PARAMS,
        name=f"back_{stage}",
    )(*args, *mus)
    return out[:RING], out[RING]


def fetch(refs, target, sem):
    _, spot, lead, _ = place()
    step = (spot + RING - lead) % RING
    for k in range(RING):

        @pl.when(step == k)
        def _():
            copy = pltpu.make_async_copy(refs[k], target, sem)
            copy.start()
            copy.wait()


def early_kernel(*refs):
    one_ref, two_ref, c_ref, refs = refs[0], refs[1], refs[2], refs[3:]
    v_refs = refs[:RING]
    states_ref, keep_ref, lhs_ref, v_ref, sem = refs[RING:]
    fetch(v_refs, v_ref, sem)
    ring, spot, _, _ = place()

    @pl.when((ring == 0) & (spot == 0))
    def _():
        v_ref[...] = swap(c_ref[...])

    v = v_ref[...]
    w0, w1 = one_ref[:, 0:576], two_ref[:, 0:576]
    t0 = jnp.tanh(conv(lhs_forward(w0), v, 1) + one_ref[:, 576:577])
    m = v + H * t0
    b1, a = two_ref[:, 576:577], two_ref[:, WPAD:BLK]
    t1 = jnp.tanh(conv(lhs_forward(w1), m, 1) + b1)
    s1 = 1.0 - t1 * t1
    s0 = 1.0 - t0 * t0
    lhs_ref[0] = lhs_backward(w0)
    behind = lhs_backward(w1)
    lhs_ref[1] = behind
    shift = H * conv(behind, s1 * a, -1)
    states_ref[0] = swap(m)
    slot = one_ref[:, WPAD:BLK]
    keep = jnp.where((ring == 0) & (spot == 0), 1.0, 0.0)
    states_ref[1] = swap(jnp.where(keep > 0.0, slot, v + 2 * H * t0 + slot))
    keep_ref[0] = v
    keep_ref[1] = m
    keep_ref[2] = s0
    keep_ref[3] = s1
    keep_ref[4] = shift
    keep_ref[5] = s0 * (H * (shift - a))


def early(one, two, c, vs):
    return pl.pallas_call(
        early_kernel,
        out_shape=(field(2), field(6), lhs_shape(2)),
        in_specs=[VMEM] * 3 + [ANY] * RING,
        scratch_shapes=[vmem(field()), pltpu.SemaphoreType.DMA],
        compiler_params=PARAMS,
        name="early",
    )(one, two, c, *vs)


def late_kernel(*refs):
    keep_ref, lhs_ref = refs[:2]
    mu_refs = refs[2 : 2 + RING]
    adjoints_ref, mine_ref, other_ref, mu_scratch, sem = refs[2 + RING :]
    fetch(mu_refs, mu_scratch, sem)
    mu = mu_scratch[...]
    s0 = keep_ref[2]
    odd_product = keep_ref[3] * mu
    odd = mu + H * conv(lhs_ref[1], odd_product, -1)
    even_term = (H / 8) * (s0 * odd)
    odd_term = (H / 8) * odd_product
    odd_grad = correlate(odd_term, keep_ref[1])
    even_grad = correlate(even_term, keep_ref[0])
    even = back_step(lhs_ref[0], mu, keep_ref[4], keep_ref[5], (2 * H) * s0)
    adjoints_ref[0] = swap(even)
    adjoints_ref[1] = swap(odd)
    pad = (CH, WPAD - 576)
    even_bias = jnp.broadcast_to(jnp.sum(even_term, axis=1, keepdims=True), pad)
    odd_bias = jnp.broadcast_to(jnp.sum(odd_term, axis=1, keepdims=True), pad)

    def write(ref, grad, bias):
        ref[:, 0:576] = grad
        ref[:, 576:WPAD] = bias

    core = place()[3]

    @pl.when(core == 0)
    def _():
        write(mine_ref, even_grad, even_bias)
        write(other_ref, odd_grad, odd_bias)

    @pl.when(core == 1)
    def _():
        write(mine_ref, odd_grad, odd_bias)
        write(other_ref, even_grad, even_bias)


def late(keep, lhs, mus):
    grad = jax.ShapeDtypeStruct((CH, WPAD), F32)
    return pl.pallas_call(
        late_kernel,
        out_shape=(field(2), grad, grad),
        in_specs=[VMEM] * 2 + [ANY] * RING,
        scratch_shapes=[vmem(field()), pltpu.SemaphoreType.DMA],
        compiler_params=PARAMS,
        name="late",
    )(keep, lhs, *mus)


def finish_kernel(mine_ref, other_ref, grad_ref, bias_ref):
    core = place()[3]
    r = lax.broadcasted_iota(jnp.int32, (CH, CH), 0)
    c = lax.broadcasted_iota(jnp.int32, (CH, CH), 1)

    def write(slot, ref):
        grad_ref[slot] = ref[:, 0:576]
        spread = jnp.broadcast_to(ref[:, 576:577], (CH, CH))
        bias_ref[slot : slot + 1] = jnp.sum(jnp.where(r == c, spread, 0.0), axis=0, keepdims=True)

    @pl.when(core == 0)
    def _():
        write(0, mine_ref)
        write(1, other_ref)

    @pl.when(core == 1)
    def _():
        write(1, mine_ref)
        write(0, other_ref)


def finish(mine, other):
    return pl.pallas_call(
        finish_kernel,
        out_shape=(
            jax.ShapeDtypeStruct((2, CH, 576), F32),
            jax.ShapeDtypeStruct((2, CH), F32),
        ),
        compiler_params=PARAMS,
        name="finish",
    )(mine, other)


def tie(*values):
    return lax.optimization_barrier(values)


NEAR = (1, 7, 2, 6, 3, 5, 4)
FAR = NEAR[::-1]
EARLY = FAR[:3]
PAIRS = ((6, 3), (2, 4), (7, 5), (1, None))


def body(coarse_guess, adjoint_guess, weights, biases):
    images = lax.axis_size("dp")
    groups = lax.axis_size("layer") // RING
    last = groups - 1

    def device(x, z, d):
        return (RING * x + z % RING) * images + d

    def lead(d):
        return 2 + 3 * (d % 2)

    everyone = [(x, d) for x in range(groups) for d in range(images)]

    def gather(value, k):
        pairs = [(device(x, lead(d) + k, d), device(x, lead(d), d)) for x, d in everyone]
        return lax.ppermute(value, AXES, pairs)

    def gather_pair(value, direct, helped):
        pairs = [(device(x, lead(d) + direct, d), device(x, lead(d), d)) for x, d in everyone]
        if helped is not None:
            pairs += [
                (device(x, lead(d) + helped, d), device(x, lead(d), d ^ 1)) for x, d in everyone
            ]
        return lax.ppermute(value, AXES, pairs)

    def hand_over(value):
        pairs = [(device(x, lead(d), d ^ 1), device(x, lead(d), d)) for x, d in everyone]
        return lax.ppermute(value, AXES, pairs)

    def scatter(value, k):
        pairs = [(device(x, lead(d), d), device(x, lead(d) + k, d)) for x, d in everyone]
        return lax.ppermute(value, AXES, pairs)

    def hop(value, source, target):
        pairs = [
            (device(source, lead(d), d), device(target, lead(d), d)) for d in range(images)
        ]
        return lax.ppermute(value, AXES, pairs)

    c, a = coarse_guess[0, 0], adjoint_guess[0, 0]
    one, two = relax(c, a, weights, biases)
    ones, twos = [one] + [None] * (RING - 1), [two] + [None] * (RING - 1)
    for direct, helped in PAIRS:
        ones[direct] = gather_pair(one, direct, helped)
        if helped is not None:
            ones[helped] = hand_over(ones[direct])
    vt, end = first_chain(ones)
    v = hop(end, 0, 1)
    ahead0, behind0 = prepare([tie(end, one)[1]] + ones[1:], "prepare")
    for k in NEAR:
        twos[k] = gather(two, k)
    for stage in range(1, last):
        if stage == 1:
            got = tie(v, *[twos[k] for k in EARLY])
            v = got[0]
            for k, value in zip(EARLY, got[1:]):
                twos[k] = value
        vt, end = chain(stage, ones, ahead0, v, vt)
        v = hop(end, stage, stage + 1)
    ahead1, behind1 = prepare(twos, "prepare2")
    vs, mus, end = turn(last, ones, twos, [ahead0, behind0, ahead1, behind1], v)
    mu = hop(end, last, last - 1)
    vs, parts = middle(last, twos, vt, ahead1, behind1, vs)
    own_v = [vs[0]] + [None] * (RING - 1)
    for stage in range(last - 1, -1, -1):
        if stage == last - 1:
            chunk, gate = FAR[:4], parts[0]
        elif stage == last - 2:
            chunk, gate = FAR[4:], end
        else:
            chunk = ()
        for k in chunk:
            own_v[k] = scatter(tie(gate, vs[k])[1], k)
        if stage == last - 1:
            mu, *parts = tie(mu, *parts)
        if stage == 0:
            states, keep, lhs = early(one, two, c, own_v)
            mu, keep = tie(mu, keep)
        mus, end = back_chain(stage, parts, behind0, mu, mus)
        if stage == last - 1:
            got = tie(end, *[own_v[k] for k in chunk])
            end = got[0]
            for k, value in zip(chunk, got[1:]):
                own_v[k] = value
        if stage > 0:
            mu = hop(end, stage, stage - 1)
    own_mu = [mus[0]] + [None] * (RING - 1)
    for k in FAR:
        own_mu[k] = scatter(mus[k], k)
    adjoints, mine, other = late(keep, lhs, own_mu)
    mine = mine + lax.ppermute(other, "dp", [(i, i ^ 1) for i in range(images)])
    for flip in (2, 6):
        mine = mine + lax.ppermute(mine, "dp", [(i, i ^ flip) for i in range(images)])
    other = lax.ppermute(mine, "dp", [(i, i ^ 1) for i in range(images)])
    grad, bias = finish(mine, other)
    return states[:, None], adjoints[:, None], grad, bias


def solution(mesh):
    return jax.shard_map(
        body,
        mesh=mesh,
        in_specs=(
            P("layer", "dp", None, None),
            P("layer", "dp", None, None),
            P("layer", None, None),
            P("layer", None),
        ),
        out_specs=(
            P("layer", "dp", None, None),
            P("layer", "dp", None, None),
            P("layer", None, None),
            P("layer", None),
        ),
        check_vma=False,
    )
```

```python
import jax
import jax.numpy as jnp
from jax import lax
from jax.experimental import pallas as pl
from jax.experimental.pallas import tpu as pltpu
from jax.sharding import PartitionSpec as P

F32 = jnp.float32
BF16 = jnp.bfloat16
H = 0.125
CH, CELLS = 64, 512
WPAD = 640
BLK = WPAD + CELLS
RING = 8
AXES = ("layer", "dp")
ANY = pl.BlockSpec(memory_space=pl.ANY)
HBM = pl.BlockSpec(memory_space=pltpu.HBM)
VMEM = pl.BlockSpec(memory_space=pltpu.VMEM)
PARAMS = pltpu.CompilerParams(vmem_limit_bytes=40 << 20)


def split(x):
    hi = x.astype(BF16)
    return hi, (x - hi.astype(F32)).astype(BF16)


def lane_index():
    return lax.broadcasted_iota(jnp.int32, (CH, 128), 1)


def columns(x):
    return [x[:, 128 * a : 128 * (a + 1)] for a in range(4)]


def swap(x):
    parts, lane, out = columns(x), lane_index(), []
    for a in range(4):
        acc = None
        for b in range(4):
            shift = ((b - a) * 32) % 128
            part = parts[b] if shift == 0 else pltpu.roll(parts[b], shift, 1)
            acc = part if acc is None else jnp.where(lane >= 32 * b, part, acc)
        out.append(acc)
    return jnp.concatenate(out, 1)


def lhs_forward(w):
    hi = w.astype(BF16).astype(F32)
    lo = w - hi
    rows = []
    for t in range(9):
        a, b = hi[:, 64 * t : 64 * t + 64], lo[:, 64 * t : 64 * t + 64]
        rows.append(jnp.concatenate([a, a, b], 1).astype(BF16))
    return jnp.concatenate(rows, 0)


def lhs_backward(w):
    wt = w.T
    hi = wt.astype(BF16).astype(F32)
    lo = wt - hi
    return jnp.concatenate([hi, hi, lo], 1).astype(BF16)


def conv(lhs, x, sign):
    hi, lo = split(x)
    z = jnp.dot(lhs, jnp.concatenate([hi, lo, hi], 0), preferred_element_type=F32)
    lane = lane_index()
    q = lane % 32
    lower, upper, right, left = lane < 96, lane >= 32, q < 31, q > 0

    def tap(a, e, col):
        t = 3 * (sign * a + 1) + (sign * e + 1)
        return z[64 * t : 64 * t + 64, 128 * col : 128 * col + 128]

    out = []
    for col in range(4):
        s = []
        for e in (-1, 0, 1):
            if col < 3:
                up = tap(1, e, col + 1)
            else:
                up = jnp.where(lower, pltpu.roll(tap(1, e, 0), 96, 1), 0.0)
            if col > 0:
                down = tap(-1, e, col - 1)
            else:
                down = jnp.where(upper, pltpu.roll(tap(-1, e, 3), 32, 1), 0.0)
            s.append(tap(0, e, col) + up + down)
        out.append(
            s[1]
            + jnp.where(right, pltpu.roll(s[2], 127, 1), 0.0)
            + jnp.where(left, pltpu.roll(s[0], 1, 1), 0.0)
        )
    return jnp.concatenate(out, 1)


def patches(x):
    lane = lane_index()
    q = lane % 32
    lower, upper, right, left = lane < 96, lane >= 32, q < 31, q > 0
    mid = columns(x)
    base = {
        0: mid,
        1: [jnp.where(right, pltpu.roll(c, 127, 1), 0.0) for c in mid],
        -1: [jnp.where(left, pltpu.roll(c, 1, 1), 0.0) for c in mid],
    }
    hi, lo = [], []
    for a in (-1, 0, 1):
        for e in (-1, 0, 1):
            c = base[e]
            if a == 1:
                c = c[1:] + [jnp.where(lower, pltpu.roll(c[0], 96, 1), 0.0)]
            elif a == -1:
                c = [jnp.where(upper, pltpu.roll(c[3], 32, 1), 0.0)] + c[:3]
            h, l = split(jnp.concatenate(c, 1))
            hi.append(h)
            lo.append(l)
    return jnp.concatenate(hi, 0), jnp.concatenate(lo, 0)


def dot_t(a, b):
    return lax.dot_general(a, b, (((1,), (1,)), ((), ())), preferred_element_type=F32)


def correlate(term, x):
    t_hi, t_lo = split(term)
    p_hi, p_lo = patches(x)
    return dot_t(t_hi, p_hi) + dot_t(t_hi, p_lo) + dot_t(t_lo, p_hi)


def as_column(row):
    r = lax.broadcasted_iota(jnp.int32, (CH, CH), 0)
    c = lax.broadcasted_iota(jnp.int32, (CH, CH), 1)
    spread = jnp.broadcast_to(row, (CH, CH))
    return jnp.sum(jnp.where(r == c, spread, 0.0), axis=1, keepdims=True)


def place():
    layer, image = lax.axis_index("layer"), lax.axis_index("dp")
    core = image % 2
    return layer // RING, layer % RING, 2 + 3 * core, core


def start_all(copies):
    for copy in copies:
        copy.start()
    return copies


def wait_all(copies):
    for copy in copies:
        copy.wait()


def field(*lead):
    return jax.ShapeDtypeStruct((*lead, CH, CELLS), F32)


def lhs_shape(*lead):
    return jax.ShapeDtypeStruct((*lead, 9 * CH, 3 * CH), BF16)


def vmem(shape):
    return pltpu.VMEM(shape.shape, shape.dtype)


def relax_kernel(c_hbm, a_hbm, w_hbm, b_hbm, one_ref, two_ref, c_ref, a_ref, w_ref, b_ref, sems):
    copies = start_all(
        [
            pltpu.make_async_copy(source, target, sems.at[i])
            for i, (source, target) in enumerate(
                [(b_hbm, b_ref), (w_hbm, w_ref), (c_hbm, c_ref), (a_hbm, a_ref)]
            )
        ]
    )
    wait_all(copies[:3])
    c = swap(c_ref[...])
    w0, w1 = w_ref[0], w_ref[1]
    b0, b1 = as_column(b_ref[0:1]), as_column(b_ref[1:2])
    t0 = jnp.tanh(conv(lhs_forward(w0), c, 1) + b0)
    t1 = jnp.tanh(conv(lhs_forward(w1), c + H * t0, 1) + b1)
    pad = WPAD - 576
    one_ref[:, 0:576] = w0
    one_ref[:, 576:WPAD] = jnp.broadcast_to(b0, (CH, pad))
    ring, spot, _, _ = place()
    keep = jnp.where((ring == 0) & (spot == 0), 1.0, 0.0)
    one_ref[:, WPAD:BLK] = jnp.where(keep > 0.0, c + H * t0 + H * t1, H * (t1 - t0))
    two_ref[:, 0:576] = w1
    two_ref[:, 576:WPAD] = jnp.broadcast_to(b1, (CH, pad))
    wait_all(copies[3:])
    two_ref[:, WPAD:BLK] = swap(a_ref[...])


def relax(c, a, w, b):
    shape = jax.ShapeDtypeStruct((CH, BLK), F32)
    return pl.pallas_call(
        relax_kernel,
        out_shape=(shape, shape),
        in_specs=[HBM] * 4,
        scratch_shapes=[
            pltpu.VMEM(c.shape, F32),
            pltpu.VMEM(a.shape, F32),
            pltpu.VMEM(w.shape, F32),
            pltpu.VMEM(b.shape, F32),
            pltpu.SemaphoreType.DMA((4,)),
        ],
        compiler_params=pltpu.CompilerParams(vmem_limit_bytes=63 << 20),
        name="relax",
    )(c, a, w, b)


MATRIX = pl.ds(0, WPAD)
REST = pl.ds(CELLS, WPAD)
BIAS = WPAD - 576


def slots(refs, target, sems, lead, part=None):
    if part is not None:
        refs = [ref.at[:, part] for ref in refs]
    copies = []
    for k, ref in enumerate(refs):
        j = (lead + k) % RING
        copies.append(pltpu.make_async_copy(ref, target.at[j], sems.at[j]))
    return copies


HALF = RING // 2


def half(array, i):
    return array.at[pl.ds(HALF * i, HALF)]


def half_out(vt, vt_ref, sems, part):
    return start_all(
        [
            pltpu.make_async_copy(half(vt.at[i], part), half(vt_ref.at[i], part), sems.at[i, part])
            for i in (0, 1)
        ]
    )


def first_kernel(*refs):
    one_refs = refs[:RING]
    vt_ref, out_ref, tau, even, vt, lhs, tau_sems, even_sems, sems = refs[RING:]
    ring, spot, lead, _ = place()

    @pl.when((ring == 0) & (spot == lead))
    def _():
        copies = slots(one_refs, even, even_sems, lead, MATRIX)
        copies += slots(one_refs, tau, tau_sems, lead, REST)
        wait_all(start_all(copies))

        def prepare(j, carry):
            lhs[j] = lhs_forward(even[j][:, 0:576])
            return carry

        lax.fori_loop(1, RING, prepare, 0)

        def step(j, v):
            now = jnp.tanh(conv(lhs[j], v, 1) + tau[j][:, BIAS : BIAS + 1])
            vt[0, j] = v
            vt[1, j] = now
            return v + 2 * H * now + tau[j][:, WPAD - CELLS :]

        v = lax.fori_loop(1, HALF, step, tau[0][:, WPAD - CELLS :])
        copies = half_out(vt, vt_ref, sems, 0)
        out_ref[...] = lax.fori_loop(HALF, RING, step, v)
        wait_all(copies + half_out(vt, vt_ref, sems, 1))


def first_chain(ones):
    return pl.pallas_call(
        first_kernel,
        out_shape=(field(2, RING), field()),
        in_specs=[ANY] * RING,
        out_specs=(ANY, VMEM),
        scratch_shapes=[
            pltpu.VMEM((RING, CH, WPAD), F32),
            pltpu.VMEM((RING, CH, WPAD), F32),
            vmem(field(2, RING)),
            vmem(lhs_shape(RING)),
            pltpu.SemaphoreType.DMA((RING,)),
            pltpu.SemaphoreType.DMA((RING,)),
            pltpu.SemaphoreType.DMA((2, 2)),
        ],
        compiler_params=PARAMS,
        name="chain_0",
    )(*ones)


def prepare_kernel(*refs):
    block_refs, outs = refs[:RING], refs[RING : RING + 2]
    w, ahead, behind, sems, out_sems = refs[RING + 2 :]
    _, spot, lead, _ = place()

    @pl.when(spot == lead)
    def _():
        wait_all(start_all(slots(block_refs, w, sems, lead, MATRIX)))

        def step(j, carry):
            ahead[j] = lhs_forward(w[j][:, 0:576])
            behind[j] = lhs_backward(w[j][:, 0:576])
            return carry

        lax.fori_loop(0, RING, step, 0)
        wait_all(
            start_all(
                [
                    pltpu.make_async_copy(ahead, outs[0], out_sems.at[0]),
                    pltpu.make_async_copy(behind, outs[1], out_sems.at[1]),
                ]
            )
        )


def prepare(blocks, name):
    return pl.pallas_call(
        prepare_kernel,
        out_shape=(lhs_shape(RING), lhs_shape(RING)),
        in_specs=[ANY] * RING,
        out_specs=(ANY, ANY),
        scratch_shapes=[
            pltpu.VMEM((RING, CH, WPAD), F32),
            vmem(lhs_shape(RING)),
            vmem(lhs_shape(RING)),
            pltpu.SemaphoreType.DMA((RING,)),
            pltpu.SemaphoreType.DMA((2,)),
        ],
        compiler_params=PARAMS,
        cost_estimate=pl.CostEstimate(flops=0, bytes_accessed=20 << 20, transcendentals=0),
        name=name,
    )(*blocks)


def chain_kernel(stage, *refs):
    tau_refs, ahead_ref, v_ref = refs[:RING], refs[RING], refs[RING + 1]
    vt_ref, out_ref, tau, vt, ahead, tau_sems, ahead_sems, sems = refs[-8:]
    ring, spot, lead, _ = place()

    @pl.when((ring == stage) & (spot == lead))
    def _():
        copies = start_all(slots(tau_refs, tau, tau_sems, lead, REST))
        halves = start_all(
            [
                pltpu.make_async_copy(half(ahead_ref, i), half(ahead, i), ahead_sems.at[i])
                for i in (0, 1)
            ]
        )
        wait_all(copies + halves[:1])

        def step(j, v):
            now = jnp.tanh(conv(ahead[j], v, 1) + tau[j][:, BIAS : BIAS + 1])
            vt[0, j] = v
            vt[1, j] = now
            return v + 2 * H * now + tau[j][:, WPAD - CELLS :]

        v = lax.fori_loop(0, HALF, step, v_ref[...], unroll=2)
        wait_all(halves[1:])
        copies = half_out(vt, vt_ref, sems, 0)
        out_ref[...] = lax.fori_loop(HALF, RING, step, v, unroll=2)
        wait_all(copies + half_out(vt, vt_ref, sems, 1))


def chain(stage, taus, ahead, v, vt):
    args = [*taus, ahead, v]
    return pl.pallas_call(
        lambda *refs: chain_kernel(stage, *refs),
        out_shape=(field(2, RING), field()),
        in_specs=[ANY] * (RING + 1) + [VMEM, ANY],
        out_specs=(ANY, VMEM),
        scratch_shapes=[
            pltpu.VMEM((RING, CH, WPAD), F32),
            vmem(field(2, RING)),
            vmem(lhs_shape(RING)),
            pltpu.SemaphoreType.DMA((RING,)),
            pltpu.SemaphoreType.DMA((2,)),
            pltpu.SemaphoreType.DMA((2, 2)),
        ],
        input_output_aliases={len(args): 0},
        compiler_params=PARAMS,
        name=f"chain_{stage}",
    )(*args, vt)


def correction(ahead, behind, v, t0, b1, a):
    t1 = jnp.tanh(conv(ahead, v + H * t0, 1) + b1)
    shift = H * conv(behind, (1.0 - t1 * t1) * a, -1)
    s0 = 1.0 - t0 * t0
    return shift, s0 * (H * (shift - a)), (2 * H) * s0


def back_step(behind, mu, shift, part, slope):
    return mu + shift + conv(behind, slope * mu + part, -1)


def middle_kernel(last, *refs):
    two_refs, (vt_ref, ahead_ref, behind_ref) = refs[:RING], refs[RING : RING + 3]
    outs = refs[-(RING + 3 + 7) : -7]
    two, vt, ahead, behind, out, two_sems, sems = refs[-7:]
    ring, spot, lead, _ = place()

    @pl.when((spot == lead) & (ring < last))
    def _():
        copies = start_all(slots(two_refs, two, two_sems, lead))
        copies += start_all(
            [
                pltpu.make_async_copy(vt_ref, vt, sems.at[0]),
                pltpu.make_async_copy(ahead_ref, ahead, sems.at[1]),
                pltpu.make_async_copy(behind_ref, behind, sems.at[2]),
            ]
        )
        wait_all(copies)
        copies = start_all(
            [
                pltpu.make_async_copy(vt.at[0, (lead + k) % RING], outs[k], two_sems.at[k])
                for k in range(RING)
            ]
        )

        def step(j, carry):
            b1, a = two[j][:, 576:577], two[j][:, WPAD:BLK]
            got = correction(ahead[j], behind[j], vt[0, j], vt[1, j], b1, a)
            for i in range(3):
                out[i, j] = got[i]
            return carry

        lax.fori_loop(0, RING, step, 0, unroll=2)
        copies += start_all(
            [pltpu.make_async_copy(out.at[i], outs[RING + i], sems.at[i]) for i in range(3)]
        )
        wait_all(copies)


def middle(last, twos, vt, ahead, behind, vs):
    args = [*twos, vt, ahead, behind]
    out = pl.pallas_call(
        lambda *refs: middle_kernel(last, *refs),
        out_shape=(field(),) * RING + (field(RING),) * 3,
        in_specs=[ANY] * (2 * RING + 3),
        out_specs=(ANY,) * (RING + 3),
        scratch_shapes=[
            pltpu.VMEM((RING, CH, BLK), F32),
            vmem(field(2, RING)),
            vmem(lhs_shape(RING)),
            vmem(lhs_shape(RING)),
            vmem(field(3, RING)),
            pltpu.SemaphoreType.DMA((RING,)),
            pltpu.SemaphoreType.DMA((3,)),
        ],
        input_output_aliases={len(args) + k: k for k in range(RING)},
        compiler_params=PARAMS,
        name="middle",
    )(*args, *vs)
    return out[:RING], out[RING:]


def turn_kernel(stage, *refs):
    tau_refs, two_refs = refs[:RING], refs[RING : 2 * RING]
    lhs_refs, v_ref = refs[2 * RING : 2 * RING + 4], refs[2 * RING + 4]
    v_refs = refs[2 * RING + 5 : 3 * RING + 5]
    mu_refs = refs[3 * RING + 5 : 4 * RING + 5]
    out_ref, tau, two, vs, t, mus, lhs, out, sems, lhs_sems = refs[4 * RING + 5 :]
    ring, spot, lead, _ = place()

    @pl.when((ring == stage) & (spot == lead))
    def _():
        copies = start_all(slots(tau_refs, tau, sems.at[0], lead, REST))
        matrices = [
            pltpu.make_async_copy(lhs_refs[i], lhs.at[i], lhs_sems.at[i]) for i in range(4)
        ]
        start_all(matrices[:1])
        block_copies = start_all(slots(two_refs, two, sems.at[1], lead))
        start_all(matrices[2:] + matrices[1:2])
        wait_all(copies + matrices[:1])

        def ahead_step(j, v):
            now = jnp.tanh(conv(lhs[0, j], v, 1) + tau[j][:, BIAS : BIAS + 1])
            vs[j] = v
            t[j] = now
            return v + 2 * H * now + tau[j][:, WPAD - CELLS :]

        def correct(j, carry):
            b1, a = two[j][:, 576:577], two[j][:, WPAD:BLK]
            got = correction(lhs[2, j], lhs[3, j], vs[j], t[j], b1, a)
            for i in range(3):
                out[i, j] = got[i]
            return carry

        lax.fori_loop(0, RING, ahead_step, v_ref[...], unroll=2)
        copies = start_all(
            [
                pltpu.make_async_copy(vs.at[(lead + k) % RING], v_refs[k], sems.at[0, k])
                for k in range(RING)
            ]
        )
        wait_all(block_copies + matrices[2:])
        lax.fori_loop(0, RING, correct, 0, unroll=2)
        wait_all(matrices[1:2])

        def back(k, mu):
            j = RING - 1 - k
            mus[j] = mu
            return back_step(lhs[1, j], mu, out[0, j], out[1, j], out[2, j])

        out_ref[...] = lax.fori_loop(0, RING, back, two[RING - 1][:, WPAD:BLK], unroll=2)
        copies += start_all(
            [
                pltpu.make_async_copy(mus.at[(lead + k) % RING], mu_refs[k], sems.at[1, k])
                for k in range(RING)
            ]
        )
        wait_all(copies)


def turn(stage, taus, twos, lhs, v):
    out = pl.pallas_call(
        lambda *refs: turn_kernel(stage, *refs),
        out_shape=(field(),) * (2 * RING + 1),
        in_specs=[ANY] * (2 * RING + 4) + [VMEM],
        out_specs=(ANY,) * (2 * RING) + (VMEM,),
        scratch_shapes=[
            pltpu.VMEM((RING, CH, WPAD), F32),
            pltpu.VMEM((RING, CH, BLK), F32),
            vmem(field(RING)),
            vmem(field(RING)),
            vmem(field(RING)),
            vmem(lhs_shape(4, RING)),
            vmem(field(3, RING)),
            pltpu.SemaphoreType.DMA((2, RING)),
            pltpu.SemaphoreType.DMA((4,)),
        ],
        compiler_params=PARAMS,
        name="turn",
    )(*taus, *twos, *lhs, v)
    return out[:RING], out[RING : 2 * RING], out[2 * RING]


def back_kernel(stage, *refs):
    part_refs, behind_ref, mu_ref = refs[:3], refs[3], refs[4]
    outs = refs[-(RING + 1 + 5) : -5]
    parts, behind, mus, sems, out_sems = refs[-5:]
    ring, spot, lead, _ = place()

    @pl.when((ring == stage) & (spot == lead))
    def _():
        copies = [pltpu.make_async_copy(part_refs[i], parts.at[i], sems.at[i]) for i in range(3)]
        copies.append(pltpu.make_async_copy(behind_ref, behind, sems.at[3]))
        wait_all(start_all(copies))

        def step(k, mu):
            j = RING - 1 - k
            mus[j] = mu
            return back_step(behind[j], mu, parts[0, j], parts[1, j], parts[2, j])

        if stage == 0:
            end = lax.fori_loop(0, RING - 1, step, mu_ref[...])
            mus[0] = end
        else:
            end = lax.fori_loop(0, RING, step, mu_ref[...], unroll=2)
        outs[RING][...] = end
        wait_all(
            start_all(
                [
                    pltpu.make_async_copy(mus.at[(lead + k) % RING], outs[k], out_sems.at[k])
                    for k in range(RING)
                ]
            )
        )


def back_chain(stage, parts, behind, mu, mus):
    args = [*parts, behind, mu]
    aliases = {len(args) + k: k for k in range(RING)}
    out = pl.pallas_call(
        lambda *refs: back_kernel(stage, *refs),
        out_shape=(field(),) * (RING + 1),
        in_specs=[ANY] * 4 + [VMEM] + [ANY] * RING,
        out_specs=(ANY,) * RING + (VMEM,),
        scratch_shapes=[
            vmem(field(3, RING)),
            vmem(lhs_shape(RING)),
            vmem(field(RING)),
            pltpu.SemaphoreType.DMA((4,)),
            pltpu.SemaphoreType.DMA((RING,)),
        ],
        input_output_aliases=aliases,
        compiler_params=PARAMS,
        name=f"back_{stage}",
    )(*args, *mus)
    return out[:RING], out[RING]


def fetch(refs, target, sem):
    _, spot, lead, _ = place()
    step = (spot + RING - lead) % RING
    for k in range(RING):

        @pl.when(step == k)
        def _():
            copy = pltpu.make_async_copy(refs[k], target, sem)
            copy.start()
            copy.wait()


def early_kernel(*refs):
    one_ref, two_ref, c_ref, refs = refs[0], refs[1], refs[2], refs[3:]
    v_refs = refs[:RING]
    states_ref, keep_ref, lhs_ref, v_ref, sem = refs[RING:]
    fetch(v_refs, v_ref, sem)
    ring, spot, _, _ = place()

    @pl.when((ring == 0) & (spot == 0))
    def _():
        v_ref[...] = swap(c_ref[...])

    v = v_ref[...]
    w0, w1 = one_ref[:, 0:576], two_ref[:, 0:576]
    t0 = jnp.tanh(conv(lhs_forward(w0), v, 1) + one_ref[:, 576:577])
    m = v + H * t0
    b1, a = two_ref[:, 576:577], two_ref[:, WPAD:BLK]
    t1 = jnp.tanh(conv(lhs_forward(w1), m, 1) + b1)
    s1 = 1.0 - t1 * t1
    s0 = 1.0 - t0 * t0
    lhs_ref[0] = lhs_backward(w0)
    behind = lhs_backward(w1)
    lhs_ref[1] = behind
    shift = H * conv(behind, s1 * a, -1)
    states_ref[0] = swap(m)
    slot = one_ref[:, WPAD:BLK]
    keep = jnp.where((ring == 0) & (spot == 0), 1.0, 0.0)
    states_ref[1] = swap(jnp.where(keep > 0.0, slot, v + 2 * H * t0 + slot))
    keep_ref[0] = v
    keep_ref[1] = m
    keep_ref[2] = s0
    keep_ref[3] = s1
    keep_ref[4] = shift
    keep_ref[5] = s0 * (H * (shift - a))


def early(one, two, c, vs):
    return pl.pallas_call(
        early_kernel,
        out_shape=(field(2), field(6), lhs_shape(2)),
        in_specs=[VMEM] * 3 + [ANY] * RING,
        scratch_shapes=[vmem(field()), pltpu.SemaphoreType.DMA],
        compiler_params=PARAMS,
        name="early",
    )(one, two, c, *vs)


def late_kernel(*refs):
    keep_ref, lhs_ref = refs[:2]
    mu_refs = refs[2 : 2 + RING]
    adjoints_ref, mine_ref, other_ref, mu_scratch, sem = refs[2 + RING :]
    fetch(mu_refs, mu_scratch, sem)
    mu = mu_scratch[...]
    s0 = keep_ref[2]
    odd_product = keep_ref[3] * mu
    odd = mu + H * conv(lhs_ref[1], odd_product, -1)
    even_term = (H / 8) * (s0 * odd)
    odd_term = (H / 8) * odd_product
    odd_grad = correlate(odd_term, keep_ref[1])
    even_grad = correlate(even_term, keep_ref[0])
    even = back_step(lhs_ref[0], mu, keep_ref[4], keep_ref[5], (2 * H) * s0)
    adjoints_ref[0] = swap(even)
    adjoints_ref[1] = swap(odd)
    pad = (CH, WPAD - 576)
    even_bias = jnp.broadcast_to(jnp.sum(even_term, axis=1, keepdims=True), pad)
    odd_bias = jnp.broadcast_to(jnp.sum(odd_term, axis=1, keepdims=True), pad)

    def write(ref, grad, bias):
        ref[:, 0:576] = grad
        ref[:, 576:WPAD] = bias

    core = place()[3]

    @pl.when(core == 0)
    def _():
        write(mine_ref, even_grad, even_bias)
        write(other_ref, odd_grad, odd_bias)

    @pl.when(core == 1)
    def _():
        write(mine_ref, odd_grad, odd_bias)
        write(other_ref, even_grad, even_bias)


def late(keep, lhs, mus):
    grad = jax.ShapeDtypeStruct((CH, WPAD), F32)
    return pl.pallas_call(
        late_kernel,
        out_shape=(field(2), grad, grad),
        in_specs=[VMEM] * 2 + [ANY] * RING,
        scratch_shapes=[vmem(field()), pltpu.SemaphoreType.DMA],
        compiler_params=PARAMS,
        name="late",
    )(keep, lhs, *mus)


def finish_kernel(mine_ref, other_ref, grad_ref, bias_ref):
    core = place()[3]
    r = lax.broadcasted_iota(jnp.int32, (CH, CH), 0)
    c = lax.broadcasted_iota(jnp.int32, (CH, CH), 1)

    def write(slot, ref):
        grad_ref[slot] = ref[:, 0:576]
        spread = jnp.broadcast_to(ref[:, 576:577], (CH, CH))
        bias_ref[slot : slot + 1] = jnp.sum(jnp.where(r == c, spread, 0.0), axis=0, keepdims=True)

    @pl.when(core == 0)
    def _():
        write(0, mine_ref)
        write(1, other_ref)

    @pl.when(core == 1)
    def _():
        write(1, mine_ref)
        write(0, other_ref)


def finish(mine, other):
    return pl.pallas_call(
        finish_kernel,
        out_shape=(
            jax.ShapeDtypeStruct((2, CH, 576), F32),
            jax.ShapeDtypeStruct((2, CH), F32),
        ),
        compiler_params=PARAMS,
        name="finish",
    )(mine, other)


def tie(*values):
    return lax.optimization_barrier(values)


NEAR = (1, 7, 2, 6, 3, 5, 4)
FAR = NEAR[::-1]
EARLY = FAR[:0]
PAIRS = ((6, 3), (2, 4), (7, 5), (1, None))


def body(coarse_guess, adjoint_guess, weights, biases):
    images = lax.axis_size("dp")
    groups = lax.axis_size("layer") // RING
    last = groups - 1

    def device(x, z, d):
        return (RING * x + z % RING) * images + d

    def lead(d):
        return 2 + 3 * (d % 2)

    everyone = [(x, d) for x in range(groups) for d in range(images)]

    def gather(value, k):
        pairs = [(device(x, lead(d) + k, d), device(x, lead(d), d)) for x, d in everyone]
        return lax.ppermute(value, AXES, pairs)

    def gather_pair(value, direct, helped):
        pairs = [(device(x, lead(d) + direct, d), device(x, lead(d), d)) for x, d in everyone]
        if helped is not None:
            pairs += [
                (device(x, lead(d) + helped, d), device(x, lead(d), d ^ 1)) for x, d in everyone
            ]
        return lax.ppermute(value, AXES, pairs)

    def hand_over(value):
        pairs = [(device(x, lead(d), d ^ 1), device(x, lead(d), d)) for x, d in everyone]
        return lax.ppermute(value, AXES, pairs)

    def scatter(value, k):
        pairs = [(device(x, lead(d), d), device(x, lead(d) + k, d)) for x, d in everyone]
        return lax.ppermute(value, AXES, pairs)

    def hop(value, source, target):
        pairs = [
            (device(source, lead(d), d), device(target, lead(d), d)) for d in range(images)
        ]
        return lax.ppermute(value, AXES, pairs)

    c, a = coarse_guess[0, 0], adjoint_guess[0, 0]
    one, two = relax(c, a, weights, biases)
    ones, twos = [one] + [None] * (RING - 1), [two] + [None] * (RING - 1)
    for direct, helped in PAIRS:
        ones[direct] = gather_pair(one, direct, helped)
        if helped is not None:
            ones[helped] = hand_over(ones[direct])
    vt, end = first_chain(ones)
    v = hop(end, 0, 1)
    ahead0, behind0 = prepare([tie(end, one)[1]] + ones[1:], "prepare")
    for k in NEAR:
        twos[k] = gather(two, k)
    for stage in range(1, last):
        vt, end = chain(stage, ones, ahead0, v, vt)
        v = hop(end, stage, stage + 1)
    ahead1, behind1 = prepare(twos, "prepare2")
    vs, mus, end = turn(last, ones, twos, [ahead0, behind0, ahead1, behind1], v)
    mu = hop(end, last, last - 1)
    vs, parts = middle(last, twos, vt, ahead1, behind1, vs)
    own_v = [vs[0]] + [None] * (RING - 1)
    for stage in range(last - 1, -1, -1):
        if stage == last - 1:
            chunk, gate = FAR[:4], parts[0]
        elif stage == last - 2:
            chunk, gate = FAR[4:], end
        else:
            chunk = ()
        for k in chunk:
            own_v[k] = scatter(tie(gate, vs[k])[1], k)
        if stage == last - 1:
            mu, *parts = tie(mu, *parts)
        if stage == 0:
            states, keep, lhs = early(one, two, c, own_v)
            mu, keep = tie(mu, keep)
        mus, end = back_chain(stage, parts, behind0, mu, mus)
        if stage == last - 1:
            got = tie(end, *[own_v[k] for k in chunk])
            end = got[0]
            for k, value in zip(chunk, got[1:]):
                own_v[k] = value
        if stage > 0:
            mu = hop(end, stage, stage - 1)
    own_mu = [mus[0]] + [None] * (RING - 1)
    for k in FAR:
        own_mu[k] = scatter(mus[k], k)
    adjoints, mine, other = late(keep, lhs, own_mu)
    mine = mine + lax.ppermute(other, "dp", [(i, i ^ 1) for i in range(images)])
    for flip in (2, 6):
        mine = mine + lax.ppermute(mine, "dp", [(i, i ^ flip) for i in range(images)])
    other = lax.ppermute(mine, "dp", [(i, i ^ 1) for i in range(images)])
    grad, bias = finish(mine, other)
    return states[:, None], adjoints[:, None], grad, bias


def solution(mesh):
    return jax.shard_map(
        body,
        mesh=mesh,
        in_specs=(
            P("layer", "dp", None, None),
            P("layer", "dp", None, None),
            P("layer", None, None),
            P("layer", None),
        ),
        out_specs=(
            P("layer", "dp", None, None),
            P("layer", "dp", None, None),
            P("layer", None, None),
            P("layer", None),
        ),
        check_vma=False,
    )
```

```python
import jax
import jax.numpy as jnp
from jax import lax
from jax.experimental import pallas as pl
from jax.experimental.pallas import tpu as pltpu
from jax.sharding import PartitionSpec as P

F32 = jnp.float32
BF16 = jnp.bfloat16
H = 0.125
CH, CELLS = 64, 512
WPAD = 640
BLK = WPAD + CELLS
RING = 8
AXES = ("layer", "dp")
ANY = pl.BlockSpec(memory_space=pl.ANY)
HBM = pl.BlockSpec(memory_space=pltpu.HBM)
VMEM = pl.BlockSpec(memory_space=pltpu.VMEM)
PARAMS = pltpu.CompilerParams(vmem_limit_bytes=28 << 20)


def split(x):
    hi = x.astype(BF16)
    return hi, (x - hi.astype(F32)).astype(BF16)


def lane_index():
    return lax.broadcasted_iota(jnp.int32, (CH, 128), 1)


def columns(x):
    return [x[:, 128 * a : 128 * (a + 1)] for a in range(4)]


def swap(x):
    parts, lane, out = columns(x), lane_index(), []
    for a in range(4):
        acc = None
        for b in range(4):
            shift = ((b - a) * 32) % 128
            part = parts[b] if shift == 0 else pltpu.roll(parts[b], shift, 1)
            acc = part if acc is None else jnp.where(lane >= 32 * b, part, acc)
        out.append(acc)
    return jnp.concatenate(out, 1)


def lhs_forward(w):
    hi = w.astype(BF16).astype(F32)
    lo = w - hi
    rows = []
    for t in range(9):
        a, b = hi[:, 64 * t : 64 * t + 64], lo[:, 64 * t : 64 * t + 64]
        rows.append(jnp.concatenate([a, a, b], 1).astype(BF16))
    return jnp.concatenate(rows, 0)


def lhs_backward(w):
    wt = w.T
    hi = wt.astype(BF16).astype(F32)
    lo = wt - hi
    return jnp.concatenate([hi, hi, lo], 1).astype(BF16)


def conv(lhs, x, sign):
    hi, lo = split(x)
    z = jnp.dot(lhs, jnp.concatenate([hi, lo, hi], 0), preferred_element_type=F32)
    lane = lane_index()
    q = lane % 32
    lower, upper, right, left = lane < 96, lane >= 32, q < 31, q > 0

    def tap(a, e, col):
        t = 3 * (sign * a + 1) + (sign * e + 1)
        return z[64 * t : 64 * t + 64, 128 * col : 128 * col + 128]

    out = []
    for col in range(4):
        s = []
        for e in (-1, 0, 1):
            if col < 3:
                up = tap(1, e, col + 1)
            else:
                up = jnp.where(lower, pltpu.roll(tap(1, e, 0), 96, 1), 0.0)
            if col > 0:
                down = tap(-1, e, col - 1)
            else:
                down = jnp.where(upper, pltpu.roll(tap(-1, e, 3), 32, 1), 0.0)
            s.append(tap(0, e, col) + up + down)
        out.append(
            s[1]
            + jnp.where(right, pltpu.roll(s[2], 127, 1), 0.0)
            + jnp.where(left, pltpu.roll(s[0], 1, 1), 0.0)
        )
    return jnp.concatenate(out, 1)


def patches(x):
    lane = lane_index()
    q = lane % 32
    lower, upper, right, left = lane < 96, lane >= 32, q < 31, q > 0
    mid = columns(x)
    base = {
        0: mid,
        1: [jnp.where(right, pltpu.roll(c, 127, 1), 0.0) for c in mid],
        -1: [jnp.where(left, pltpu.roll(c, 1, 1), 0.0) for c in mid],
    }
    hi, lo = [], []
    for a in (-1, 0, 1):
        for e in (-1, 0, 1):
            c = base[e]
            if a == 1:
                c = c[1:] + [jnp.where(lower, pltpu.roll(c[0], 96, 1), 0.0)]
            elif a == -1:
                c = [jnp.where(upper, pltpu.roll(c[3], 32, 1), 0.0)] + c[:3]
            h, l = split(jnp.concatenate(c, 1))
            hi.append(h)
            lo.append(l)
    return jnp.concatenate(hi, 0), jnp.concatenate(lo, 0)


def dot_t(a, b):
    return lax.dot_general(a, b, (((1,), (1,)), ((), ())), preferred_element_type=F32)


def correlate(term, x):
    t_hi, t_lo = split(term)
    p_hi, p_lo = patches(x)
    return dot_t(t_hi, p_hi) + dot_t(t_hi, p_lo) + dot_t(t_lo, p_hi)


def as_column(row):
    r = lax.broadcasted_iota(jnp.int32, (CH, CH), 0)
    c = lax.broadcasted_iota(jnp.int32, (CH, CH), 1)
    spread = jnp.broadcast_to(row, (CH, CH))
    return jnp.sum(jnp.where(r == c, spread, 0.0), axis=1, keepdims=True)


def place():
    layer, image = lax.axis_index("layer"), lax.axis_index("dp")
    core = image % 2
    return layer // RING, layer % RING, 2 + 3 * core, core


def start_all(copies):
    for copy in copies:
        copy.start()
    return copies


def wait_all(copies):
    for copy in copies:
        copy.wait()


def field(*lead):
    return jax.ShapeDtypeStruct((*lead, CH, CELLS), F32)


def lhs_shape(*lead):
    return jax.ShapeDtypeStruct((*lead, 9 * CH, 3 * CH), BF16)


def vmem(shape):
    return pltpu.VMEM(shape.shape, shape.dtype)


def relax_kernel(c_hbm, a_hbm, w_hbm, b_hbm, one_ref, two_ref, c_ref, a_ref, w_ref, b_ref, sems):
    copies = start_all(
        [
            pltpu.make_async_copy(source, target, sems.at[i])
            for i, (source, target) in enumerate(
                [(b_hbm, b_ref), (w_hbm, w_ref), (c_hbm, c_ref), (a_hbm, a_ref)]
            )
        ]
    )
    wait_all(copies[:3])
    c = swap(c_ref[...])
    w0, w1 = w_ref[0], w_ref[1]
    b0, b1 = as_column(b_ref[0:1]), as_column(b_ref[1:2])
    t0 = jnp.tanh(conv(lhs_forward(w0), c, 1) + b0)
    t1 = jnp.tanh(conv(lhs_forward(w1), c + H * t0, 1) + b1)
    pad = WPAD - 576
    one_ref[:, 0:576] = w0
    one_ref[:, 576:WPAD] = jnp.broadcast_to(b0, (CH, pad))
    ring, spot, _, _ = place()
    keep = jnp.where((ring == 0) & (spot == 0), 1.0, 0.0)
    one_ref[:, WPAD:BLK] = jnp.where(keep > 0.0, c + H * t0 + H * t1, H * (t1 - t0))
    two_ref[:, 0:576] = w1
    two_ref[:, 576:WPAD] = jnp.broadcast_to(b1, (CH, pad))
    wait_all(copies[3:])
    two_ref[:, WPAD:BLK] = swap(a_ref[...])


def relax(c, a, w, b):
    shape = jax.ShapeDtypeStruct((CH, BLK), F32)
    return pl.pallas_call(
        relax_kernel,
        out_shape=(shape, shape),
        in_specs=[HBM] * 4,
        scratch_shapes=[
            pltpu.VMEM(c.shape, F32),
            pltpu.VMEM(a.shape, F32),
            pltpu.VMEM(w.shape, F32),
            pltpu.VMEM(b.shape, F32),
            pltpu.SemaphoreType.DMA((4,)),
        ],
        compiler_params=pltpu.CompilerParams(vmem_limit_bytes=63 << 20),
        name="relax",
    )(c, a, w, b)


MATRIX = pl.ds(0, WPAD)
REST = pl.ds(CELLS, WPAD)
BIAS = WPAD - 576


def slots(refs, target, sems, lead, part=None):
    if part is not None:
        refs = [ref.at[:, part] for ref in refs]
    copies = []
    for k, ref in enumerate(refs):
        j = (lead + k) % RING
        copies.append(pltpu.make_async_copy(ref, target.at[j], sems.at[j]))
    return copies


HALF = RING // 2


def half(array, i):
    return array.at[pl.ds(HALF * i, HALF)]


def half_out(vt, vt_ref, sems, part):
    return start_all(
        [
            pltpu.make_async_copy(half(vt.at[i], part), half(vt_ref.at[i], part), sems.at[i, part])
            for i in (0, 1)
        ]
    )


def first_kernel(*refs):
    one_refs = refs[:RING]
    vt_ref, out_ref, tau, even, vt, lhs, tau_sems, even_sems, sems = refs[RING:]
    ring, spot, lead, _ = place()

    @pl.when((ring == 0) & (spot == lead))
    def _():
        copies = slots(one_refs, even, even_sems, lead, MATRIX)
        copies += slots(one_refs, tau, tau_sems, lead, REST)
        wait_all(start_all(copies))

        def prepare(j, carry):
            lhs[j] = lhs_forward(even[j][:, 0:576])
            return carry

        lax.fori_loop(1, RING, prepare, 0)

        def step(j, v):
            now = jnp.tanh(conv(lhs[j], v, 1) + tau[j][:, BIAS : BIAS + 1])
            vt[0, j] = v
            vt[1, j] = now
            return v + 2 * H * now + tau[j][:, WPAD - CELLS :]

        v = lax.fori_loop(1, HALF, step, tau[0][:, WPAD - CELLS :])
        copies = half_out(vt, vt_ref, sems, 0)
        out_ref[...] = lax.fori_loop(HALF, RING, step, v)
        wait_all(copies + half_out(vt, vt_ref, sems, 1))


def first_chain(ones):
    return pl.pallas_call(
        first_kernel,
        out_shape=(field(2, RING), field()),
        in_specs=[ANY] * RING,
        out_specs=(ANY, VMEM),
        scratch_shapes=[
            pltpu.VMEM((RING, CH, WPAD), F32),
            pltpu.VMEM((RING, CH, WPAD), F32),
            vmem(field(2, RING)),
            vmem(lhs_shape(RING)),
            pltpu.SemaphoreType.DMA((RING,)),
            pltpu.SemaphoreType.DMA((RING,)),
            pltpu.SemaphoreType.DMA((2, 2)),
        ],
        compiler_params=PARAMS,
        name="chain_0",
    )(*ones)


def prepare_kernel(*refs):
    block_refs, outs = refs[:RING], refs[RING : RING + 2]
    w, ahead, behind, sems, out_sems = refs[RING + 2 :]
    _, spot, lead, _ = place()

    @pl.when(spot == lead)
    def _():
        wait_all(start_all(slots(block_refs, w, sems, lead, MATRIX)))

        def step(j, carry):
            ahead[j] = lhs_forward(w[j][:, 0:576])
            behind[j] = lhs_backward(w[j][:, 0:576])
            return carry

        lax.fori_loop(0, RING, step, 0)
        wait_all(
            start_all(
                [
                    pltpu.make_async_copy(ahead, outs[0], out_sems.at[0]),
                    pltpu.make_async_copy(behind, outs[1], out_sems.at[1]),
                ]
            )
        )


def prepare(blocks, name):
    return pl.pallas_call(
        prepare_kernel,
        out_shape=(lhs_shape(RING), lhs_shape(RING)),
        in_specs=[ANY] * RING,
        out_specs=(ANY, ANY),
        scratch_shapes=[
            pltpu.VMEM((RING, CH, WPAD), F32),
            vmem(lhs_shape(RING)),
            vmem(lhs_shape(RING)),
            pltpu.SemaphoreType.DMA((RING,)),
            pltpu.SemaphoreType.DMA((2,)),
        ],
        compiler_params=PARAMS,
        cost_estimate=pl.CostEstimate(flops=0, bytes_accessed=20 << 20, transcendentals=0),
        name=name,
    )(*blocks)


def chain_kernel(stage, *refs):
    tau_refs, ahead_ref, v_ref = refs[:RING], refs[RING], refs[RING + 1]
    vt_ref, out_ref, tau, vt, ahead, tau_sems, ahead_sems, sems = refs[-8:]
    ring, spot, lead, _ = place()

    @pl.when((ring == stage) & (spot == lead))
    def _():
        copies = start_all(slots(tau_refs, tau, tau_sems, lead, REST))
        halves = start_all(
            [
                pltpu.make_async_copy(half(ahead_ref, i), half(ahead, i), ahead_sems.at[i])
                for i in (0, 1)
            ]
        )
        wait_all(copies + halves[:1])

        def step(j, v):
            now = jnp.tanh(conv(ahead[j], v, 1) + tau[j][:, BIAS : BIAS + 1])
            vt[0, j] = v
            vt[1, j] = now
            return v + 2 * H * now + tau[j][:, WPAD - CELLS :]

        v = lax.fori_loop(0, HALF, step, v_ref[...], unroll=2)
        wait_all(halves[1:])
        copies = half_out(vt, vt_ref, sems, 0)
        out_ref[...] = lax.fori_loop(HALF, RING, step, v, unroll=2)
        wait_all(copies + half_out(vt, vt_ref, sems, 1))


def chain(stage, taus, ahead, v, vt):
    args = [*taus, ahead, v]
    return pl.pallas_call(
        lambda *refs: chain_kernel(stage, *refs),
        out_shape=(field(2, RING), field()),
        in_specs=[ANY] * (RING + 1) + [VMEM, ANY],
        out_specs=(ANY, VMEM),
        scratch_shapes=[
            pltpu.VMEM((RING, CH, WPAD), F32),
            vmem(field(2, RING)),
            vmem(lhs_shape(RING)),
            pltpu.SemaphoreType.DMA((RING,)),
            pltpu.SemaphoreType.DMA((2,)),
            pltpu.SemaphoreType.DMA((2, 2)),
        ],
        input_output_aliases={len(args): 0},
        compiler_params=PARAMS,
        name=f"chain_{stage}",
    )(*args, vt)


def correction(ahead, behind, v, t0, b1, a):
    t1 = jnp.tanh(conv(ahead, v + H * t0, 1) + b1)
    shift = H * conv(behind, (1.0 - t1 * t1) * a, -1)
    s0 = 1.0 - t0 * t0
    return shift, s0 * (H * (shift - a)), (2 * H) * s0


def back_step(behind, mu, shift, part, slope):
    return mu + shift + conv(behind, slope * mu + part, -1)


def middle_kernel(last, *refs):
    two_refs, (vt_ref, ahead_ref, behind_ref) = refs[:RING], refs[RING : RING + 3]
    outs = refs[-(RING + 3 + 7) : -7]
    two, vt, ahead, behind, out, two_sems, sems = refs[-7:]
    ring, spot, lead, _ = place()

    @pl.when((spot == lead) & (ring < last))
    def _():
        copies = start_all(slots(two_refs, two, two_sems, lead))
        copies += start_all(
            [
                pltpu.make_async_copy(vt_ref, vt, sems.at[0]),
                pltpu.make_async_copy(ahead_ref, ahead, sems.at[1]),
                pltpu.make_async_copy(behind_ref, behind, sems.at[2]),
            ]
        )
        wait_all(copies)
        copies = start_all(
            [
                pltpu.make_async_copy(vt.at[0, (lead + k) % RING], outs[k], two_sems.at[k])
                for k in range(RING)
            ]
        )

        def step(j, carry):
            b1, a = two[j][:, 576:577], two[j][:, WPAD:BLK]
            got = correction(ahead[j], behind[j], vt[0, j], vt[1, j], b1, a)
            for i in range(3):
                out[i, j] = got[i]
            return carry

        lax.fori_loop(0, RING, step, 0, unroll=2)
        copies += start_all(
            [pltpu.make_async_copy(out.at[i], outs[RING + i], sems.at[i]) for i in range(3)]
        )
        wait_all(copies)


def middle(last, twos, vt, ahead, behind, vs):
    args = [*twos, vt, ahead, behind]
    out = pl.pallas_call(
        lambda *refs: middle_kernel(last, *refs),
        out_shape=(field(),) * RING + (field(RING),) * 3,
        in_specs=[ANY] * (2 * RING + 3),
        out_specs=(ANY,) * (RING + 3),
        scratch_shapes=[
            pltpu.VMEM((RING, CH, BLK), F32),
            vmem(field(2, RING)),
            vmem(lhs_shape(RING)),
            vmem(lhs_shape(RING)),
            vmem(field(3, RING)),
            pltpu.SemaphoreType.DMA((RING,)),
            pltpu.SemaphoreType.DMA((3,)),
        ],
        input_output_aliases={len(args) + k: k for k in range(RING)},
        compiler_params=PARAMS,
        name="middle",
    )(*args, *vs)
    return out[:RING], out[RING:]


def turn_kernel(stage, *refs):
    tau_refs, two_refs = refs[:RING], refs[RING : 2 * RING]
    lhs_refs, v_ref = refs[2 * RING : 2 * RING + 4], refs[2 * RING + 4]
    v_refs = refs[2 * RING + 5 : 3 * RING + 5]
    mu_refs = refs[3 * RING + 5 : 4 * RING + 5]
    out_ref, tau, two, vs, t, mus, lhs, out, sems, lhs_sems = refs[4 * RING + 5 :]
    ring, spot, lead, _ = place()

    @pl.when((ring == stage) & (spot == lead))
    def _():
        copies = start_all(slots(tau_refs, tau, sems.at[0], lead, REST))
        matrices = [
            pltpu.make_async_copy(lhs_refs[i], lhs.at[i], lhs_sems.at[i]) for i in range(4)
        ]
        start_all(matrices[:1])
        block_copies = start_all(slots(two_refs, two, sems.at[1], lead))
        start_all(matrices[2:] + matrices[1:2])
        wait_all(copies + matrices[:1])

        def ahead_step(j, v):
            now = jnp.tanh(conv(lhs[0, j], v, 1) + tau[j][:, BIAS : BIAS + 1])
            vs[j] = v
            t[j] = now
            return v + 2 * H * now + tau[j][:, WPAD - CELLS :]

        def correct(j, carry):
            b1, a = two[j][:, 576:577], two[j][:, WPAD:BLK]
            got = correction(lhs[2, j], lhs[3, j], vs[j], t[j], b1, a)
            for i in range(3):
                out[i, j] = got[i]
            return carry

        lax.fori_loop(0, RING, ahead_step, v_ref[...], unroll=2)
        copies = start_all(
            [
                pltpu.make_async_copy(vs.at[(lead + k) % RING], v_refs[k], sems.at[0, k])
                for k in range(RING)
            ]
        )
        wait_all(block_copies + matrices[2:])
        lax.fori_loop(0, RING, correct, 0, unroll=2)
        wait_all(matrices[1:2])

        def back(k, mu):
            j = RING - 1 - k
            mus[j] = mu
            return back_step(lhs[1, j], mu, out[0, j], out[1, j], out[2, j])

        out_ref[...] = lax.fori_loop(0, RING, back, two[RING - 1][:, WPAD:BLK], unroll=2)
        copies += start_all(
            [
                pltpu.make_async_copy(mus.at[(lead + k) % RING], mu_refs[k], sems.at[1, k])
                for k in range(RING)
            ]
        )
        wait_all(copies)


def turn(stage, taus, twos, lhs, v):
    out = pl.pallas_call(
        lambda *refs: turn_kernel(stage, *refs),
        out_shape=(field(),) * (2 * RING + 1),
        in_specs=[ANY] * (2 * RING + 4) + [VMEM],
        out_specs=(ANY,) * (2 * RING) + (VMEM,),
        scratch_shapes=[
            pltpu.VMEM((RING, CH, WPAD), F32),
            pltpu.VMEM((RING, CH, BLK), F32),
            vmem(field(RING)),
            vmem(field(RING)),
            vmem(field(RING)),
            vmem(lhs_shape(4, RING)),
            vmem(field(3, RING)),
            pltpu.SemaphoreType.DMA((2, RING)),
            pltpu.SemaphoreType.DMA((4,)),
        ],
        compiler_params=PARAMS,
        name="turn",
    )(*taus, *twos, *lhs, v)
    return out[:RING], out[RING : 2 * RING], out[2 * RING]


def back_kernel(stage, *refs):
    part_refs, behind_ref, mu_ref = refs[:3], refs[3], refs[4]
    outs = refs[-(RING + 1 + 5) : -5]
    parts, behind, mus, sems, out_sems = refs[-5:]
    ring, spot, lead, _ = place()

    @pl.when((ring == stage) & (spot == lead))
    def _():
        copies = [pltpu.make_async_copy(part_refs[i], parts.at[i], sems.at[i]) for i in range(3)]
        copies.append(pltpu.make_async_copy(behind_ref, behind, sems.at[3]))
        wait_all(start_all(copies))

        def step(k, mu):
            j = RING - 1 - k
            mus[j] = mu
            return back_step(behind[j], mu, parts[0, j], parts[1, j], parts[2, j])

        if stage == 0:
            end = lax.fori_loop(0, RING - 1, step, mu_ref[...])
            mus[0] = end
        else:
            end = lax.fori_loop(0, RING, step, mu_ref[...], unroll=2)
        outs[RING][...] = end
        wait_all(
            start_all(
                [
                    pltpu.make_async_copy(mus.at[(lead + k) % RING], outs[k], out_sems.at[k])
                    for k in range(RING)
                ]
            )
        )


def back_chain(stage, parts, behind, mu, mus):
    args = [*parts, behind, mu]
    aliases = {len(args) + k: k for k in range(RING)}
    out = pl.pallas_call(
        lambda *refs: back_kernel(stage, *refs),
        out_shape=(field(),) * (RING + 1),
        in_specs=[ANY] * 4 + [VMEM] + [ANY] * RING,
        out_specs=(ANY,) * RING + (VMEM,),
        scratch_shapes=[
            vmem(field(3, RING)),
            vmem(lhs_shape(RING)),
            vmem(field(RING)),
            pltpu.SemaphoreType.DMA((4,)),
            pltpu.SemaphoreType.DMA((RING,)),
        ],
        input_output_aliases=aliases,
        compiler_params=PARAMS,
        name=f"back_{stage}",
    )(*args, *mus)
    return out[:RING], out[RING]


def fetch(refs, target, sem):
    _, spot, lead, _ = place()
    step = (spot + RING - lead) % RING
    for k in range(RING):

        @pl.when(step == k)
        def _():
            copy = pltpu.make_async_copy(refs[k], target, sem)
            copy.start()
            copy.wait()


def early_kernel(*refs):
    one_ref, two_ref, c_ref, refs = refs[0], refs[1], refs[2], refs[3:]
    v_refs = refs[:RING]
    states_ref, keep_ref, lhs_ref, v_ref, sem = refs[RING:]
    fetch(v_refs, v_ref, sem)
    ring, spot, _, _ = place()

    @pl.when((ring == 0) & (spot == 0))
    def _():
        v_ref[...] = swap(c_ref[...])

    v = v_ref[...]
    w0, w1 = one_ref[:, 0:576], two_ref[:, 0:576]
    t0 = jnp.tanh(conv(lhs_forward(w0), v, 1) + one_ref[:, 576:577])
    m = v + H * t0
    b1, a = two_ref[:, 576:577], two_ref[:, WPAD:BLK]
    t1 = jnp.tanh(conv(lhs_forward(w1), m, 1) + b1)
    s1 = 1.0 - t1 * t1
    s0 = 1.0 - t0 * t0
    lhs_ref[0] = lhs_backward(w0)
    behind = lhs_backward(w1)
    lhs_ref[1] = behind
    shift = H * conv(behind, s1 * a, -1)
    states_ref[0] = swap(m)
    slot = one_ref[:, WPAD:BLK]
    keep = jnp.where((ring == 0) & (spot == 0), 1.0, 0.0)
    states_ref[1] = swap(jnp.where(keep > 0.0, slot, v + 2 * H * t0 + slot))
    keep_ref[0] = v
    keep_ref[1] = m
    keep_ref[2] = s0
    keep_ref[3] = s1
    keep_ref[4] = shift
    keep_ref[5] = s0 * (H * (shift - a))


def early(one, two, c, vs):
    return pl.pallas_call(
        early_kernel,
        out_shape=(field(2), field(6), lhs_shape(2)),
        in_specs=[VMEM] * 3 + [ANY] * RING,
        scratch_shapes=[vmem(field()), pltpu.SemaphoreType.DMA],
        compiler_params=PARAMS,
        name="early",
    )(one, two, c, *vs)


def late_kernel(*refs):
    keep_ref, lhs_ref = refs[:2]
    mu_refs = refs[2 : 2 + RING]
    adjoints_ref, mine_ref, other_ref, mu_scratch, sem = refs[2 + RING :]
    fetch(mu_refs, mu_scratch, sem)
    mu = mu_scratch[...]
    s0 = keep_ref[2]
    odd_product = keep_ref[3] * mu
    odd = mu + H * conv(lhs_ref[1], odd_product, -1)
    even_term = (H / 8) * (s0 * odd)
    odd_term = (H / 8) * odd_product
    odd_grad = correlate(odd_term, keep_ref[1])
    even_grad = correlate(even_term, keep_ref[0])
    even = back_step(lhs_ref[0], mu, keep_ref[4], keep_ref[5], (2 * H) * s0)
    adjoints_ref[0] = swap(even)
    adjoints_ref[1] = swap(odd)
    pad = (CH, WPAD - 576)
    even_bias = jnp.broadcast_to(jnp.sum(even_term, axis=1, keepdims=True), pad)
    odd_bias = jnp.broadcast_to(jnp.sum(odd_term, axis=1, keepdims=True), pad)

    def write(ref, grad, bias):
        ref[:, 0:576] = grad
        ref[:, 576:WPAD] = bias

    core = place()[3]

    @pl.when(core == 0)
    def _():
        write(mine_ref, even_grad, even_bias)
        write(other_ref, odd_grad, odd_bias)

    @pl.when(core == 1)
    def _():
        write(mine_ref, odd_grad, odd_bias)
        write(other_ref, even_grad, even_bias)


def late(keep, lhs, mus):
    grad = jax.ShapeDtypeStruct((CH, WPAD), F32)
    return pl.pallas_call(
        late_kernel,
        out_shape=(field(2), grad, grad),
        in_specs=[VMEM] * 2 + [ANY] * RING,
        scratch_shapes=[vmem(field()), pltpu.SemaphoreType.DMA],
        compiler_params=PARAMS,
        name="late",
    )(keep, lhs, *mus)


def finish_kernel(mine_ref, other_ref, grad_ref, bias_ref):
    core = place()[3]
    r = lax.broadcasted_iota(jnp.int32, (CH, CH), 0)
    c = lax.broadcasted_iota(jnp.int32, (CH, CH), 1)

    def write(slot, ref):
        grad_ref[slot] = ref[:, 0:576]
        spread = jnp.broadcast_to(ref[:, 576:577], (CH, CH))
        bias_ref[slot : slot + 1] = jnp.sum(jnp.where(r == c, spread, 0.0), axis=0, keepdims=True)

    @pl.when(core == 0)
    def _():
        write(0, mine_ref)
        write(1, other_ref)

    @pl.when(core == 1)
    def _():
        write(1, mine_ref)
        write(0, other_ref)


def finish(mine, other):
    return pl.pallas_call(
        finish_kernel,
        out_shape=(
            jax.ShapeDtypeStruct((2, CH, 576), F32),
            jax.ShapeDtypeStruct((2, CH), F32),
        ),
        compiler_params=PARAMS,
        name="finish",
    )(mine, other)


def tie(*values):
    return lax.optimization_barrier(values)


NEAR = (1, 7, 2, 6, 3, 5, 4)
FAR = NEAR[::-1]
EARLY = FAR[:0]
PAIRS = ((6, 3), (2, 4), (7, 5), (1, None))


def body(coarse_guess, adjoint_guess, weights, biases):
    images = lax.axis_size("dp")
    groups = lax.axis_size("layer") // RING
    last = groups - 1

    def device(x, z, d):
        return (RING * x + z % RING) * images + d

    def lead(d):
        return 2 + 3 * (d % 2)

    everyone = [(x, d) for x in range(groups) for d in range(images)]

    def gather(value, k):
        pairs = [(device(x, lead(d) + k, d), device(x, lead(d), d)) for x, d in everyone]
        return lax.ppermute(value, AXES, pairs)

    def gather_pair(value, direct, helped):
        pairs = [(device(x, lead(d) + direct, d), device(x, lead(d), d)) for x, d in everyone]
        if helped is not None:
            pairs += [
                (device(x, lead(d) + helped, d), device(x, lead(d), d ^ 1)) for x, d in everyone
            ]
        return lax.ppermute(value, AXES, pairs)

    def hand_over(value):
        pairs = [(device(x, lead(d), d ^ 1), device(x, lead(d), d)) for x, d in everyone]
        return lax.ppermute(value, AXES, pairs)

    def scatter(value, k):
        pairs = [(device(x, lead(d), d), device(x, lead(d) + k, d)) for x, d in everyone]
        return lax.ppermute(value, AXES, pairs)

    def hop(value, source, target):
        pairs = [
            (device(source, lead(d), d), device(target, lead(d), d)) for d in range(images)
        ]
        return lax.ppermute(value, AXES, pairs)

    c, a = coarse_guess[0, 0], adjoint_guess[0, 0]
    one, two = relax(c, a, weights, biases)
    ones, twos = [one] + [None] * (RING - 1), [two] + [None] * (RING - 1)
    for direct, helped in PAIRS:
        ones[direct] = gather_pair(one, direct, helped)
        if helped is not None:
            ones[helped] = hand_over(ones[direct])
    vt, end = first_chain(ones)
    v = hop(end, 0, 1)
    ahead0, behind0 = prepare([tie(end, one)[1]] + ones[1:], "prepare")
    for k in NEAR:
        twos[k] = gather(two, k)
    for stage in range(1, last):
        vt, end = chain(stage, ones, ahead0, v, vt)
        v = hop(end, stage, stage + 1)
    ahead1, behind1 = prepare(twos, "prepare2")
    vs, mus, end = turn(last, ones, twos, [ahead0, behind0, ahead1, behind1], v)
    mu = hop(end, last, last - 1)
    vs, parts = middle(last, twos, vt, ahead1, behind1, vs)
    own_v = [vs[0]] + [None] * (RING - 1)
    for stage in range(last - 1, -1, -1):
        if stage == last - 1:
            chunk, gate = FAR[:4], parts[0]
        elif stage == last - 2:
            chunk, gate = FAR[4:], end
        else:
            chunk = ()
        for k in chunk:
            own_v[k] = scatter(tie(gate, vs[k])[1], k)
        if stage == last - 1:
            mu, *parts = tie(mu, *parts)
        if stage == 0:
            states, keep, lhs = early(one, two, c, own_v)
            mu, keep = tie(mu, keep)
        mus, end = back_chain(stage, parts, behind0, mu, mus)
        if stage == last - 1:
            got = tie(end, *[own_v[k] for k in chunk])
            end = got[0]
            for k, value in zip(chunk, got[1:]):
                own_v[k] = value
        if stage > 0:
            mu = hop(end, stage, stage - 1)
    own_mu = [mus[0]] + [None] * (RING - 1)
    for k in FAR:
        own_mu[k] = scatter(mus[k], k)
    adjoints, mine, other = late(keep, lhs, own_mu)
    mine = mine + lax.ppermute(other, "dp", [(i, i ^ 1) for i in range(images)])
    for flip in (2, 6):
        mine = mine + lax.ppermute(mine, "dp", [(i, i ^ flip) for i in range(images)])
    other = lax.ppermute(mine, "dp", [(i, i ^ 1) for i in range(images)])
    grad, bias = finish(mine, other)
    return states[:, None], adjoints[:, None], grad, bias


def solution(mesh):
    return jax.shard_map(
        body,
        mesh=mesh,
        in_specs=(
            P("layer", "dp", None, None),
            P("layer", "dp", None, None),
            P("layer", None, None),
            P("layer", None),
        ),
        out_specs=(
            P("layer", "dp", None, None),
            P("layer", "dp", None, None),
            P("layer", None, None),
            P("layer", None),
        ),
        check_vma=False,
    )
```

```python
import jax
import jax.numpy as jnp
from jax import lax
from jax.experimental import pallas as pl
from jax.experimental.pallas import tpu as pltpu
from jax.sharding import PartitionSpec as P

F32 = jnp.float32
BF16 = jnp.bfloat16
H = 0.125
CH, CELLS = 64, 512
WPAD = 640
BLK = WPAD + CELLS
RING = 8
AXES = ("layer", "dp")
ANY = pl.BlockSpec(memory_space=pl.ANY)
HBM = pl.BlockSpec(memory_space=pltpu.HBM)
VMEM = pl.BlockSpec(memory_space=pltpu.VMEM)
PARAMS = pltpu.CompilerParams(vmem_limit_bytes=28 << 20)


def split(x):
    hi = x.astype(BF16)
    return hi, (x - hi.astype(F32)).astype(BF16)


def lane_index():
    return lax.broadcasted_iota(jnp.int32, (CH, 128), 1)


def columns(x):
    return [x[:, 128 * a : 128 * (a + 1)] for a in range(4)]


def swap(x):
    parts, lane, out = columns(x), lane_index(), []
    for a in range(4):
        acc = None
        for b in range(4):
            shift = ((b - a) * 32) % 128
            part = parts[b] if shift == 0 else pltpu.roll(parts[b], shift, 1)
            acc = part if acc is None else jnp.where(lane >= 32 * b, part, acc)
        out.append(acc)
    return jnp.concatenate(out, 1)


def lhs_forward(w):
    hi = w.astype(BF16).astype(F32)
    lo = w - hi
    rows = []
    for t in range(9):
        a, b = hi[:, 64 * t : 64 * t + 64], lo[:, 64 * t : 64 * t + 64]
        rows.append(jnp.concatenate([a, a, b], 1).astype(BF16))
    return jnp.concatenate(rows, 0)


def lhs_backward(w):
    wt = w.T
    hi = wt.astype(BF16).astype(F32)
    lo = wt - hi
    return jnp.concatenate([hi, hi, lo], 1).astype(BF16)


def conv(lhs, x, sign):
    hi, lo = split(x)
    z = jnp.dot(lhs, jnp.concatenate([hi, lo, hi], 0), preferred_element_type=F32)
    lane = lane_index()
    q = lane % 32
    lower, upper, right, left = lane < 96, lane >= 32, q < 31, q > 0

    def tap(a, e, col):
        t = 3 * (sign * a + 1) + (sign * e + 1)
        return z[64 * t : 64 * t + 64, 128 * col : 128 * col + 128]

    out = []
    for col in range(4):
        s = []
        for e in (-1, 0, 1):
            if col < 3:
                up = tap(1, e, col + 1)
            else:
                up = jnp.where(lower, pltpu.roll(tap(1, e, 0), 96, 1), 0.0)
            if col > 0:
                down = tap(-1, e, col - 1)
            else:
                down = jnp.where(upper, pltpu.roll(tap(-1, e, 3), 32, 1), 0.0)
            s.append(tap(0, e, col) + up + down)
        out.append(
            s[1]
            + jnp.where(right, pltpu.roll(s[2], 127, 1), 0.0)
            + jnp.where(left, pltpu.roll(s[0], 1, 1), 0.0)
        )
    return jnp.concatenate(out, 1)


def patches(x):
    lane = lane_index()
    q = lane % 32
    lower, upper, right, left = lane < 96, lane >= 32, q < 31, q > 0
    mid = columns(x)
    base = {
        0: mid,
        1: [jnp.where(right, pltpu.roll(c, 127, 1), 0.0) for c in mid],
        -1: [jnp.where(left, pltpu.roll(c, 1, 1), 0.0) for c in mid],
    }
    hi, lo = [], []
    for a in (-1, 0, 1):
        for e in (-1, 0, 1):
            c = base[e]
            if a == 1:
                c = c[1:] + [jnp.where(lower, pltpu.roll(c[0], 96, 1), 0.0)]
            elif a == -1:
                c = [jnp.where(upper, pltpu.roll(c[3], 32, 1), 0.0)] + c[:3]
            h, l = split(jnp.concatenate(c, 1))
            hi.append(h)
            lo.append(l)
    return jnp.concatenate(hi, 0), jnp.concatenate(lo, 0)


def dot_t(a, b):
    return lax.dot_general(a, b, (((1,), (1,)), ((), ())), preferred_element_type=F32)


def correlate(term, x):
    t_hi, t_lo = split(term)
    p_hi, p_lo = patches(x)
    return dot_t(t_hi, p_hi) + dot_t(t_hi, p_lo) + dot_t(t_lo, p_hi)


def as_column(row):
    r = lax.broadcasted_iota(jnp.int32, (CH, CH), 0)
    c = lax.broadcasted_iota(jnp.int32, (CH, CH), 1)
    spread = jnp.broadcast_to(row, (CH, CH))
    return jnp.sum(jnp.where(r == c, spread, 0.0), axis=1, keepdims=True)


def place():
    layer, image = lax.axis_index("layer"), lax.axis_index("dp")
    core = image % 2
    return layer // RING, layer % RING, 2 + 3 * core, core


def start_all(copies):
    for copy in copies:
        copy.start()
    return copies


def wait_all(copies):
    for copy in copies:
        copy.wait()


def field(*lead):
    return jax.ShapeDtypeStruct((*lead, CH, CELLS), F32)


def lhs_shape(*lead):
    return jax.ShapeDtypeStruct((*lead, 9 * CH, 3 * CH), BF16)


def vmem(shape):
    return pltpu.VMEM(shape.shape, shape.dtype)


def relax_kernel(c_hbm, a_hbm, w_hbm, b_hbm, one_ref, two_ref, c_ref, a_ref, w_ref, b_ref, sems):
    copies = start_all(
        [
            pltpu.make_async_copy(source, target, sems.at[i])
            for i, (source, target) in enumerate(
                [(b_hbm, b_ref), (w_hbm, w_ref), (c_hbm, c_ref), (a_hbm, a_ref)]
            )
        ]
    )
    wait_all(copies[:3])
    c = swap(c_ref[...])
    w0, w1 = w_ref[0], w_ref[1]
    b0, b1 = as_column(b_ref[0:1]), as_column(b_ref[1:2])
    t0 = jnp.tanh(conv(lhs_forward(w0), c, 1) + b0)
    t1 = jnp.tanh(conv(lhs_forward(w1), c + H * t0, 1) + b1)
    pad = WPAD - 576
    one_ref[:, 0:576] = w0
    one_ref[:, 576:WPAD] = jnp.broadcast_to(b0, (CH, pad))
    ring, spot, _, _ = place()
    keep = jnp.where((ring == 0) & (spot == 0), 1.0, 0.0)
    one_ref[:, WPAD:BLK] = jnp.where(keep > 0.0, c + H * t0 + H * t1, H * (t1 - t0))
    two_ref[:, 0:576] = w1
    two_ref[:, 576:WPAD] = jnp.broadcast_to(b1, (CH, pad))
    wait_all(copies[3:])
    two_ref[:, WPAD:BLK] = swap(a_ref[...])


def relax(c, a, w, b):
    shape = jax.ShapeDtypeStruct((CH, BLK), F32)
    return pl.pallas_call(
        relax_kernel,
        out_shape=(shape, shape),
        in_specs=[HBM] * 4,
        scratch_shapes=[
            pltpu.VMEM(c.shape, F32),
            pltpu.VMEM(a.shape, F32),
            pltpu.VMEM(w.shape, F32),
            pltpu.VMEM(b.shape, F32),
            pltpu.SemaphoreType.DMA((4,)),
        ],
        compiler_params=pltpu.CompilerParams(vmem_limit_bytes=63 << 20),
        name="relax",
    )(c, a, w, b)


MATRIX = pl.ds(0, WPAD)
REST = pl.ds(CELLS, WPAD)
BIAS = WPAD - 576


def slots(refs, target, sems, lead, part=None):
    if part is not None:
        refs = [ref.at[:, part] for ref in refs]
    copies = []
    for k, ref in enumerate(refs):
        j = (lead + k) % RING
        copies.append(pltpu.make_async_copy(ref, target.at[j], sems.at[j]))
    return copies


HALF = RING // 2


def half(array, i):
    return array.at[pl.ds(HALF * i, HALF)]


def half_out(vt, vt_ref, sems, part):
    return start_all(
        [
            pltpu.make_async_copy(half(vt.at[i], part), half(vt_ref.at[i], part), sems.at[i, part])
            for i in (0, 1)
        ]
    )


def first_kernel(*refs):
    one_refs = refs[:RING]
    vt_ref, out_ref, tau, even, vt, lhs, tau_sems, even_sems, sems = refs[RING:]
    ring, spot, lead, _ = place()

    @pl.when((ring == 0) & (spot == lead))
    def _():
        copies = slots(one_refs, even, even_sems, lead, MATRIX)
        copies += slots(one_refs, tau, tau_sems, lead, REST)
        wait_all(start_all(copies))

        def prepare(j, carry):
            lhs[j] = lhs_forward(even[j][:, 0:576])
            return carry

        lax.fori_loop(1, RING, prepare, 0)

        def step(j, v):
            now = jnp.tanh(conv(lhs[j], v, 1) + tau[j][:, BIAS : BIAS + 1])
            vt[0, j] = v
            vt[1, j] = now
            return v + 2 * H * now + tau[j][:, WPAD - CELLS :]

        v = lax.fori_loop(1, HALF, step, tau[0][:, WPAD - CELLS :])
        copies = half_out(vt, vt_ref, sems, 0)
        out_ref[...] = lax.fori_loop(HALF, RING, step, v, unroll=2)
        wait_all(copies + half_out(vt, vt_ref, sems, 1))


def first_chain(ones):
    return pl.pallas_call(
        first_kernel,
        out_shape=(field(2, RING), field()),
        in_specs=[ANY] * RING,
        out_specs=(ANY, VMEM),
        scratch_shapes=[
            pltpu.VMEM((RING, CH, WPAD), F32),
            pltpu.VMEM((RING, CH, WPAD), F32),
            vmem(field(2, RING)),
            vmem(lhs_shape(RING)),
            pltpu.SemaphoreType.DMA((RING,)),
            pltpu.SemaphoreType.DMA((RING,)),
            pltpu.SemaphoreType.DMA((2, 2)),
        ],
        compiler_params=PARAMS,
        name="chain_0",
    )(*ones)


def prepare_kernel(*refs):
    block_refs, outs = refs[:RING], refs[RING : RING + 2]
    w, ahead, behind, sems, out_sems = refs[RING + 2 :]
    _, spot, lead, _ = place()

    @pl.when(spot == lead)
    def _():
        wait_all(start_all(slots(block_refs, w, sems, lead, MATRIX)))

        def step(j, carry):
            ahead[j] = lhs_forward(w[j][:, 0:576])
            behind[j] = lhs_backward(w[j][:, 0:576])
            return carry

        lax.fori_loop(0, RING, step, 0)
        wait_all(
            start_all(
                [
                    pltpu.make_async_copy(ahead, outs[0], out_sems.at[0]),
                    pltpu.make_async_copy(behind, outs[1], out_sems.at[1]),
                ]
            )
        )


def prepare(blocks, name):
    return pl.pallas_call(
        prepare_kernel,
        out_shape=(lhs_shape(RING), lhs_shape(RING)),
        in_specs=[ANY] * RING,
        out_specs=(ANY, ANY),
        scratch_shapes=[
            pltpu.VMEM((RING, CH, WPAD), F32),
            vmem(lhs_shape(RING)),
            vmem(lhs_shape(RING)),
            pltpu.SemaphoreType.DMA((RING,)),
            pltpu.SemaphoreType.DMA((2,)),
        ],
        compiler_params=PARAMS,
        cost_estimate=pl.CostEstimate(flops=0, bytes_accessed=20 << 20, transcendentals=0),
        name=name,
    )(*blocks)


def chain_kernel(stage, *refs):
    tau_refs, ahead_ref, v_ref = refs[:RING], refs[RING], refs[RING + 1]
    vt_ref, out_ref, tau, vt, ahead, tau_sems, ahead_sems, sems = refs[-8:]
    ring, spot, lead, _ = place()

    @pl.when((ring == stage) & (spot == lead))
    def _():
        copies = start_all(slots(tau_refs, tau, tau_sems, lead, REST))
        halves = start_all(
            [
                pltpu.make_async_copy(half(ahead_ref, i), half(ahead, i), ahead_sems.at[i])
                for i in (0, 1)
            ]
        )
        wait_all(copies + halves[:1])

        def step(j, v):
            now = jnp.tanh(conv(ahead[j], v, 1) + tau[j][:, BIAS : BIAS + 1])
            vt[0, j] = v
            vt[1, j] = now
            return v + 2 * H * now + tau[j][:, WPAD - CELLS :]

        v = lax.fori_loop(0, HALF, step, v_ref[...], unroll=2)
        wait_all(halves[1:])
        copies = half_out(vt, vt_ref, sems, 0)
        out_ref[...] = lax.fori_loop(HALF, RING, step, v, unroll=2)
        wait_all(copies + half_out(vt, vt_ref, sems, 1))


def chain(stage, taus, ahead, v, vt):
    args = [*taus, ahead, v]
    return pl.pallas_call(
        lambda *refs: chain_kernel(stage, *refs),
        out_shape=(field(2, RING), field()),
        in_specs=[ANY] * (RING + 1) + [VMEM, ANY],
        out_specs=(ANY, VMEM),
        scratch_shapes=[
            pltpu.VMEM((RING, CH, WPAD), F32),
            vmem(field(2, RING)),
            vmem(lhs_shape(RING)),
            pltpu.SemaphoreType.DMA((RING,)),
            pltpu.SemaphoreType.DMA((2,)),
            pltpu.SemaphoreType.DMA((2, 2)),
        ],
        input_output_aliases={len(args): 0},
        compiler_params=PARAMS,
        name=f"chain_{stage}",
    )(*args, vt)


def correction(ahead, behind, v, t0, b1, a):
    t1 = jnp.tanh(conv(ahead, v + H * t0, 1) + b1)
    shift = H * conv(behind, (1.0 - t1 * t1) * a, -1)
    s0 = 1.0 - t0 * t0
    return shift, s0 * (H * (shift - a)), (2 * H) * s0


def back_step(behind, mu, shift, part, slope):
    return mu + shift + conv(behind, slope * mu + part, -1)


def middle_kernel(last, *refs):
    two_refs, (vt_ref, ahead_ref, behind_ref) = refs[:RING], refs[RING : RING + 3]
    outs = refs[-(RING + 3 + 7) : -7]
    two, vt, ahead, behind, out, two_sems, sems = refs[-7:]
    ring, spot, lead, _ = place()

    @pl.when((spot == lead) & (ring < last))
    def _():
        copies = start_all(slots(two_refs, two, two_sems, lead))
        copies += start_all(
            [
                pltpu.make_async_copy(vt_ref, vt, sems.at[0]),
                pltpu.make_async_copy(ahead_ref, ahead, sems.at[1]),
                pltpu.make_async_copy(behind_ref, behind, sems.at[2]),
            ]
        )
        wait_all(copies)
        copies = start_all(
            [
                pltpu.make_async_copy(vt.at[0, (lead + k) % RING], outs[k], two_sems.at[k])
                for k in range(RING)
            ]
        )

        def step(j, carry):
            b1, a = two[j][:, 576:577], two[j][:, WPAD:BLK]
            got = correction(ahead[j], behind[j], vt[0, j], vt[1, j], b1, a)
            for i in range(3):
                out[i, j] = got[i]
            return carry

        lax.fori_loop(0, RING, step, 0, unroll=2)
        copies += start_all(
            [pltpu.make_async_copy(out.at[i], outs[RING + i], sems.at[i]) for i in range(3)]
        )
        wait_all(copies)


def middle(last, twos, vt, ahead, behind, vs):
    args = [*twos, vt, ahead, behind]
    out = pl.pallas_call(
        lambda *refs: middle_kernel(last, *refs),
        out_shape=(field(),) * RING + (field(RING),) * 3,
        in_specs=[ANY] * (2 * RING + 3),
        out_specs=(ANY,) * (RING + 3),
        scratch_shapes=[
            pltpu.VMEM((RING, CH, BLK), F32),
            vmem(field(2, RING)),
            vmem(lhs_shape(RING)),
            vmem(lhs_shape(RING)),
            vmem(field(3, RING)),
            pltpu.SemaphoreType.DMA((RING,)),
            pltpu.SemaphoreType.DMA((3,)),
        ],
        input_output_aliases={len(args) + k: k for k in range(RING)},
        compiler_params=PARAMS,
        name="middle",
    )(*args, *vs)
    return out[:RING], out[RING:]


def turn_kernel(stage, *refs):
    tau_refs, two_refs = refs[:RING], refs[RING : 2 * RING]
    lhs_refs, v_ref = refs[2 * RING : 2 * RING + 4], refs[2 * RING + 4]
    v_refs = refs[2 * RING + 5 : 3 * RING + 5]
    mu_refs = refs[3 * RING + 5 : 4 * RING + 5]
    out_ref, tau, two, vs, t, mus, lhs, out, sems, lhs_sems = refs[4 * RING + 5 :]
    ring, spot, lead, _ = place()

    @pl.when((ring == stage) & (spot == lead))
    def _():
        copies = start_all(slots(tau_refs, tau, sems.at[0], lead, REST))
        matrices = [
            pltpu.make_async_copy(lhs_refs[i], lhs.at[i], lhs_sems.at[i]) for i in range(4)
        ]
        start_all(matrices[:1])
        block_copies = start_all(slots(two_refs, two, sems.at[1], lead))
        start_all(matrices[2:] + matrices[1:2])
        wait_all(copies + matrices[:1])

        def ahead_step(j, v):
            now = jnp.tanh(conv(lhs[0, j], v, 1) + tau[j][:, BIAS : BIAS + 1])
            vs[j] = v
            t[j] = now
            return v + 2 * H * now + tau[j][:, WPAD - CELLS :]

        def correct(j, carry):
            b1, a = two[j][:, 576:577], two[j][:, WPAD:BLK]
            got = correction(lhs[2, j], lhs[3, j], vs[j], t[j], b1, a)
            for i in range(3):
                out[i, j] = got[i]
            return carry

        lax.fori_loop(0, RING, ahead_step, v_ref[...], unroll=2)
        copies = start_all(
            [
                pltpu.make_async_copy(vs.at[(lead + k) % RING], v_refs[k], sems.at[0, k])
                for k in range(RING)
            ]
        )
        wait_all(block_copies + matrices[2:])
        lax.fori_loop(0, RING, correct, 0, unroll=2)
        wait_all(matrices[1:2])

        def back(k, mu):
            j = RING - 1 - k
            mus[j] = mu
            return back_step(lhs[1, j], mu, out[0, j], out[1, j], out[2, j])

        out_ref[...] = lax.fori_loop(0, RING, back, two[RING - 1][:, WPAD:BLK], unroll=2)
        copies += start_all(
            [
                pltpu.make_async_copy(mus.at[(lead + k) % RING], mu_refs[k], sems.at[1, k])
                for k in range(RING)
            ]
        )
        wait_all(copies)


def turn(stage, taus, twos, lhs, v):
    out = pl.pallas_call(
        lambda *refs: turn_kernel(stage, *refs),
        out_shape=(field(),) * (2 * RING + 1),
        in_specs=[ANY] * (2 * RING + 4) + [VMEM],
        out_specs=(ANY,) * (2 * RING) + (VMEM,),
        scratch_shapes=[
            pltpu.VMEM((RING, CH, WPAD), F32),
            pltpu.VMEM((RING, CH, BLK), F32),
            vmem(field(RING)),
            vmem(field(RING)),
            vmem(field(RING)),
            vmem(lhs_shape(4, RING)),
            vmem(field(3, RING)),
            pltpu.SemaphoreType.DMA((2, RING)),
            pltpu.SemaphoreType.DMA((4,)),
        ],
        compiler_params=PARAMS,
        name="turn",
    )(*taus, *twos, *lhs, v)
    return out[:RING], out[RING : 2 * RING], out[2 * RING]


def back_kernel(stage, *refs):
    part_refs, behind_ref, mu_ref = refs[:3], refs[3], refs[4]
    outs = refs[-(RING + 1 + 5) : -5]
    parts, behind, mus, sems, out_sems = refs[-5:]
    ring, spot, lead, _ = place()

    @pl.when((ring == stage) & (spot == lead))
    def _():
        copies = [pltpu.make_async_copy(part_refs[i], parts.at[i], sems.at[i]) for i in range(3)]
        copies.append(pltpu.make_async_copy(behind_ref, behind, sems.at[3]))
        wait_all(start_all(copies))

        def step(k, mu):
            j = RING - 1 - k
            mus[j] = mu
            return back_step(behind[j], mu, parts[0, j], parts[1, j], parts[2, j])

        if stage == 0:
            end = lax.fori_loop(0, RING - 2, step, mu_ref[...], unroll=2)
            end = step(RING - 2, end)
            mus[0] = end
        else:
            end = lax.fori_loop(0, RING, step, mu_ref[...], unroll=2)
        outs[RING][...] = end
        wait_all(
            start_all(
                [
                    pltpu.make_async_copy(mus.at[(lead + k) % RING], outs[k], out_sems.at[k])
                    for k in range(RING)
                ]
            )
        )


def back_chain(stage, parts, behind, mu, mus):
    args = [*parts, behind, mu]
    aliases = {len(args) + k: k for k in range(RING)}
    out = pl.pallas_call(
        lambda *refs: back_kernel(stage, *refs),
        out_shape=(field(),) * (RING + 1),
        in_specs=[ANY] * 4 + [VMEM] + [ANY] * RING,
        out_specs=(ANY,) * RING + (VMEM,),
        scratch_shapes=[
            vmem(field(3, RING)),
            vmem(lhs_shape(RING)),
            vmem(field(RING)),
            pltpu.SemaphoreType.DMA((4,)),
            pltpu.SemaphoreType.DMA((RING,)),
        ],
        input_output_aliases=aliases,
        compiler_params=PARAMS,
        name=f"back_{stage}",
    )(*args, *mus)
    return out[:RING], out[RING]


def fetch(refs, target, sem):
    _, spot, lead, _ = place()
    step = (spot + RING - lead) % RING
    for k in range(RING):

        @pl.when(step == k)
        def _():
            copy = pltpu.make_async_copy(refs[k], target, sem)
            copy.start()
            copy.wait()


def early_kernel(*refs):
    one_ref, two_ref, c_ref, refs = refs[0], refs[1], refs[2], refs[3:]
    v_refs = refs[:RING]
    states_ref, keep_ref, lhs_ref, v_ref, sem = refs[RING:]
    fetch(v_refs, v_ref, sem)
    ring, spot, _, _ = place()

    @pl.when((ring == 0) & (spot == 0))
    def _():
        v_ref[...] = swap(c_ref[...])

    v = v_ref[...]
    w0, w1 = one_ref[:, 0:576], two_ref[:, 0:576]
    t0 = jnp.tanh(conv(lhs_forward(w0), v, 1) + one_ref[:, 576:577])
    m = v + H * t0
    b1, a = two_ref[:, 576:577], two_ref[:, WPAD:BLK]
    t1 = jnp.tanh(conv(lhs_forward(w1), m, 1) + b1)
    s1 = 1.0 - t1 * t1
    s0 = 1.0 - t0 * t0
    lhs_ref[0] = lhs_backward(w0)
    behind = lhs_backward(w1)
    lhs_ref[1] = behind
    shift = H * conv(behind, s1 * a, -1)
    states_ref[0] = swap(m)
    slot = one_ref[:, WPAD:BLK]
    keep = jnp.where((ring == 0) & (spot == 0), 1.0, 0.0)
    states_ref[1] = swap(jnp.where(keep > 0.0, slot, v + 2 * H * t0 + slot))
    keep_ref[0] = v
    keep_ref[1] = m
    keep_ref[2] = s0
    keep_ref[3] = s1
    keep_ref[4] = shift
    keep_ref[5] = s0 * (H * (shift - a))


def early(one, two, c, vs):
    return pl.pallas_call(
        early_kernel,
        out_shape=(field(2), field(6), lhs_shape(2)),
        in_specs=[VMEM] * 3 + [ANY] * RING,
        scratch_shapes=[vmem(field()), pltpu.SemaphoreType.DMA],
        compiler_params=PARAMS,
        name="early",
    )(one, two, c, *vs)


def late_kernel(*refs):
    keep_ref, lhs_ref = refs[:2]
    mu_refs = refs[2 : 2 + RING]
    adjoints_ref, mine_ref, other_ref, mu_scratch, sem = refs[2 + RING :]
    fetch(mu_refs, mu_scratch, sem)
    mu = mu_scratch[...]
    s0 = keep_ref[2]
    odd_product = keep_ref[3] * mu
    odd = mu + H * conv(lhs_ref[1], odd_product, -1)
    even_term = (H / 8) * (s0 * odd)
    odd_term = (H / 8) * odd_product
    odd_grad = correlate(odd_term, keep_ref[1])
    even_grad = correlate(even_term, keep_ref[0])
    even = back_step(lhs_ref[0], mu, keep_ref[4], keep_ref[5], (2 * H) * s0)
    adjoints_ref[0] = swap(even)
    adjoints_ref[1] = swap(odd)
    pad = (CH, WPAD - 576)
    even_bias = jnp.broadcast_to(jnp.sum(even_term, axis=1, keepdims=True), pad)
    odd_bias = jnp.broadcast_to(jnp.sum(odd_term, axis=1, keepdims=True), pad)

    def write(ref, grad, bias):
        ref[:, 0:576] = grad
        ref[:, 576:WPAD] = bias

    core = place()[3]

    @pl.when(core == 0)
    def _():
        write(mine_ref, even_grad, even_bias)
        write(other_ref, odd_grad, odd_bias)

    @pl.when(core == 1)
    def _():
        write(mine_ref, odd_grad, odd_bias)
        write(other_ref, even_grad, even_bias)


def late(keep, lhs, mus):
    grad = jax.ShapeDtypeStruct((CH, WPAD), F32)
    return pl.pallas_call(
        late_kernel,
        out_shape=(field(2), grad, grad),
        in_specs=[VMEM] * 2 + [ANY] * RING,
        scratch_shapes=[vmem(field()), pltpu.SemaphoreType.DMA],
        compiler_params=PARAMS,
        name="late",
    )(keep, lhs, *mus)


def finish_kernel(mine_ref, other_ref, grad_ref, bias_ref):
    core = place()[3]
    r = lax.broadcasted_iota(jnp.int32, (CH, CH), 0)
    c = lax.broadcasted_iota(jnp.int32, (CH, CH), 1)

    def write(slot, ref):
        grad_ref[slot] = ref[:, 0:576]
        spread = jnp.broadcast_to(ref[:, 576:577], (CH, CH))
        bias_ref[slot : slot + 1] = jnp.sum(jnp.where(r == c, spread, 0.0), axis=0, keepdims=True)

    @pl.when(core == 0)
    def _():
        write(0, mine_ref)
        write(1, other_ref)

    @pl.when(core == 1)
    def _():
        write(1, mine_ref)
        write(0, other_ref)


def finish(mine, other):
    return pl.pallas_call(
        finish_kernel,
        out_shape=(
            jax.ShapeDtypeStruct((2, CH, 576), F32),
            jax.ShapeDtypeStruct((2, CH), F32),
        ),
        compiler_params=PARAMS,
        name="finish",
    )(mine, other)


def tie(*values):
    return lax.optimization_barrier(values)


NEAR = (1, 7, 2, 6, 3, 5, 4)
FAR = NEAR[::-1]
EARLY = FAR[:0]
PAIRS = ((6, 3), (2, 4), (7, 5), (1, None))


def body(coarse_guess, adjoint_guess, weights, biases):
    images = lax.axis_size("dp")
    groups = lax.axis_size("layer") // RING
    last = groups - 1

    def device(x, z, d):
        return (RING * x + z % RING) * images + d

    def lead(d):
        return 2 + 3 * (d % 2)

    everyone = [(x, d) for x in range(groups) for d in range(images)]

    def gather(value, k):
        pairs = [(device(x, lead(d) + k, d), device(x, lead(d), d)) for x, d in everyone]
        return lax.ppermute(value, AXES, pairs)

    def gather_pair(value, direct, helped):
        pairs = [(device(x, lead(d) + direct, d), device(x, lead(d), d)) for x, d in everyone]
        if helped is not None:
            pairs += [
                (device(x, lead(d) + helped, d), device(x, lead(d), d ^ 1)) for x, d in everyone
            ]
        return lax.ppermute(value, AXES, pairs)

    def hand_over(value):
        pairs = [(device(x, lead(d), d ^ 1), device(x, lead(d), d)) for x, d in everyone]
        return lax.ppermute(value, AXES, pairs)

    def scatter(value, k):
        pairs = [(device(x, lead(d), d), device(x, lead(d) + k, d)) for x, d in everyone]
        return lax.ppermute(value, AXES, pairs)

    def hop(value, source, target):
        pairs = [
            (device(source, lead(d), d), device(target, lead(d), d)) for d in range(images)
        ]
        return lax.ppermute(value, AXES, pairs)

    c, a = coarse_guess[0, 0], adjoint_guess[0, 0]
    one, two = relax(c, a, weights, biases)
    ones, twos = [one] + [None] * (RING - 1), [two] + [None] * (RING - 1)
    for direct, helped in PAIRS:
        ones[direct] = gather_pair(one, direct, helped)
        if helped is not None:
            ones[helped] = hand_over(ones[direct])
    vt, end = first_chain(ones)
    v = hop(end, 0, 1)
    ahead0, behind0 = prepare([tie(end, one)[1]] + ones[1:], "prepare")
    for k in NEAR:
        twos[k] = gather(two, k)
    for stage in range(1, last):
        vt, end = chain(stage, ones, ahead0, v, vt)
        v = hop(end, stage, stage + 1)
    ahead1, behind1 = prepare(twos, "prepare2")
    vs, mus, end = turn(last, ones, twos, [ahead0, behind0, ahead1, behind1], v)
    mu = hop(end, last, last - 1)
    vs, parts = middle(last, twos, vt, ahead1, behind1, vs)
    own_v = [vs[0]] + [None] * (RING - 1)
    for stage in range(last - 1, -1, -1):
        if stage == last - 1:
            chunk, gate = FAR[:4], parts[0]
        elif stage == last - 2:
            chunk, gate = FAR[4:], end
        else:
            chunk = ()
        for k in chunk:
            own_v[k] = scatter(tie(gate, vs[k])[1], k)
        if stage == last - 1:
            mu, *parts = tie(mu, *parts)
        if stage == 0:
            states, keep, lhs = early(one, two, c, own_v)
            mu, keep = tie(mu, keep)
        mus, end = back_chain(stage, parts, behind0, mu, mus)
        if stage == last - 1:
            got = tie(end, *[own_v[k] for k in chunk])
            end = got[0]
            for k, value in zip(chunk, got[1:]):
                own_v[k] = value
        if stage > 0:
            mu = hop(end, stage, stage - 1)
    own_mu = [mus[0]] + [None] * (RING - 1)
    for k in FAR:
        own_mu[k] = scatter(mus[k], k)
    adjoints, mine, other = late(keep, lhs, own_mu)
    mine = mine + lax.ppermute(other, "dp", [(i, i ^ 1) for i in range(images)])
    for flip in (2, 6):
        mine = mine + lax.ppermute(mine, "dp", [(i, i ^ flip) for i in range(images)])
    other = lax.ppermute(mine, "dp", [(i, i ^ 1) for i in range(images)])
    grad, bias = finish(mine, other)
    return states[:, None], adjoints[:, None], grad, bias


def solution(mesh):
    return jax.shard_map(
        body,
        mesh=mesh,
        in_specs=(
            P("layer", "dp", None, None),
            P("layer", "dp", None, None),
            P("layer", None, None),
            P("layer", None),
        ),
        out_specs=(
            P("layer", "dp", None, None),
            P("layer", "dp", None, None),
            P("layer", None, None),
            P("layer", None),
        ),
        check_vma=False,
    )
```
